128 devices in a mesh: batch: 16 (over y, z), proto: 8 (over x, core).
Axes of the slice: x: 4, y: 4, z: 4, core: 2. Of those that a mesh axis runs over, the one named last changes fastest.
Arguments:
- features: bfloat16 [16384, 2048], P(('batch', 'proto')), may hold values from -24 to 24
- w_first: bfloat16 [2048, 2048], replicated, may hold values from -0.125 to 0.125
- bn_gain: float32 [2048], replicated, may hold values from 0.1 to 1.9
- bn_bias: float32 [2048], replicated, may hold values from -3 to 3
- w_second: bfloat16 [2048, 256], replicated, may hold values from -0.125 to 0.125
- prototypes: bfloat16 [16384, 256], P('proto'), may hold values from -16 to 16
- pair: int32 [16384], P('batch'), may hold values from 0 to 16383, as said below
Outputs:
- grad_first: float32 [2048, 2048], P(('batch', 'proto'))
- grad_second: float32 [2048, 256], P(('batch', 'proto'))
- grad_gain: float32 [2048], replicated
- grad_bias: float32 [2048], replicated
- grad_proto: float32 [16384, 256], P('proto', 'batch')
- loss: float32 [], replicated
The draws below stay inside these ranges and needn't reach their ends.
Inputs may be any that keep to these rules, and one draw needn't show every extreme that they name: pair is an involution without fixed points: pair[pair[i]] = i and pair[i] != i, and rows i and pair[i] lie in the same aligned block of 1024 rows.
All inputs are finite; a program needn't handle non-finite values.
Results may differ from the reference program's by a relative error of at most 0.015.
Values may be sent and summed in bfloat16 or wider, within the bound.
No kernel may reach another device: no remote copies, remote signals or barrier semaphores. Data moves between devices by JAX's collectives and lax.ppermute only.
A program may use at most 128 MiB of HBM per device.

```python
import jax
import jax.numpy as jnp
from jax import lax

D_IN = 2048
HIDDEN_SIZE = 2048
EMBED = 256
PROTOS = 16384
ITERS = 3
ROWS = 16384
GROUP_ROWS = 1024
N_BATCH = 16
N_PROTO = 8


def draw_pair(key, part):
    blocks = ROWS // GROUP_ROWS
    block_keys = jax.random.split(jax.random.fold_in(key, 17), blocks)
    shuffled = jax.vmap(lambda block_key: jax.random.permutation(block_key, GROUP_ROWS))(block_keys).astype(jnp.int32)
    positions = jnp.arange(GROUP_ROWS, dtype=jnp.int32)
    partner_slot = jnp.bitwise_xor(positions, 1)

    def invert_block(permuted):
        return jnp.zeros((GROUP_ROWS,), jnp.int32).at[permuted].set(permuted[partner_slot])
    in_block = jax.vmap(invert_block)(shuffled)
    offsets = (jnp.arange(blocks, dtype=jnp.int32) * GROUP_ROWS)[:, None]
    return (in_block + offsets).reshape(ROWS)


def draw_prototypes(key, part):
    noise_key = jax.random.fold_in(key, 31)
    center_key = jax.random.fold_in(key, 43)
    centers = jnp.clip(jax.random.normal(center_key, (N_PROTO, EMBED), jnp.float32), -4.0, 4.0)
    position = jnp.arange(PROTOS, dtype=jnp.int32)
    group_index = position * N_PROTO // PROTOS
    chosen = jnp.take(centers, group_index, axis=0)
    fraction = position.astype(jnp.float32) / PROTOS
    noise = jnp.clip(jax.random.normal(noise_key, (PROTOS, EMBED), jnp.float32), -6.0, 6.0)
    strength = 0.6 + 1.8 * fraction
    return (noise + strength[:, None] * chosen).astype(jnp.bfloat16)


def with_spikes(values, stream_key, source, target, shards_of, factor):
    def block_of(axis_at):
        return (jnp.arange(values.shape[axis_at]) // (values.shape[axis_at] // shards_of)).reshape((-1,) + (1,) * (values.ndim - 1 - axis_at))

    near = jax.random.permutation(stream_key, shards_of)[block_of(target)]
    far = (block_of(target) + shards_of // 2) % shards_of
    return jnp.where((block_of(source) == near) | (block_of(source) == far), factor * values, values)


def shard_levels(stream_key, extent, cuts, least, largest):
    factor_of, own = 1.0, jax.random.fold_in(stream_key, 6)
    for dim, shards_of in cuts:
        steps = jnp.exp(jax.random.uniform(jax.random.fold_in(own, dim), (shards_of,), jnp.float32, least / len(cuts), largest / len(cuts)))
        factor_of = factor_of * jnp.repeat(steps, extent[dim] // shards_of).reshape([-1 if axis == dim else 1 for axis in range(len(extent))])
    return factor_of


def bell_draw(own_key, dims, width, limit, cuts=(), kind=jnp.bfloat16):
    factor_of = shard_levels(own_key, dims, cuts, -0.22, 0.18) if cuts else 1.0
    drawn = jax.random.normal(own_key, dims, jnp.float32) * width * factor_of
    return jnp.minimum(jnp.maximum(drawn, -limit), limit).astype(kind)


def noise_with(rng, extent, scale, reach, cuts, heavy, kind=jnp.bfloat16):
    entries = scale * jax.random.normal(rng, extent, jnp.float32)
    if cuts:
        entries = entries * shard_levels(rng, extent, cuts, -0.22, 0.18)
    return jnp.clip(with_spikes(entries, jax.random.fold_in(rng, 3), *heavy), -reach, reach).astype(kind)


def setup_inputs(seed: int = 0) -> dict:
    arg_keys = jax.random.split(jax.random.key(seed), 8)
    return {
        "features": noise_with(arg_keys[0], (ROWS, D_IN), 1.0, 24.0, ((0, 128),), (0, 1, 128, 5.5)),
        "w_first": bell_draw(arg_keys[1], (D_IN, HIDDEN_SIZE), D_IN ** -0.5, 0.125),
        "bn_gain": jnp.clip(1.0 + 0.18 * jax.random.normal(arg_keys[2], (HIDDEN_SIZE,), jnp.float32), 0.1, 1.9),
        "bn_bias": bell_draw(arg_keys[3], (HIDDEN_SIZE,), 0.5, 3.0, (), jnp.float32),
        "w_second": bell_draw(arg_keys[4], (HIDDEN_SIZE, EMBED), HIDDEN_SIZE ** -0.5, 0.125),
        "prototypes": draw_prototypes(jax.random.fold_in(arg_keys[7], 71), 0),
        "pair": draw_pair(jax.random.fold_in(arg_keys[7], 71), 0),
    }


transport_entropy_weight = 0.05
sharpness_divisor = 0.1

def unit_rows(values):
    rescaling_multiplier = lax.rsqrt(lax.optimization_barrier(jnp.sum(values * values, axis=1, keepdims=True)) + 1e-06)
    return (values * rescaling_multiplier, rescaling_multiplier)

def reference(features, w_first, bn_gain, bn_bias, w_second, prototypes, pair):
    pre = jnp.dot(features, w_first, preferred_element_type=jnp.float32)
    mean_act = lax.optimization_barrier(jnp.sum(pre, axis=0)) / ROWS
    second_moment = lax.optimization_barrier(jnp.sum(pre * pre, axis=0)) / ROWS
    inv_std = lax.rsqrt(second_moment - mean_act * mean_act + 1e-05)
    normed = (pre - mean_act) * inv_std
    shifted = normed * bn_gain + bn_bias
    hidden = jax.nn.gelu(shifted).astype(jnp.bfloat16)
    embed = jnp.dot(hidden, w_second, preferred_element_type=jnp.float32)
    unit_embed, embed_scale = unit_rows(embed)
    embed_bf = unit_embed.astype(jnp.bfloat16)
    unit_proto, proto_scale = unit_rows(prototypes.astype(jnp.float32))
    proto_bf = unit_proto.astype(jnp.bfloat16)
    block = GROUP_ROWS * min(N_BATCH, max(1, 4096 // GROUP_ROWS))
    nblocks = ROWS // block
    embed_blocks = embed_bf.reshape(nblocks, block, EMBED)

    def evaluate_similarities(sample_lowprecision):
        return lax.dot_general(sample_lowprecision, proto_bf, (((1,), (1,)), ((), ())), preferred_element_type=jnp.float32)

    def kernel_of(sample_lowprecision):
        return jnp.exp(evaluate_similarities(sample_lowprecision) / transport_entropy_weight)
    sample_normalizer = jnp.ones((nblocks, block), jnp.float32)
    per_cluster_multiplier = jnp.ones((PROTOS,), jnp.float32)
    for step in range(ITERS):

        def add_columns(total, item):
            sample_lowprecision, rescaling_multiplier = item
            return (total + jnp.dot(rescaling_multiplier, kernel_of(sample_lowprecision), precision=lax.Precision.HIGHEST), None)
        col_total = lax.scan(add_columns, jnp.zeros((PROTOS,), jnp.float32), (embed_blocks, sample_normalizer))[0]
        per_cluster_multiplier = 1.0 / col_total

        def row_pass(sample_lowprecision):
            return 1.0 / jnp.dot(kernel_of(sample_lowprecision), per_cluster_multiplier, precision=lax.Precision.HIGHEST)
        sample_normalizer = lax.map(row_pass, embed_blocks)

    def final_pass(carry, item):
        proto_acc, loss_acc = carry
        sample_lowprecision, rescaling_multiplier, mates, first = item
        centroid_similarity_matrix = evaluate_similarities(sample_lowprecision)
        cluster_allocation = jnp.exp(centroid_similarity_matrix / transport_entropy_weight) * rescaling_multiplier[:, None] * per_cluster_multiplier[None, :]
        goal_allocations = jnp.take(cluster_allocation, (mates - first).astype(jnp.int32), axis=0)
        centroid_affinities = centroid_similarity_matrix / sharpness_divisor
        exponentiated_entries = jnp.exp(centroid_affinities)
        normalizing_partition = lax.optimization_barrier(jnp.sum(exponentiated_entries, axis=1, keepdims=True))
        logp = centroid_affinities - jnp.log(normalizing_partition)
        loss_acc = loss_acc - jnp.sum(goal_allocations * logp)
        similarity_derivative = ((exponentiated_entries / normalizing_partition - goal_allocations) / sharpness_divisor).astype(jnp.bfloat16)
        d_rows = jnp.dot(similarity_derivative, proto_bf, preferred_element_type=jnp.float32)
        proto_acc = proto_acc + lax.dot_general(similarity_derivative, sample_lowprecision, (((0,), (0,)), ((), ())), preferred_element_type=jnp.float32)
        return ((proto_acc, loss_acc), d_rows)
    firsts = (jnp.arange(nblocks) * block).astype(jnp.int32)
    pair_blocks = pair.reshape(nblocks, block)
    start = (jnp.zeros((PROTOS, EMBED), jnp.float32), jnp.zeros((), jnp.float32))
    (proto_acc, loss_sum), d_unit = lax.scan(final_pass, start, (embed_blocks, sample_normalizer, pair_blocks, firsts))
    d_unit = d_unit.reshape(ROWS, EMBED)
    grad_proto = (proto_acc - unit_proto * lax.optimization_barrier(jnp.sum(unit_proto * proto_acc, axis=1, keepdims=True))) * proto_scale
    loss = loss_sum / ROWS
    d_embed = ((d_unit - unit_embed * lax.optimization_barrier(jnp.sum(unit_embed * d_unit, axis=1, keepdims=True))) * embed_scale).astype(jnp.bfloat16)
    grad_second = lax.dot_general(hidden, d_embed, (((0,), (0,)), ((), ())), preferred_element_type=jnp.float32)
    d_hidden = lax.dot_general(d_embed, w_second, (((1,), (1,)), ((), ())), preferred_element_type=jnp.float32)
    d_shift = jax.vjp(jax.nn.gelu, shifted)[1](d_hidden)[0]
    grad_gain = lax.optimization_barrier(jnp.sum(d_shift * normed, axis=0))
    grad_bias = lax.optimization_barrier(jnp.sum(d_shift, axis=0))
    d_pre = (bn_gain * inv_std * (d_shift - grad_bias / ROWS - normed * grad_gain / ROWS)).astype(jnp.bfloat16)
    grad_first = lax.dot_general(features, d_pre, (((0,), (0,)), ((), ())), preferred_element_type=jnp.float32)
    return (grad_first, grad_second, grad_gain, grad_bias, grad_proto, loss)
```

```python
import jax
import jax.numpy as jnp
from jax import lax
from jax.experimental import pallas as pl
from jax.experimental.pallas import tpu as pltpu
from jax.sharding import PartitionSpec as P

ITERS = 3
BF = jnp.bfloat16
F32 = jnp.float32


def spread(x, axis):
    n = lax.axis_size(axis)
    return lax.all_to_all(jnp.broadcast_to(x[None], (n,) + x.shape), axis, 0, 0, tiled=True)


def deal(x, axis):
    return lax.all_to_all(x, axis, 0, 0, tiled=True)


def split3(v):
    hi = v.astype(BF)
    rest = v - hi.astype(F32)
    mid = rest.astype(BF)
    low = (rest - mid.astype(F32)).astype(BF)
    shape = (8, v.shape[1])
    row = lax.broadcasted_iota(jnp.int32, shape, 0)
    parts = jnp.where(row == 0, hi.astype(F32), jnp.where(row == 1, mid.astype(F32), low.astype(F32)))
    return jnp.where(row < 3, parts, 0.0).astype(BF)


def score_kernel(embed_ref, proto_t_ref, kern_ref, col_ref, soft_ref, acc_ref):
    step = pl.program_id(0)

    @pl.when(step == 0)
    def _():
        acc_ref[...] = jnp.zeros_like(acc_ref)

    scores = jnp.dot(embed_ref[...], proto_t_ref[...], preferred_element_type=F32)
    tempered = jnp.exp(scores * 10.0)
    kern = tempered * tempered
    kern_ref[...] = kern.astype(BF)
    acc_ref[0:1, :] += jnp.sum(kern, axis=0, keepdims=True)
    soft = jnp.sum(tempered, axis=1, keepdims=True)
    rows = soft.shape[0]
    eye = lax.broadcasted_iota(jnp.int32, (rows, rows), 0) == lax.broadcasted_iota(jnp.int32, (rows, rows), 1)
    soft_row = jnp.sum(jnp.where(eye, soft, 0.0), axis=0, keepdims=True)
    soft_ref[...] = jnp.broadcast_to(soft_row, soft_ref.shape)

    @pl.when(step == pl.num_programs(0) - 1)
    def _():
        col_ref[...] = jnp.broadcast_to(acc_ref[0:1, :], col_ref.shape)


def row_kernel(recv_ref, kern_ref, out_ref, split_ref):
    @pl.when(pl.program_id(0) == 0)
    def _():
        split_ref[...] = split3(1.0 / jnp.sum(recv_ref[...], axis=0, keepdims=True))

    sums = lax.dot_general(split_ref[...], kern_ref[...], (((1,), (1,)), ((), ())), preferred_element_type=F32)
    out_ref[...] = jnp.broadcast_to(jnp.sum(sums, axis=0, keepdims=True), out_ref.shape)


def col_kernel(recv_ref, kern_ref, out_ref, acc_ref):
    step = pl.program_id(0)

    @pl.when(step == 0)
    def _():
        acc_ref[...] = jnp.zeros_like(acc_ref)

    scale = split3(1.0 / jnp.sum(recv_ref[...], axis=0, keepdims=True))
    acc_ref[...] += jnp.dot(scale, kern_ref[...], preferred_element_type=F32)

    @pl.when(step == pl.num_programs(0) - 1)
    def _():
        out_ref[...] = jnp.broadcast_to(jnp.sum(acc_ref[...], axis=0, keepdims=True), out_ref.shape)


def final_kernel(
    embed_ref, mate_ref, pair_ref, proto_t_ref, proto_ref, raw_t_ref, recv_col_ref, recv_row_ref, recv_soft_ref,
    d_unit_ref, term_ref, loss_ref, acc_ref, loss_acc_ref,
):
    step = pl.program_id(0)
    rows = embed_ref.shape[0]

    @pl.when(step == 0)
    def _():
        acc_ref[...] = jnp.zeros_like(acc_ref)
        loss_acc_ref[...] = jnp.zeros_like(loss_acc_ref)

    row_scale = 1.0 / jnp.sum(recv_row_ref[...], axis=0, keepdims=True)
    soft_row = jnp.sum(recv_soft_ref[...], axis=0, keepdims=True)
    col_scale = 1.0 / jnp.sum(recv_col_ref[...], axis=0, keepdims=True)
    total = row_scale.shape[1]
    lane = lax.broadcasted_iota(jnp.int32, (rows, total), 1)
    here = lax.broadcasted_iota(jnp.int32, (rows, total), 0) + step * rows
    mate_scale = jnp.sum(jnp.where(lane == pair_ref[...], row_scale, 0.0), axis=1, keepdims=True)
    soft = jnp.sum(jnp.where(lane == here, soft_row, 0.0), axis=1, keepdims=True)
    scores = jnp.dot(embed_ref[...], proto_t_ref[...], preferred_element_type=F32) * 10.0
    mates = jnp.dot(mate_ref[...], proto_t_ref[...], preferred_element_type=F32)
    target = jnp.exp(mates * 20.0) * mate_scale * col_scale
    loss_acc_ref[0:1, :] += jnp.sum(target * (scores - jnp.log(soft)), axis=0, keepdims=True)
    grad = ((jnp.exp(scores) * (1.0 / soft) - target) * 10.0).astype(BF)
    d_unit_ref[...] = jnp.dot(grad, proto_ref[...], preferred_element_type=F32).astype(d_unit_ref.dtype)
    acc_ref[...] += lax.dot_general(
        embed_ref[...], grad, (((0,), (0,)), ((), ())), preferred_element_type=F32
    )

    @pl.when(step == pl.num_programs(0) - 1)
    def _():
        raw = raw_t_ref[...].astype(F32)
        scale = lax.rsqrt(jnp.sum(raw * raw, axis=0, keepdims=True) + 1e-06)
        unit = raw * scale
        acc = acc_ref[...]
        term = (acc - unit * jnp.sum(unit * acc, axis=0, keepdims=True)) * scale
        term_ref[...] = term.astype(BF)
        loss_ref[...] = jnp.broadcast_to(jnp.sum(loss_acc_ref[0:1, :], axis=1, keepdims=True), loss_ref.shape)


def whole(shape):
    return pl.BlockSpec(shape, lambda i: (0,) * len(shape))


def tiled_rows(rows, width):
    return pl.BlockSpec((rows, width), lambda i: (i, 0))


def sinkhorn_and_loss(block_embed, mates, pair_col, proto_t, proto_bf, raw_t):
    n_batch = lax.axis_size("batch")
    n_proto = lax.axis_size("proto")
    rows, width = block_embed.shape
    cols = proto_t.shape[1]
    tile = 256
    steps = rows // tile
    kern, col_part, soft_part = pl.pallas_call(
        score_kernel,
        grid=(steps,),
        in_specs=[tiled_rows(tile, width), whole((width, cols))],
        out_specs=[tiled_rows(tile, cols), whole((n_batch, cols)), pl.BlockSpec((n_proto, tile), lambda i: (0, i))],
        out_shape=[
            jax.ShapeDtypeStruct((rows, cols), BF),
            jax.ShapeDtypeStruct((n_batch, cols), F32),
            jax.ShapeDtypeStruct((n_proto, rows), F32),
        ],
        scratch_shapes=[pltpu.VMEM((8, cols), F32)],
        name="score_kernel",
    )(block_embed, proto_t)
    row_pass = pl.pallas_call(
        row_kernel,
        grid=(steps,),
        in_specs=[whole((n_batch, cols)), tiled_rows(tile, cols)],
        out_specs=pl.BlockSpec((n_proto, tile), lambda i: (0, i)),
        out_shape=jax.ShapeDtypeStruct((n_proto, rows), F32),
        scratch_shapes=[pltpu.VMEM((8, cols), BF)],
        name="row_kernel",
    )
    col_pass = pl.pallas_call(
        col_kernel,
        grid=(steps,),
        in_specs=[pl.BlockSpec((n_proto, tile), lambda i: (0, i)), tiled_rows(tile, cols)],
        out_specs=whole((n_batch, cols)),
        out_shape=jax.ShapeDtypeStruct((n_batch, cols), F32),
        scratch_shapes=[pltpu.VMEM((8, cols), F32)],
        name="col_kernel",
    )
    recv_soft = deal(soft_part, "proto")
    for step in range(ITERS):
        recv_col = deal(col_part, "batch")
        recv_row = deal(row_pass(recv_col, kern), "proto")
        if step + 1 < ITERS:
            col_part = col_pass(recv_row, kern)
    return pl.pallas_call(
        final_kernel,
        grid=(steps,),
        in_specs=[
            tiled_rows(tile, width),
            tiled_rows(tile, width),
            tiled_rows(tile, 1),
            whole((width, cols)),
            whole((cols, width)),
            whole((width, cols)),
            whole((n_batch, cols)),
            whole((n_proto, rows)),
            whole((n_proto, rows)),
        ],
        out_specs=[tiled_rows(tile, width), whole((width, cols)), whole((8, 128))],
        out_shape=[
            jax.ShapeDtypeStruct((rows, width), BF),
            jax.ShapeDtypeStruct((width, cols), BF),
            jax.ShapeDtypeStruct((8, 128), F32),
        ],
        scratch_shapes=[pltpu.VMEM((width, cols), F32), pltpu.VMEM((8, cols), F32)],
        name="final_kernel",
    )(block_embed, mates, pair_col, proto_t, proto_bf, raw_t, recv_col, recv_row, recv_soft)


def unit_rows(values):
    scale = lax.rsqrt(jnp.sum(values * values, axis=1, keepdims=True) + 1e-06)
    return (values * scale, scale)


def local(features, w_first, bn_gain, bn_bias, w_second, prototypes, pair):
    n_batch = lax.axis_size("batch")
    n_proto = lax.axis_size("proto")
    own_rows, d_in = features.shape
    d_hid, width = w_second.shape
    total_rows = own_rows * n_batch * n_proto
    block_rows = own_rows * n_proto
    part = lax.axis_index("proto")
    slab = d_hid // n_proto

    raw_t = prototypes.T
    raw_t32 = raw_t.astype(F32)
    proto_t = (raw_t32 * lax.rsqrt(jnp.sum(raw_t32 * raw_t32, axis=0, keepdims=True) + 1e-06)).astype(BF)
    proto_bf = unit_rows(prototypes.astype(F32))[0].astype(BF)

    pre = jnp.dot(features, w_first, preferred_element_type=F32)
    stats = jnp.stack([jnp.sum(pre, axis=0), jnp.sum(pre * pre, axis=0)])
    stats = jnp.sum(spread(stats, "batch"), axis=0)
    stats = jnp.sum(spread(stats, "proto"), axis=0)
    mean_act = stats[0] / total_rows
    inv_std = lax.rsqrt(stats[1] / total_rows - mean_act * mean_act + 1e-05)
    hidden = jax.nn.gelu((pre - mean_act) * inv_std * bn_gain + bn_bias).astype(BF)
    embed = jnp.dot(hidden, w_second, preferred_element_type=F32)
    unit_embed, embed_scale = unit_rows(embed)
    block_embed = spread(unit_embed.astype(BF), "proto").reshape(block_rows, width)

    first_row = lax.axis_index("batch") * block_rows
    mate_row = pair - first_row
    mates = jnp.take(block_embed, mate_row, axis=0)
    d_unit_part, term_t, loss_tile = sinkhorn_and_loss(
        block_embed, mates, mate_row[:, None], proto_t, proto_bf, raw_t
    )

    block_features = spread(features, "proto").reshape(block_rows, d_in)
    w_slab = lax.dynamic_slice(w_first, (0, part * slab), (d_in, slab))
    w2_slab = lax.dynamic_slice(w_second, (part * slab, 0), (slab, width))

    def cut(v):
        return lax.dynamic_slice(v, (part * slab,), (slab,))

    mean_s, inv_s, gain_s, bias_s = cut(mean_act), cut(inv_std), cut(bn_gain), cut(bn_bias)
    normed = (jnp.dot(block_features, w_slab, preferred_element_type=F32) - mean_s) * inv_s
    shifted = normed * gain_s + bias_s
    hidden_s, gelu_back = jax.vjp(jax.nn.gelu, shifted)
    hidden_s = hidden_s.astype(BF)

    term_got = deal(term_t.reshape(n_batch, width // n_batch, -1), "batch")
    grad_proto = jnp.sum(term_got.astype(F32), axis=0).T

    d_unit = jnp.sum(deal(d_unit_part.reshape(n_proto, own_rows, width), "proto").astype(F32), axis=0)
    d_embed = (
        (d_unit - unit_embed * jnp.sum(unit_embed * d_unit, axis=1, keepdims=True)) * embed_scale
    ).astype(BF)
    d_embed = spread(d_embed, "proto").reshape(block_rows, width)

    d_hidden = lax.dot_general(d_embed, w2_slab, (((1,), (1,)), ((), ())), preferred_element_type=F32)
    d_shift = gelu_back(d_hidden)[0]
    sums = jnp.stack(
        [jnp.sum(d_shift * normed, axis=0), jnp.sum(d_shift, axis=0), jnp.broadcast_to(loss_tile[0, :1], (slab,))]
    )
    sums = jnp.sum(spread(sums, "batch"), axis=0)
    gain_sum, bias_sum = sums[0], sums[1]
    d_pre = (gain_s * inv_s * (d_shift - bias_sum / total_rows - normed * gain_sum / total_rows)).astype(BF)
    first_part = lax.dot_general(
        block_features, d_pre, (((0,), (0,)), ((), ())), preferred_element_type=F32
    ).astype(BF)
    got = deal(first_part.reshape(n_batch * n_proto, -1, slab), ("batch", "proto"))
    got = jnp.sum(got.reshape(n_batch, n_proto, -1, slab).astype(F32), axis=0)
    grad_first = jnp.transpose(got, (1, 0, 2)).reshape(-1, d_hid)

    second_part = lax.dot_general(hidden_s, d_embed, (((0,), (0,)), ((), ())), preferred_element_type=F32)
    second = jnp.sum(deal(second_part.reshape(n_batch, -1, width), "batch"), axis=0)
    grad_second = lax.ppermute(
        second,
        ("batch", "proto"),
        [(b * n_proto + p, p * n_batch + b) for b in range(n_batch) for p in range(n_proto)],
    )
    everywhere = spread(sums, "proto")
    grad_gain = everywhere[:, 0].reshape(-1)
    grad_bias = everywhere[:, 1].reshape(-1)
    loss = -jnp.sum(everywhere[:, 2, 0]) / total_rows
    return (grad_first, grad_second, grad_gain, grad_bias, grad_proto, loss)


def solution(mesh):
    return jax.shard_map(
        local,
        mesh=mesh,
        in_specs=(P(("batch", "proto"), None), P(), P(), P(), P(), P("proto", None), P("batch")),
        out_specs=(
            P(("batch", "proto"), None),
            P(("batch", "proto"), None),
            P(),
            P(),
            P("proto", "batch"),
            P(),
        ),
        check_vma=False,
    )
```

```python
import jax
import jax.numpy as jnp
from jax import lax
from jax.experimental import pallas as pl
from jax.experimental.pallas import tpu as pltpu
from jax.sharding import PartitionSpec as P

ITERS = 3
BF = jnp.bfloat16
F32 = jnp.float32
LANES = 128
TILE = 256
LOG2_E = 1.4426950408889634


def deal(x, axis):
    return lax.all_to_all(x, axis, 0, 0, tiled=True)


def tdot(a, b, a_dim, b_dim):
    return lax.dot_general(a, b, (((a_dim,), (b_dim,)), ((), ())), preferred_element_type=F32)


def fold_rows(v):
    return jnp.sum(v.reshape(v.shape[0] // 8, 8, LANES), axis=0)


def as_column(row):
    return jnp.broadcast_to(row, (LANES, LANES)).T


def lane(j):
    return slice(j * LANES, (j + 1) * LANES)


def whole(shape):
    return pl.BlockSpec(shape, lambda i, *_: (0,) * len(shape))


def rows_of(rows, width):
    return pl.BlockSpec((rows, width), lambda i, *_: (i, 0))


def cols_of(rows, width):
    return pl.BlockSpec((rows, width), lambda i, *_: (0, i))


def pre_kernel(features_ref, w_ref, pre_ref, msg_ref, stat_ref):
    step = pl.program_id(0)
    last = pl.num_programs(0) - 1
    pre = jnp.dot(features_ref[...], w_ref[...], preferred_element_type=F32)
    pre_ref[...] = pre
    chunks = TILE // LANES
    half = stat_ref.shape[0] // 2
    for h in range(chunks):
        part = pre[:, lane(h)]
        stat_ref[pl.ds(step * chunks + h, 1), :] = jnp.sum(part, axis=0, keepdims=True)
        stat_ref[pl.ds(half + step * chunks + h, 1), :] = jnp.sum(part * part, axis=0, keepdims=True)

    @pl.when(step == last)
    def _():
        msg_ref[...] = jnp.broadcast_to(stat_ref[...][None], msg_ref.shape)


def relay_kernel(recv_ref, msg_ref):
    msg_ref[...] = jnp.broadcast_to(jnp.sum(recv_ref[...], axis=0, keepdims=True), msg_ref.shape)


def embed_kernel(
    total_rows, pre_ref, recv_ref, gain_ref, bias_ref, w2_ref, unit_ref, scale_ref, mean_ref, inv_ref, msg_ref, hid_ref
):
    stats = jnp.sum(recv_ref[...], axis=0)
    half = stats.shape[0] // 2
    mean = stats[:half] / total_rows
    inv = lax.rsqrt(stats[half:] / total_rows - mean * mean + 1e-05)
    mean_ref[...] = mean
    inv_ref[...] = inv
    for j in range(half):
        normed = (pre_ref[:, lane(j)] - mean[j : j + 1]) * inv[j : j + 1]
        hid_ref[:, lane(j)] = jax.nn.gelu(normed * gain_ref[j : j + 1, :] + bias_ref[j : j + 1, :]).astype(BF)
    embed = jnp.dot(hid_ref[...], w2_ref[...], preferred_element_type=F32)
    scale = lax.rsqrt(jnp.sum(embed * embed, axis=1, keepdims=True) + 1e-06)
    unit = embed * scale
    unit_ref[...] = unit
    scale_ref[...] = jnp.broadcast_to(scale, scale_ref.shape)
    msg_ref[...] = jnp.broadcast_to(unit.astype(BF)[None], msg_ref.shape)


def proto_kernel(raw_ref, raw_t_ref, proto_ref, proto_t_ref):
    raw = raw_ref[...].astype(F32)
    proto_ref[...] = (raw * lax.rsqrt(jnp.sum(raw * raw, axis=1, keepdims=True) + 1e-06)).astype(BF)
    raw_t = raw_t_ref[...].astype(F32)
    proto_t_ref[...] = (raw_t * lax.rsqrt(jnp.sum(raw_t * raw_t, axis=0, keepdims=True) + 1e-06)).astype(BF)


def mate_kernel(pair_ref, embed_ref, mate_ref):
    rows = pair_ref.shape[0]
    total = embed_ref.shape[0]
    hot = lax.broadcasted_iota(jnp.int32, (rows, total), 1) == pair_ref[...]
    mate_ref[...] = jnp.dot(
        jnp.where(hot, 1.0, 0.0).astype(BF), embed_ref[...], preferred_element_type=F32
    ).astype(BF)


def score_kernel(embed_ref, proto_t_ref, kern_ref, msg_ref, soft_ref, acc_ref):
    step = pl.program_id(0)
    rows = embed_ref.shape[0]
    cols = proto_t_ref.shape[1]

    @pl.when(step == 0)
    def _():
        acc_ref[...] = jnp.zeros_like(acc_ref)

    soft = [None] * (rows // LANES)
    for j in range(cols // TILE):
        span = slice(j * TILE, (j + 1) * TILE)
        scores = jnp.dot(embed_ref[...], proto_t_ref[:, span], preferred_element_type=F32)
        tempered = jnp.exp2(scores * (10.0 * LOG2_E))
        kern = tempered * tempered
        kern_ref[:, span] = kern.astype(BF)
        for h in range(TILE // LANES):
            at = (j * (TILE // LANES) + h) * 8
            acc_ref[at : at + 8, :] += fold_rows(kern[:, lane(h)])
        for b in range(rows // LANES):
            part = tempered[b * LANES : (b + 1) * LANES]
            part = part[:, :LANES] + part[:, LANES:]
            soft[b] = part if soft[b] is None else soft[b] + part
    for b in range(rows // LANES):
        soft_ref[pl.ds(step * (rows // LANES) + b, 1), :] = jnp.sum(soft[b].T, axis=0, keepdims=True)

    @pl.when(step == pl.num_programs(0) - 1)
    def _():
        total = jnp.sum(acc_ref[...].reshape(cols // LANES, 8, LANES), axis=1)
        msg_ref[...] = jnp.broadcast_to(total[None], msg_ref.shape)


def row_kernel(recv_ref, kern_ref, *rest):
    soft_ref = rest[0] if len(rest) == 3 else None
    msg_ref, scale_ref = rest[-2:]
    step = pl.program_id(0)
    rows = kern_ref.shape[0]
    copies = msg_ref.shape[0]

    @pl.when(step == 0)
    def _():
        scale_ref[...] = 1.0 / jnp.sum(recv_ref[...], axis=0)
        if soft_ref is not None:
            half = soft_ref.shape[0]
            msg_ref[:, half:, :] = jnp.broadcast_to(soft_ref[...][None], (copies, half, LANES))

    for b in range(rows // LANES):
        acc = None
        for j in range(scale_ref.shape[0]):
            part = kern_ref[b * LANES : (b + 1) * LANES, lane(j)].astype(F32) * scale_ref[j : j + 1, :]
            acc = part if acc is None else acc + part
        row = jnp.sum(acc.T, axis=0, keepdims=True)
        msg_ref[:, pl.ds(step * (rows // LANES) + b, 1), :] = jnp.broadcast_to(row[None], (copies, 1, LANES))


def col_kernel(recv_ref, kern_ref, msg_ref, acc_ref, scale_ref):
    step = pl.program_id(0)
    rows, cols = kern_ref.shape

    @pl.when(step == 0)
    def _():
        acc_ref[...] = jnp.zeros_like(acc_ref)
        scale_ref[...] = 1.0 / jnp.sum(recv_ref[:, : scale_ref.shape[0], :], axis=0)

    for b in range(rows // LANES):
        scale = as_column(scale_ref[pl.ds(step * (rows // LANES) + b, 1), :])
        for j in range(cols // LANES):
            part = kern_ref[b * LANES : (b + 1) * LANES, lane(j)].astype(F32) * scale
            acc_ref[j * 8 : (j + 1) * 8, :] += fold_rows(part)

    @pl.when(step == pl.num_programs(0) - 1)
    def _():
        total = jnp.sum(acc_ref[...].reshape(cols // LANES, 8, LANES), axis=1)
        msg_ref[...] = jnp.broadcast_to(total[None], msg_ref.shape)


def final_kernel(
    embed_ref, mate_ref, pair_ref, proto_t_ref, proto_ref, raw_t_ref, recv_col_ref, recv_row_ref, recv_soft_ref,
    d_unit_ref, term_ref, loss_ref, acc_ref, loss_acc_ref, col_ref, row_ref, soft_ref,
):
    step = pl.program_id(0)
    rows = embed_ref.shape[0]
    cols = proto_t_ref.shape[1]
    bands = row_ref.shape[0]
    chunks = TILE // LANES

    @pl.when(step == 0)
    def _():
        acc_ref[...] = jnp.zeros_like(acc_ref)
        loss_acc_ref[...] = jnp.zeros_like(loss_acc_ref)
        col_ref[...] = 10.0 / jnp.sum(recv_col_ref[...], axis=0)
        row_ref[...] = 1.0 / jnp.sum(recv_row_ref[:, :bands, :], axis=0)
        soft_ref[...] = jnp.sum(recv_soft_ref[:, bands:, :], axis=0)
        loss_acc_ref[8:16, :] = jnp.log(soft_ref[...])

    pair = pair_ref[...]
    spot = lax.broadcasted_iota(jnp.int32, (rows, LANES), 1)
    found = jnp.zeros((rows, LANES), F32)
    for q in range(bands):
        found += jnp.where(spot + q * LANES == pair, row_ref[q : q + 1, :], 0.0)
    mate_scale = jnp.sum(found, axis=1, keepdims=True)
    base = step * (rows // LANES)
    soft = jnp.concatenate([as_column(soft_ref[pl.ds(base + b, 1), :]) for b in range(rows // LANES)], axis=0)
    inv_soft = 10.0 / soft
    d_unit = None
    loss_acc = jnp.zeros((8, LANES), F32)
    for j in range(cols // TILE):
        span = slice(j * TILE, (j + 1) * TILE)
        scores = jnp.dot(embed_ref[...], proto_t_ref[:, span], preferred_element_type=F32)
        mates = jnp.dot(mate_ref[...], proto_t_ref[:, span], preferred_element_type=F32)
        grads = []
        for h in range(chunks):
            at = j * chunks + h
            target = jnp.exp2(mates[:, lane(h)] * (20.0 * LOG2_E)) * mate_scale * col_ref[at : at + 1, :]
            score = scores[:, lane(h)]
            loss_acc += fold_rows(target * score)
            grads.append((jnp.exp2(score * (10.0 * LOG2_E)) * inv_soft - target).astype(BF))
        grad = jnp.concatenate(grads, axis=1)
        part = jnp.dot(grad, proto_ref[span, :], preferred_element_type=F32)
        d_unit = part if d_unit is None else d_unit + part
        acc_ref[:, span] += tdot(embed_ref[...], grad, 0, 0)
    d_unit_ref[...] = d_unit.astype(BF)
    loss_acc_ref[0:8, :] += loss_acc

    @pl.when(step == pl.num_programs(0) - 1)
    def _():
        for j in range(cols // TILE):
            span = slice(j * TILE, (j + 1) * TILE)
            raw = raw_t_ref[:, span].astype(F32)
            scale = lax.rsqrt(jnp.sum(raw * raw, axis=0, keepdims=True) + 1e-06)
            unit = raw * scale
            acc = acc_ref[:, span]
            term_ref[:, span] = ((acc - unit * jnp.sum(unit * acc, axis=0, keepdims=True)) * scale).astype(BF)
        loss_ref[...] = loss_acc_ref[...]


def d_embed_kernel(recv_ref, unit_ref, scale_ref, msg_ref):
    d_unit = jnp.sum(recv_ref[...].astype(F32), axis=0)
    unit = unit_ref[...]
    d_embed = (d_unit - unit * jnp.sum(unit * d_unit, axis=1, keepdims=True)) * scale_ref[:, :1]
    msg_ref[...] = jnp.broadcast_to(d_embed.astype(BF)[None], msg_ref.shape)


def gather_parts(refs):
    return jnp.concatenate([ref[...] for ref in refs], axis=0)


def slab_kernel(order_ref, mean_ref, inv_ref, gain_ref, bias_ref, w_ref, *rest):
    parts = rest[:-4]
    normed_ref, slope_ref, hid_ref, acc_ref = rest[-4:]
    step = pl.program_id(0)

    @pl.when(step == 0)
    def _():
        acc_ref[...] = jnp.zeros_like(acc_ref)

    acc_ref[...] += jnp.dot(gather_parts(parts), w_ref[...], preferred_element_type=F32)

    @pl.when(step == pl.num_programs(0) - 1)
    def _():
        chunks = acc_ref.shape[1] // LANES
        ones = jnp.ones((LANES, LANES), F32)
        for h in range(chunks):
            at = pl.ds(order_ref[0] * chunks + h, 1)
            mean, inv, gain, bias = mean_ref[at, :], inv_ref[at, :], gain_ref[at, :], bias_ref[at, :]
            for b in range(acc_ref.shape[0] // LANES):
                band = slice(b * LANES, (b + 1) * LANES)
                normed = (acc_ref[band, lane(h)] - mean) * inv
                hidden, back = jax.vjp(jax.nn.gelu, normed * gain + bias)
                normed_ref[band, lane(h)] = normed
                slope_ref[band, lane(h)] = back(ones)[0]
                hid_ref[band, lane(h)] = hidden.astype(BF)


def shift_kernel(order_ref, d_embed_ref, w2_ref, normed_ref, slope_ref, hid_ref, loss_ref, shift_ref, msg_ref, sum_ref, second_ref):
    step = pl.program_id(0)

    @pl.when(step == 0)
    def _():
        sum_ref[...] = jnp.zeros_like(sum_ref)
        second_ref[...] = jnp.zeros_like(second_ref)

    d_embed = d_embed_ref[0]
    d_shift = tdot(d_embed, w2_ref[...], 1, 1) * slope_ref[...]
    shift_ref[...] = d_shift
    sum_ref[0:1, :] += jnp.sum(d_shift * normed_ref[...], axis=0, keepdims=True)
    sum_ref[1:2, :] += jnp.sum(d_shift, axis=0, keepdims=True)
    second_ref[...] += tdot(hid_ref[...], d_embed, 0, 0)

    @pl.when(step == pl.num_programs(0) - 1)
    def _():
        hits = jnp.sum(loss_ref[0:8, :], axis=0, keepdims=True)
        logs = jnp.sum(loss_ref[8:16, :], axis=0, keepdims=True)
        sum_ref[2:3, :] = jnp.concatenate([hits, logs], axis=1)
        n, height, slab = msg_ref.shape
        msg_ref[:, :8, :] = jnp.broadcast_to(sum_ref[...][None], (n, 8, slab))
        msg_ref[:, 8:, :] = second_ref[...].reshape(n, height - 8, slab)


def first_kernel(
    total_rows, order_ref, recv_ref, shift_ref, normed_ref, inv_ref, gain_ref, *rest
):
    parts = rest[:-4]
    out_ref, sums_ref, second_ref, d_pre_ref = rest[-4:]
    step = pl.program_id(0)

    @pl.when(step == 0)
    def _():
        got = jnp.sum(recv_ref[...], axis=0)
        sums_ref[...] = jnp.broadcast_to(got[:8][None], sums_ref.shape)
        second_ref[...] = got[8:]
        chunks = d_pre_ref.shape[1] // LANES
        for h in range(chunks):
            at = pl.ds(order_ref[0] * chunks + h, 1)
            factor = gain_ref[at, :] * inv_ref[at, :]
            gain_mean = got[0:1, lane(h)] / total_rows
            bias_mean = got[1:2, lane(h)] / total_rows
            for b in range(d_pre_ref.shape[0] // LANES):
                band = slice(b * LANES, (b + 1) * LANES)
                d_pre = factor * (shift_ref[band, lane(h)] - bias_mean - normed_ref[band, lane(h)] * gain_mean)
                d_pre_ref[band, lane(h)] = d_pre.astype(BF)

    grad = tdot(gather_parts(parts), d_pre_ref[...], 0, 0)
    out_ref[...] = grad.astype(BF).reshape(out_ref.shape)


def tail_kernel(recv_ref, out_ref):
    out_ref[...] = jnp.sum(recv_ref[:, 0].astype(F32), axis=0)


def shape(dims, kind=F32):
    return jax.ShapeDtypeStruct(dims, kind)


def local(features, w_first, bn_gain, bn_bias, w_second, prototypes, pair):
    n_batch = lax.axis_size("batch")
    n_proto = lax.axis_size("proto")
    own, d_in = features.shape
    d_hid, width = w_second.shape
    cols = prototypes.shape[0]
    total_rows = own * n_batch * n_proto
    rows = own * n_proto
    part = lax.axis_index("proto")
    slab = d_hid // n_proto
    col_bands = cols // LANES
    row_bands = rows // LANES
    hid_bands = d_hid // LANES
    steps = rows // TILE
    gain = bn_gain.reshape(hid_bands, LANES)
    bias = bn_bias.reshape(hid_bands, LANES)

    def hop(x, moves):
        return lax.ppermute(x, "proto", moves)

    ring = n_proto // 2
    right = [(i * 2 + c, (i + 1) % ring * 2 + c) for i in range(ring) for c in range(2)]
    left = [(t, s) for s, t in right]
    swap = [(i, i ^ 1) for i in range(n_proto)]
    from_left = hop(features, right)
    from_right = hop(features, left)
    far_top = hop(from_left[: own // 2], right)
    far_low = hop(from_right[own // 2 :], left)
    mine = [features, from_right, from_left, far_top, far_low]
    parts = mine + [hop(piece, swap) for piece in mine]
    order = jnp.stack(
        [part] + [((part // 2 + d) % ring) * 2 + (part % 2) ^ o for o in range(2) for d in (0, 1, 3, 2)]
    ).astype(jnp.int32)

    raw_t = prototypes.T
    proto_bf, proto_t = pl.pallas_call(
        proto_kernel,
        grid=(cols // 512,),
        in_specs=[rows_of(512, width), cols_of(width, 512)],
        out_specs=[rows_of(512, width), cols_of(width, 512)],
        out_shape=[shape((cols, width), BF), shape((width, cols), BF)],
        name="proto_kernel",
    )(prototypes, raw_t)

    pre, msg = pl.pallas_call(
        pre_kernel,
        grid=(d_hid // TILE,),
        in_specs=[whole((own, d_in)), cols_of(d_in, TILE)],
        out_specs=[cols_of(own, TILE), whole((n_batch, 2 * hid_bands, LANES))],
        out_shape=[shape((own, d_hid)), shape((n_batch, 2 * hid_bands, LANES))],
        scratch_shapes=[pltpu.VMEM((2 * hid_bands, LANES), F32)],
        name="pre_kernel",
    )(features, w_first)
    msg = pl.pallas_call(
        relay_kernel, out_shape=shape((n_proto, 2 * hid_bands, LANES)), name="relay_kernel"
    )(deal(msg, "batch"))
    unit_embed, embed_scale, mean, inv, msg = pl.pallas_call(
        lambda *refs: embed_kernel(total_rows, *refs),
        out_shape=[
            shape((own, width)),
            shape((own, LANES)),
            shape((hid_bands, LANES)),
            shape((hid_bands, LANES)),
            shape((n_proto, own, width), BF),
        ],
        scratch_shapes=[pltpu.VMEM((own, d_hid), BF)],
        name="embed_kernel",
    )(pre, deal(msg, "proto"), gain, bias, w_second)
    block_embed = deal(msg, "proto").reshape(rows, width)

    kern, col_msg, soft = pl.pallas_call(
        score_kernel,
        grid=(steps,),
        in_specs=[rows_of(TILE, width), whole((width, cols))],
        out_specs=[rows_of(TILE, cols), whole((n_batch, col_bands, LANES)), whole((row_bands, LANES))],
        out_shape=[shape((rows, cols), BF), shape((n_batch, col_bands, LANES)), shape((row_bands, LANES))],
        scratch_shapes=[pltpu.VMEM((col_bands * 8, LANES), F32)],
        name="score_kernel",
    )(block_embed, proto_t)

    def row_pass(recv, extra):
        height = row_bands * (2 if extra else 1)
        return pl.pallas_call(
            row_kernel,
            grid=(steps,),
            in_specs=[whole((n_batch, col_bands, LANES)), rows_of(TILE, cols)]
            + [whole((row_bands, LANES)) for _ in extra],
            out_specs=whole((n_proto, height, LANES)),
            out_shape=shape((n_proto, height, LANES)),
            scratch_shapes=[pltpu.VMEM((col_bands, LANES), F32)],
            name="row_kernel",
        )(recv, kern, *extra)

    def col_pass(recv):
        return pl.pallas_call(
            col_kernel,
            grid=(steps,),
            in_specs=[whole(recv.shape), rows_of(TILE, cols)],
            out_specs=whole((n_batch, col_bands, LANES)),
            out_shape=shape((n_batch, col_bands, LANES)),
            scratch_shapes=[pltpu.VMEM((col_bands * 8, LANES), F32), pltpu.VMEM((row_bands, LANES), F32)],
            name="col_kernel",
        )(recv, kern)

    first_row = lax.axis_index("batch") * rows
    mate_row = (pair - first_row)[:, None]
    mates = pl.pallas_call(
        mate_kernel,
        grid=(steps,),
        in_specs=[rows_of(TILE, 1), whole((rows, width))],
        out_specs=rows_of(TILE, width),
        out_shape=shape((rows, width), BF),
        name="mate_kernel",
    )(mate_row, block_embed)

    recv_soft = None
    for step in range(ITERS):
        recv_col = deal(col_msg, "batch")
        recv_row = deal(row_pass(recv_col, () if step else (soft,)), "proto")
        recv_soft = recv_row if recv_soft is None else recv_soft
        if step + 1 < ITERS:
            col_msg = col_pass(recv_row)

    d_unit, term, loss_tile = pl.pallas_call(
        final_kernel,
        grid=(steps,),
        in_specs=[
            rows_of(TILE, width),
            rows_of(TILE, width),
            rows_of(TILE, 1),
            whole((width, cols)),
            whole((cols, width)),
            whole((width, cols)),
            whole(recv_col.shape),
            whole(recv_row.shape),
            whole(recv_soft.shape),
        ],
        out_specs=[rows_of(TILE, width), whole((width, cols)), whole((16, LANES))],
        out_shape=[shape((rows, width), BF), shape((width, cols), BF), shape((16, LANES))],
        scratch_shapes=[
            pltpu.VMEM((width, cols), F32),
            pltpu.VMEM((16, LANES), F32),
            pltpu.VMEM((col_bands, LANES), F32),
            pltpu.VMEM((row_bands, LANES), F32),
            pltpu.VMEM((row_bands, LANES), F32),
        ],
        name="final_kernel",
    )(block_embed, mates, mate_row, proto_t, proto_bf, raw_t, recv_col, recv_row, recv_soft)

    d_embed = pl.pallas_call(
        d_embed_kernel, out_shape=shape((n_proto, own, width), BF), name="d_embed_kernel"
    )(deal(d_unit.reshape(n_proto, own, width), "proto"), unit_embed, embed_scale)
    d_embed = deal(d_embed, "proto")
    term_got = deal(term.reshape(n_batch, width // n_batch, cols), "batch")
    grad_proto = jnp.sum(term_got.astype(F32), axis=0).T

    stat_spec = whole((hid_bands, LANES))
    part_specs = [pl.BlockSpec((piece.shape[0], TILE), lambda i, *_: (0, i)) for piece in parts]
    normed, slope, hid = pl.pallas_call(
        slab_kernel,
        grid_spec=pltpu.PrefetchScalarGridSpec(
            num_scalar_prefetch=1,
            grid=(d_in // TILE,),
            in_specs=[stat_spec] * 4 + [pl.BlockSpec((TILE, slab), lambda i, s: (i, s[0]))] + part_specs,
            out_specs=[whole((rows, slab))] * 3,
            scratch_shapes=[pltpu.VMEM((rows, slab), F32)],
        ),
        out_shape=[shape((rows, slab)), shape((rows, slab)), shape((rows, slab), BF)],
        name="slab_kernel",
    )(order, mean, inv, gain, bias, w_first, *parts)

    shift, msg = pl.pallas_call(
        shift_kernel,
        grid_spec=pltpu.PrefetchScalarGridSpec(
            num_scalar_prefetch=1,
            grid=(n_proto,),
            in_specs=[
                pl.BlockSpec((1, own, width), lambda i, s: (s[i + 1], 0, 0)),
                pl.BlockSpec((slab, width), lambda i, s: (s[0], 0)),
                rows_of(own, slab),
                rows_of(own, slab),
                rows_of(own, slab),
                whole((16, LANES)),
            ],
            out_specs=[rows_of(own, slab), whole((n_batch, 8 + slab // n_batch, width))],
            scratch_shapes=[pltpu.VMEM((8, slab), F32), pltpu.VMEM((slab, width), F32)],
        ),
        out_shape=[shape((rows, slab)), shape((n_batch, 8 + slab // n_batch, width))],
        name="shift_kernel",
    )(order, d_embed, w_second, normed, slope, hid, loss_tile)
    recv = deal(msg, "batch")

    share = d_in // (n_batch * n_proto)
    first, sums, second = pl.pallas_call(
        lambda *refs: first_kernel(total_rows, *refs),
        grid_spec=pltpu.PrefetchScalarGridSpec(
            num_scalar_prefetch=1,
            grid=(d_in // TILE,),
            in_specs=[whole(recv.shape), whole((rows, slab)), whole((rows, slab)), stat_spec, stat_spec] + part_specs,
            out_specs=[
                pl.BlockSpec((TILE // share, share, slab), lambda i, s: (i, 0, 0)),
                whole((n_proto, 8, slab)),
                whole((slab // n_batch, width)),
            ],
            scratch_shapes=[pltpu.VMEM((rows, slab), BF)],
        ),
        out_shape=[
            shape((n_batch * n_proto, share, slab), BF),
            shape((n_proto, 8, slab)),
            shape((slab // n_batch, width)),
        ],
        name="first_kernel",
    )(order, recv, shift, normed, inv, gain, *parts)

    first = deal(first, ("batch", "proto")).reshape(n_batch, n_proto, share, slab)
    grad_first = pl.pallas_call(
        tail_kernel,
        grid=(n_proto,),
        in_specs=[pl.BlockSpec((n_batch, 1, share, slab), lambda i: (0, i, 0, 0))],
        out_specs=cols_of(share, slab),
        out_shape=shape((share, d_hid)),
        name="tail_kernel",
    )(first)
    grad_second = lax.ppermute(
        second,
        ("batch", "proto"),
        [(b * n_proto + p, p * n_batch + b) for b in range(n_batch) for p in range(n_proto)],
    )
    sums = deal(sums, "proto")
    grad_gain = sums[:, 0].reshape(-1)
    grad_bias = sums[:, 1].reshape(-1)
    hits = jnp.sum(sums[:, 2, :LANES])
    logs = jnp.sum(sums[0, 2, LANES:])
    loss = (logs - hits) / total_rows
    return (grad_first, grad_second, grad_gain, grad_bias, grad_proto, loss)


def solution(mesh):
    return jax.shard_map(
        local,
        mesh=mesh,
        in_specs=(P(("batch", "proto"), None), P(), P(), P(), P(), P("proto", None), P("batch")),
        out_specs=(
            P(("batch", "proto"), None),
            P(("batch", "proto"), None),
            P(),
            P(),
            P("proto", "batch"),
            P(),
        ),
        check_vma=False,
    )
```

```python
import jax
import jax.numpy as jnp
from jax import lax
from jax.experimental import pallas as pl
from jax.experimental.pallas import tpu as pltpu
from jax.sharding import PartitionSpec as P


ITERS = 3
BF = jnp.bfloat16
F32 = jnp.float32
LANES = 128
TILE = 256
LOG2_E = 1.4426950408889634
PARAMS = pltpu.CompilerParams(vmem_limit_bytes=24 * 1024 * 1024)


def deal(x, axis):
    return lax.all_to_all(x, axis, 0, 0, tiled=True)


def tdot(a, b, a_dim, b_dim):
    return lax.dot_general(a, b, (((a_dim,), (b_dim,)), ((), ())), preferred_element_type=F32)


def fold_rows(v):
    return jnp.sum(v.reshape(v.shape[0] // 8, 8, LANES), axis=0)


def as_column(row):
    return jnp.broadcast_to(row, (LANES, LANES)).T


def lane(j):
    return slice(j * LANES, (j + 1) * LANES)


def whole(shape):
    return pl.BlockSpec(shape, lambda i, *_: (0,) * len(shape))


def rows_of(rows, width):
    return pl.BlockSpec((rows, width), lambda i, *_: (i, 0))


def cols_of(rows, width):
    return pl.BlockSpec((rows, width), lambda i, *_: (0, i))


def pre_kernel(features_ref, w_hbm, pre_ref, msg_ref, stat_ref, w_buf, sems):
    pieces = w_buf.shape[0]
    copies = [
        pltpu.make_async_copy(w_hbm.at[:, k * TILE : (k + 1) * TILE], w_buf.at[k], sems.at[k]) for k in range(pieces)
    ]
    for copy in copies:
        copy.start()
    chunks = TILE // LANES
    half = stat_ref.shape[0] // 2
    for k in range(pieces):
        copies[k].wait()
        pre = jnp.dot(features_ref[...], w_buf[k], preferred_element_type=F32)
        pre_ref[:, k * TILE : (k + 1) * TILE] = pre
        for h in range(chunks):
            at = k * chunks + h
            part = pre[:, lane(h)]
            stat_ref[at : at + 1, :] = jnp.sum(part, axis=0, keepdims=True)
            stat_ref[half + at : half + at + 1, :] = jnp.sum(part * part, axis=0, keepdims=True)
    msg_ref[...] = jnp.broadcast_to(stat_ref[...][None], msg_ref.shape)


def relay_kernel(recv_ref, msg_ref):
    msg_ref[...] = jnp.broadcast_to(jnp.sum(recv_ref[...], axis=0, keepdims=True), msg_ref.shape)


def embed_kernel(
    total_rows, pre_hbm, recv_ref, gain_ref, bias_ref, w2_hbm, unit_ref, scale_ref, mean_ref, inv_ref, msg_ref, hid_ref,
    pre_ref, w2_ref, sems,
):
    pre_copy = pltpu.make_async_copy(pre_hbm, pre_ref, sems.at[0])
    w2_copy = pltpu.make_async_copy(w2_hbm, w2_ref, sems.at[1])
    pre_copy.start()
    w2_copy.start()
    stats = jnp.sum(recv_ref[...], axis=0)
    half = stats.shape[0] // 2
    mean = stats[:half] / total_rows
    inv = lax.rsqrt(stats[half:] / total_rows - mean * mean + 1e-05)
    mean_ref[...] = mean
    inv_ref[...] = inv
    pre_copy.wait()
    for j in range(half):
        normed = (pre_ref[:, lane(j)] - mean[j : j + 1]) * inv[j : j + 1]
        hid_ref[:, lane(j)] = jax.nn.gelu(normed * gain_ref[j : j + 1, :] + bias_ref[j : j + 1, :]).astype(BF)
    w2_copy.wait()
    embed = jnp.dot(hid_ref[...], w2_ref[...], preferred_element_type=F32)
    scale = lax.rsqrt(jnp.sum(embed * embed, axis=1, keepdims=True) + 1e-06)
    unit = embed * scale
    unit_ref[...] = unit
    scale_ref[...] = jnp.broadcast_to(scale, scale_ref.shape)
    msg_ref[...] = jnp.broadcast_to(unit.astype(BF)[None], msg_ref.shape)


def proto_kernel(raw_ref, raw_t_ref, proto_ref, proto_t_ref):
    raw = raw_ref[...].astype(F32)
    proto_ref[...] = (raw * lax.rsqrt(jnp.sum(raw * raw, axis=1, keepdims=True) + 1e-06)).astype(BF)
    raw_t = raw_t_ref[...].astype(F32)
    proto_t_ref[...] = (raw_t * lax.rsqrt(jnp.sum(raw_t * raw_t, axis=0, keepdims=True) + 1e-06)).astype(BF)


def score_kernel(embed_ref, proto_t_hbm, kern_ref, msg_ref, soft_ref, acc_ref, proto_t_ref, sems):
    step = pl.program_id(0)
    rows = embed_ref.shape[0]
    cols = proto_t_ref.shape[1]

    def copy(j):
        span = slice(j * TILE, (j + 1) * TILE)
        return pltpu.make_async_copy(proto_t_hbm.at[:, span], proto_t_ref.at[:, span], sems.at[j])

    @pl.when(step == 0)
    def _():
        for j in range(cols // TILE):
            copy(j).start()
        acc_ref[...] = jnp.zeros_like(acc_ref)
        for j in range(cols // TILE):
            copy(j).wait()

    soft = [None] * (rows // LANES)
    for j in range(cols // TILE):
        span = slice(j * TILE, (j + 1) * TILE)
        scores = jnp.dot(embed_ref[...], proto_t_ref[:, span], preferred_element_type=F32)
        tempered = jnp.exp2(scores * (10.0 * LOG2_E))
        kern = tempered * tempered
        kern_ref[:, span] = kern.astype(BF)
        for h in range(TILE // LANES):
            at = (j * (TILE // LANES) + h) * 8
            acc_ref[at : at + 8, :] += fold_rows(kern[:, lane(h)])
        for b in range(rows // LANES):
            part = tempered[b * LANES : (b + 1) * LANES]
            part = part[:, :LANES] + part[:, LANES:]
            soft[b] = part if soft[b] is None else soft[b] + part
    for b in range(rows // LANES):
        soft_ref[pl.ds(step * (rows // LANES) + b, 1), :] = jnp.sum(soft[b].T, axis=0, keepdims=True)

    @pl.when(step == pl.num_programs(0) - 1)
    def _():
        total = jnp.sum(acc_ref[...].reshape(cols // LANES, 8, LANES), axis=1)
        msg_ref[...] = jnp.broadcast_to(total[None], msg_ref.shape)


def row_kernel(recv_ref, kern_ref, *rest):
    soft_ref = rest[0] if len(rest) == 3 else None
    msg_ref, scale_ref = rest[-2:]
    step = pl.program_id(0)
    rows = kern_ref.shape[0]
    copies = msg_ref.shape[0]

    @pl.when(step == 0)
    def _():
        scale_ref[...] = 1.0 / jnp.sum(recv_ref[...], axis=0)
        if soft_ref is not None:
            half = soft_ref.shape[0]
            msg_ref[:, half:, :] = jnp.broadcast_to(soft_ref[...][None], (copies, half, LANES))

    for b in range(rows // LANES):
        acc = None
        for j in range(scale_ref.shape[0]):
            part = kern_ref[b * LANES : (b + 1) * LANES, lane(j)].astype(F32) * scale_ref[j : j + 1, :]
            acc = part if acc is None else acc + part
        row = jnp.sum(acc.T, axis=0, keepdims=True)
        msg_ref[:, pl.ds(step * (rows // LANES) + b, 1), :] = jnp.broadcast_to(row[None], (copies, 1, LANES))


def col_kernel(recv_ref, kern_ref, msg_ref, acc_ref, scale_ref):
    step = pl.program_id(0)
    rows, cols = kern_ref.shape

    @pl.when(step == 0)
    def _():
        acc_ref[...] = jnp.zeros_like(acc_ref)
        scale_ref[...] = 1.0 / jnp.sum(recv_ref[:, : scale_ref.shape[0], :], axis=0)

    for b in range(rows // LANES):
        scale = as_column(scale_ref[pl.ds(step * (rows // LANES) + b, 1), :])
        for j in range(cols // LANES):
            part = kern_ref[b * LANES : (b + 1) * LANES, lane(j)].astype(F32) * scale
            acc_ref[j * 8 : (j + 1) * 8, :] += fold_rows(part)

    @pl.when(step == pl.num_programs(0) - 1)
    def _():
        total = jnp.sum(acc_ref[...].reshape(cols // LANES, 8, LANES), axis=1)
        msg_ref[...] = jnp.broadcast_to(total[None], msg_ref.shape)


def final_kernel(
    embed_ref, pair_ref, proto_t_ref, proto_ref, raw_t_ref, recv_col_ref, recv_row_ref, recv_soft_ref,
    d_unit_ref, term_ref, loss_ref, grad_ref, mate_ref, loss_acc_ref, col_ref, row_ref, soft_ref,
):
    step = pl.program_id(0)
    rows = d_unit_ref.shape[0]
    cols = proto_t_ref.shape[1]
    bands = row_ref.shape[0]
    chunks = TILE // LANES

    @pl.when(step == 0)
    def _():
        loss_acc_ref[...] = jnp.zeros_like(loss_acc_ref)
        col_ref[...] = 10.0 / jnp.sum(recv_col_ref[...], axis=0)
        row_ref[...] = 1.0 / jnp.sum(recv_row_ref[:, :bands, :], axis=0)
        soft_ref[...] = jnp.sum(recv_soft_ref[:, bands:, :], axis=0)
        loss_acc_ref[8:16, :] = jnp.log(soft_ref[...])

    base = step * (rows // LANES)
    here = pl.ds(pl.multiple_of(step * rows, rows), rows)
    spot = lax.broadcasted_iota(jnp.int32, (LANES, LANES), 1)
    scales = []
    for b in range(rows // LANES):
        pair = as_column(pair_ref[pl.ds(base + b, 1), :]).astype(jnp.int32)
        found = jnp.zeros((LANES, LANES), F32)
        for q in range(bands):
            hot = spot + q * LANES == pair
            found += jnp.where(hot, row_ref[q : q + 1, :], 0.0)
            mate_ref[b * LANES : (b + 1) * LANES, lane(q)] = jnp.where(hot, 1.0, 0.0).astype(BF)
        scales.append(jnp.broadcast_to(jnp.sum(found, axis=1, keepdims=True), (LANES, LANES)))
    mate_scale = jnp.concatenate(scales, axis=0)
    mate = jnp.dot(mate_ref[...], embed_ref[...], preferred_element_type=F32).astype(BF)
    soft = jnp.concatenate([as_column(soft_ref[pl.ds(base + b, 1), :]) for b in range(rows // LANES)], axis=0)
    inv_soft = 10.0 / soft
    loss_acc = jnp.zeros((8, LANES), F32)
    for j in range(cols // TILE):
        span = slice(j * TILE, (j + 1) * TILE)
        scores = jnp.dot(embed_ref[here, :], proto_t_ref[:, span], preferred_element_type=F32)
        mates = jnp.dot(mate, proto_t_ref[:, span], preferred_element_type=F32)
        for h in range(chunks):
            at = j * chunks + h
            target = jnp.exp2(mates[:, lane(h)] * (20.0 * LOG2_E)) * mate_scale * col_ref[at : at + 1, :]
            score = scores[:, lane(h)]
            loss_acc += fold_rows(target * score)
            grad_ref[here, lane(at)] = (jnp.exp2(score * (10.0 * LOG2_E)) * inv_soft - target).astype(BF)
    d_unit_ref[...] = jnp.dot(grad_ref[here, :], proto_ref[...], preferred_element_type=F32).astype(BF)
    loss_acc_ref[0:8, :] += loss_acc

    @pl.when(step == pl.num_programs(0) - 1)
    def _():
        embed_t = embed_ref[...].T
        for j in range(cols // TILE):
            span = slice(j * TILE, (j + 1) * TILE)
            raw = raw_t_ref[:, span].astype(F32)
            scale = lax.rsqrt(jnp.sum(raw * raw, axis=0, keepdims=True) + 1e-06)
            unit = raw * scale
            acc = jnp.dot(embed_t, grad_ref[:, span], preferred_element_type=F32)
            term_ref[:, span] = ((acc - unit * jnp.sum(unit * acc, axis=0, keepdims=True)) * scale).astype(BF)
        loss_ref[...] = loss_acc_ref[...]


def d_embed_kernel(recv_ref, unit_ref, scale_ref, msg_ref):
    d_unit = jnp.sum(recv_ref[...].astype(F32), axis=0)
    unit = unit_ref[...]
    d_embed = (d_unit - unit * jnp.sum(unit * d_unit, axis=1, keepdims=True)) * scale_ref[:, :1]
    msg_ref[...] = jnp.broadcast_to(d_embed.astype(BF)[None], msg_ref.shape)


def start_parts(parts, buf_ref, sems):
    copies = []
    at = 0
    for k, part in enumerate(parts):
        height = part.shape[0]
        copies.append(pltpu.make_async_copy(part, buf_ref.at[at : at + height], sems.at[k]))
        at += height
    for copy in copies:
        copy.start()
    return copies


def slab_kernel(order_ref, mean_ref, inv_ref, gain_ref, bias_ref, w_hbm, *rest):
    parts = rest[:-6]
    normed_ref, slope_ref, hid_ref, buf_ref, w_ref, sems = rest[-6:]
    rows, slab = normed_ref.shape
    at = pl.ds(pl.multiple_of(order_ref[0] * slab, slab), slab)
    w_copy = pltpu.make_async_copy(w_hbm.at[:, at], w_ref, sems.at[len(parts)])
    w_copy.start()
    copies = start_parts(parts, buf_ref, sems)
    w_copy.wait()
    chunks = slab // LANES
    ones = jnp.ones((LANES, LANES), F32)
    for g in range(2):
        for copy in copies[g * len(parts) // 2 : (g + 1) * len(parts) // 2]:
            copy.wait()
        start = g * rows // 2
        pre = jnp.dot(buf_ref[start : start + rows // 2, :], w_ref[...], preferred_element_type=F32)
        for h in range(chunks):
            at = pl.ds(order_ref[0] * chunks + h, 1)
            mean, inv, gain, bias = mean_ref[at, :], inv_ref[at, :], gain_ref[at, :], bias_ref[at, :]
            for b in range(rows // 2 // LANES):
                band = slice(start + b * LANES, start + (b + 1) * LANES)
                normed = (pre[b * LANES : (b + 1) * LANES, lane(h)] - mean) * inv
                hidden, back = jax.vjp(jax.nn.gelu, normed * gain + bias)
                normed_ref[band, lane(h)] = normed
                slope_ref[band, lane(h)] = back(ones)[0]
                hid_ref[band, lane(h)] = hidden.astype(BF)


def shift_kernel(
    order_ref, d_embed_ref, w2_ref, normed_ref, slope_ref, hid_ref, loss_ref, shift_ref, msg_ref, sum_ref
):
    n_blocks, own, _ = d_embed_ref.shape
    sum_ref[...] = jnp.zeros_like(sum_ref)
    gains = biases = second = None
    for k in range(0, n_blocks, 2):
        d_embed = jnp.concatenate([d_embed_ref[order_ref[k + 1]], d_embed_ref[order_ref[k + 2]]], axis=0)
        band = slice(k * own, (k + 2) * own)
        d_shift = tdot(d_embed, w2_ref[...], 1, 1) * slope_ref[band, :]
        shift_ref[band, :] = d_shift
        gain = jnp.sum(d_shift * normed_ref[band, :], axis=0, keepdims=True)
        bias = jnp.sum(d_shift, axis=0, keepdims=True)
        part = tdot(hid_ref[band, :], d_embed, 0, 0)
        gains = gain if gains is None else gains + gain
        biases = bias if biases is None else biases + bias
        second = part if second is None else second + part
    sum_ref[0:1, :] = gains
    sum_ref[1:2, :] = biases
    hits = jnp.sum(loss_ref[0:8, :], axis=0, keepdims=True)
    logs = jnp.sum(loss_ref[8:16, :], axis=0, keepdims=True)
    sum_ref[2:3, :] = jnp.concatenate([hits, logs], axis=1)
    n, height, slab = msg_ref.shape
    msg_ref[:, :8, :] = jnp.broadcast_to(sum_ref[...][None], (n, 8, slab))
    msg_ref[:, 8:, :] = second.reshape(n, height - 8, slab)


def first_kernel(total_rows, order_ref, recv_ref, shift_ref, normed_ref, inv_ref, gain_ref, *rest):
    parts = rest[:-6]
    out_ref, sums_ref, second_ref, d_pre_ref, buf_ref, sems = rest[-6:]
    copies = start_parts(parts, buf_ref, sems)
    got = jnp.sum(recv_ref[...], axis=0)
    sums_ref[...] = got[:8]
    second_ref[...] = got[8:]
    chunks = d_pre_ref.shape[1] // LANES
    for h in range(chunks):
        at = pl.ds(order_ref[0] * chunks + h, 1)
        factor = gain_ref[at, :] * inv_ref[at, :]
        gain_mean = got[0:1, lane(h)] / total_rows
        bias_mean = got[1:2, lane(h)] / total_rows
        for b in range(d_pre_ref.shape[0] // LANES):
            band = slice(b * LANES, (b + 1) * LANES)
            d_pre = factor * (shift_ref[band, lane(h)] - bias_mean - normed_ref[band, lane(h)] * gain_mean)
            d_pre_ref[band, lane(h)] = d_pre.astype(BF)
    for copy in copies:
        copy.wait()
    _, share, slab = out_ref.shape
    group = TILE // share
    for j in range(buf_ref.shape[1] // TILE):
        grad = tdot(buf_ref[:, j * TILE : (j + 1) * TILE], d_pre_ref[...], 0, 0)
        out_ref[j * group : (j + 1) * group] = grad.astype(BF).reshape(group, share, slab)


def tail_kernel(recv_ref, out_ref):
    n_batch, n_proto, _, slab = recv_ref.shape
    for p in range(n_proto):
        acc = recv_ref[0, p].astype(F32)
        for b in range(1, n_batch):
            acc += recv_ref[b, p].astype(F32)
        out_ref[:, p * slab : (p + 1) * slab] = acc


def sums_kernel(total_rows, order_ref, *rest):
    shown = rest[:-3]
    gain_ref, bias_ref, loss_ref = rest[-3:]
    n_proto = len(shown)
    hits = jnp.zeros((1, LANES), F32)
    for d, ref in enumerate(shown):
        at = pl.ds(lax.rem(order_ref[0] + n_proto - d, n_proto), 1)
        gain_ref[at, :] = ref[0:1, :]
        bias_ref[at, :] = ref[1:2, :]
        hits += ref[2:3, :LANES]
    loss = jnp.sum(shown[0][2:3, LANES:] - hits, axis=1, keepdims=True) / total_rows
    loss_ref[...] = jnp.broadcast_to(loss, loss_ref.shape)


def shape(dims, kind=F32):
    return jax.ShapeDtypeStruct(dims, kind)


def step_of_device(features, w_first, bn_gain, bn_bias, w_second, prototypes, pair):
    n_batch = lax.axis_size("batch")
    n_proto = lax.axis_size("proto")
    own, d_in = features.shape
    d_hid, width = w_second.shape
    cols = prototypes.shape[0]
    total_rows = own * n_batch * n_proto
    rows = own * n_proto
    part = lax.axis_index("proto")
    slab = d_hid // n_proto
    col_bands = cols // LANES
    row_bands = rows // LANES
    hid_bands = d_hid // LANES
    steps = rows // TILE
    gain = bn_gain.reshape(hid_bands, LANES)
    bias = bn_bias.reshape(hid_bands, LANES)

    def hop(x, moves):
        return lax.ppermute(x, "proto", moves)

    ring = n_proto // 2
    right = [(i * 2 + c, (i + 1) % ring * 2 + c) for i in range(ring) for c in range(2)]
    left = [(t, s) for s, t in right]
    swap = [(i, i ^ 1) for i in range(n_proto)]
    from_left = hop(features, right)
    from_right = hop(features, left)
    across = lax.shift_right_logical(part, 1)
    order = jnp.stack(
        [part]
        + [
            (lax.bitwise_and(across + d, ring - 1) * 2 + lax.bitwise_and(part, 1)) ^ o
            for o in range(2)
            for d in (0, 1, 3, 2)
        ]
    ).astype(jnp.int32)
    mate_row = (pair - lax.axis_index("batch") * rows).astype(F32).reshape(row_bands, LANES)

    raw_t = prototypes.T
    proto_bf, proto_t = pl.pallas_call(
        proto_kernel,
        grid=(cols // 512,),
        in_specs=[rows_of(512, width), cols_of(width, 512)],
        out_specs=[rows_of(512, width), cols_of(width, 512)],
        out_shape=[shape((cols, width), BF), shape((width, cols), BF)],
        name="proto_kernel",
    )(prototypes, raw_t)

    anywhere = pl.BlockSpec(memory_space=pl.ANY)
    pre, msg = pl.pallas_call(
        pre_kernel,
        in_specs=[pl.BlockSpec(features.shape, lambda: (0, 0)), anywhere],
        out_shape=[shape((own, d_hid)), shape((n_batch, 2 * hid_bands, LANES))],
        scratch_shapes=[
            pltpu.VMEM((2 * hid_bands, LANES), F32),
            pltpu.VMEM((d_hid // TILE, d_in, TILE), BF),
            pltpu.SemaphoreType.DMA((d_hid // TILE,)),
        ],
        name="pre_kernel",
    )(features, w_first)
    near_left, near_right, _ = lax.optimization_barrier((from_left, from_right, pre))
    far_top = hop(near_left[: own // 2], right)
    far_low = hop(near_right[own // 2 :], left)
    got = deal(msg, "batch")
    got, far_top, far_low, mate_row, order, proto_bf, proto_t, raw_t = lax.optimization_barrier(
        (got, far_top, far_low, mate_row, order, proto_bf, proto_t, raw_t)
    )
    mine = [features, from_right, from_left, far_top, far_low]
    parts = mine + [hop(piece, swap) for piece in mine]
    msg = pl.pallas_call(
        relay_kernel, out_shape=shape((n_proto, 2 * hid_bands, LANES)), compiler_params=PARAMS, name="relay_kernel"
    )(got)
    unit_embed, embed_scale, mean, inv, msg = pl.pallas_call(
        lambda *refs: embed_kernel(total_rows, *refs),
        in_specs=[anywhere, pl.BlockSpec((n_proto, 2 * hid_bands, LANES), lambda: (0, 0, 0))]
        + [pl.BlockSpec((hid_bands, LANES), lambda: (0, 0))] * 2
        + [anywhere],
        out_shape=[
            shape((own, width)),
            shape((own, LANES)),
            shape((hid_bands, LANES)),
            shape((hid_bands, LANES)),
            shape((n_proto, own, width), BF),
        ],
        scratch_shapes=[
            pltpu.VMEM((own, d_hid), BF),
            pltpu.VMEM((own, d_hid), F32),
            pltpu.VMEM((d_hid, width), BF),
            pltpu.SemaphoreType.DMA((2,)),
        ],
        name="embed_kernel",
    )(pre, deal(msg, "proto"), gain, bias, w_second)
    stat_spec = whole((hid_bands, LANES))
    normed, slope, hid = pl.pallas_call(
        slab_kernel,
        grid_spec=pltpu.PrefetchScalarGridSpec(
            num_scalar_prefetch=1,
            grid=(1,),
            in_specs=[stat_spec] * 4 + [anywhere] * (1 + len(parts)),
            out_specs=[whole((rows, slab))] * 3,
            scratch_shapes=[
                pltpu.VMEM((rows, d_in), BF),
                pltpu.VMEM((d_in, slab), BF),
                pltpu.SemaphoreType.DMA((len(parts) + 1,)),
            ],
        ),
        out_shape=[shape((rows, slab)), shape((rows, slab)), shape((rows, slab), BF)],
        name="slab_kernel",
    )(order, mean, inv, gain, bias, w_first, *parts)
    block_embed, normed, slope, hid = lax.optimization_barrier((deal(msg, "proto"), normed, slope, hid))
    block_embed = block_embed.reshape(rows, width)

    kern, col_msg, soft = pl.pallas_call(
        score_kernel,
        grid=(steps,),
        in_specs=[rows_of(TILE, width), anywhere],
        out_specs=[rows_of(TILE, cols), whole((n_batch, col_bands, LANES)), whole((row_bands, LANES))],
        out_shape=[shape((rows, cols), BF), shape((n_batch, col_bands, LANES)), shape((row_bands, LANES))],
        scratch_shapes=[
            pltpu.VMEM((col_bands * 8, LANES), F32),
            pltpu.VMEM((width, cols), BF),
            pltpu.SemaphoreType.DMA((cols // TILE,)),
        ],
        compiler_params=PARAMS,
        name="score_kernel",
    )(block_embed, proto_t)

    def row_pass(recv, extra):
        height = row_bands * (2 if extra else 1)
        return pl.pallas_call(
            row_kernel,
            grid=(steps,),
            in_specs=[whole((n_batch, col_bands, LANES)), rows_of(TILE, cols)]
            + [whole((row_bands, LANES)) for _ in extra],
            out_specs=whole((n_proto, height, LANES)),
            out_shape=shape((n_proto, height, LANES)),
            scratch_shapes=[pltpu.VMEM((col_bands, LANES), F32)],
            compiler_params=PARAMS,
        name="row_kernel",
        )(recv, kern, *extra)

    def col_pass(recv):
        return pl.pallas_call(
            col_kernel,
            grid=(steps,),
            in_specs=[whole(recv.shape), rows_of(TILE, cols)],
            out_specs=whole((n_batch, col_bands, LANES)),
            out_shape=shape((n_batch, col_bands, LANES)),
            scratch_shapes=[pltpu.VMEM((col_bands * 8, LANES), F32), pltpu.VMEM((row_bands, LANES), F32)],
            compiler_params=PARAMS,
        name="col_kernel",
        )(recv, kern)

    recv_soft = None
    for step in range(ITERS):
        recv_col = deal(col_msg, "batch")
        recv_row = deal(row_pass(recv_col, () if step else (soft,)), "proto")
        recv_soft = recv_row if recv_soft is None else recv_soft
        if step + 1 < ITERS:
            col_msg = col_pass(recv_row)

    d_unit, term, loss_tile = pl.pallas_call(
        final_kernel,
        grid=(steps,),
        in_specs=[
            whole((rows, width)),
            whole((row_bands, LANES)),
            whole((width, cols)),
            whole((cols, width)),
            whole((width, cols)),
            whole(recv_col.shape),
            whole(recv_row.shape),
            whole(recv_soft.shape),
        ],
        out_specs=[rows_of(TILE, width), whole((width, cols)), whole((16, LANES))],
        out_shape=[shape((rows, width), BF), shape((width, cols), BF), shape((16, LANES))],
        scratch_shapes=[
            pltpu.VMEM((rows, cols), BF),
            pltpu.VMEM((TILE, rows), BF),
            pltpu.VMEM((16, LANES), F32),
            pltpu.VMEM((col_bands, LANES), F32),
            pltpu.VMEM((row_bands, LANES), F32),
            pltpu.VMEM((row_bands, LANES), F32),
        ],
        compiler_params=PARAMS,
        name="final_kernel",
    )(block_embed, mate_row, proto_t, proto_bf, raw_t, recv_col, recv_row, recv_soft)

    side = 4
    b_of = [(b // side, b % side) for b in range(n_batch)]

    def shifted(axis, d):
        return [
            (b, (y + d) % side * side + z if axis == 0 else y * side + (z + d) % side) for b, (y, z) in enumerate(b_of)
        ]

    place = lax.axis_index("batch")
    spots = (lax.shift_right_logical(place, 2), lax.bitwise_and(place, side - 1))

    def scatter_sum(x, axis):
        pieces = x.reshape((side, -1) + x.shape[1:])
        kept = [lax.dynamic_index_in_dim(pieces, spots[axis], 0, keepdims=False)]
        for d in range(1, side):
            piece = lax.dynamic_index_in_dim(
                pieces, lax.bitwise_and(spots[axis] + d, side - 1), 0, keepdims=False
            )
            kept.append(lax.ppermute(piece, "batch", shifted(axis, d)))
        return kept

    def total(kept):
        acc = kept[0].astype(F32)
        for piece in kept[1:]:
            acc += piece.astype(F32)
        return acc

    first_stage = scatter_sum(term, 0)
    d_unit = deal(d_unit.reshape(n_proto, own, width), "proto")
    d_unit, *first_stage = lax.optimization_barrier((d_unit, *first_stage))
    d_embed = pl.pallas_call(
        d_embed_kernel, out_shape=shape((n_proto, own, width), BF), name="d_embed_kernel"
    )(d_unit, unit_embed, embed_scale)
    second_stage = scatter_sum(total(first_stage).astype(BF), 1)
    d_embed = deal(d_embed, "proto")
    d_embed, *second_stage = lax.optimization_barrier((d_embed, *second_stage))
    grad_proto = total(second_stage).T

    shift, msg = pl.pallas_call(
        shift_kernel,
        grid_spec=pltpu.PrefetchScalarGridSpec(
            num_scalar_prefetch=1,
            grid=(1,),
            in_specs=[
                whole((n_proto, own, width)),
                pl.BlockSpec((slab, width), lambda i, s: (s[0], 0)),
                whole((rows, slab)),
                whole((rows, slab)),
                whole((rows, slab)),
                whole((16, LANES)),
            ],
            out_specs=[whole((rows, slab)), whole((n_batch, 8 + slab // n_batch, width))],
            scratch_shapes=[pltpu.VMEM((8, slab), F32)],
        ),
        out_shape=[shape((rows, slab)), shape((n_batch, 8 + slab // n_batch, width))],
        name="shift_kernel",
    )(order, d_embed, w_second, normed, slope, hid, loss_tile)
    recv = deal(msg, "batch")

    share = d_in // (n_batch * n_proto)
    first, sums, second = pl.pallas_call(
        lambda *refs: first_kernel(total_rows, *refs),
        grid_spec=pltpu.PrefetchScalarGridSpec(
            num_scalar_prefetch=1,
            grid=(1,),
            in_specs=[whole(recv.shape), whole((rows, slab)), whole((rows, slab)), stat_spec, stat_spec]
            + [anywhere] * len(parts),
            out_specs=[
                whole((n_batch * n_proto, share, slab)),
                whole((8, slab)),
                whole((slab // n_batch, width)),
            ],
            scratch_shapes=[
                pltpu.VMEM((rows, slab), BF),
                pltpu.VMEM((rows, d_in), BF),
                pltpu.SemaphoreType.DMA((len(parts),)),
            ],
        ),
        out_shape=[
            shape((n_batch * n_proto, share, slab), BF),
            shape((8, slab)),
            shape((slab // n_batch, width)),
        ],
        compiler_params=PARAMS,
        name="first_kernel",
    )(order, recv, shift, normed, inv, gain, *parts)

    first = deal(first, ("batch", "proto")).reshape(n_batch, n_proto, share, slab)
    grad_first = pl.pallas_call(
        tail_kernel, out_shape=shape((share, d_hid)), compiler_params=PARAMS, name="tail_kernel"
    )(first)
    grad_second = lax.ppermute(
        second,
        ("batch", "proto"),
        [(b * n_proto + p, p * n_batch + b) for b in range(n_batch) for p in range(n_proto)],
    )
    shown = [sums] + [
        hop(sums, [(i, (i + d) % n_proto) for i in range(n_proto)]) for d in range(1, n_proto)
    ]
    grad_gain, grad_bias, loss = pl.pallas_call(
        lambda *refs: sums_kernel(total_rows, *refs),
        in_specs=[pl.BlockSpec(memory_space=pltpu.SMEM)] + [pl.BlockSpec((8, slab), lambda: (0, 0))] * n_proto,
        out_shape=[shape((n_proto, slab)), shape((n_proto, slab)), shape((1, LANES))],
        compiler_params=PARAMS,
        name="sums_kernel",
    )(order, *shown)
    grad_gain = grad_gain.reshape(-1)
    grad_bias = grad_bias.reshape(-1)
    loss = loss[0, 0]
    return (grad_first, grad_second, grad_gain, grad_bias, grad_proto, loss)


def solution(mesh):
    return jax.shard_map(
        step_of_device,
        mesh=mesh,
        in_specs=(P(("batch", "proto"), None), P(), P(), P(), P(), P("proto", None), P("batch")),
        out_specs=(
            P(("batch", "proto"), None),
            P(("batch", "proto"), None),
            P(),
            P(),
            P("proto", "batch"),
            P(),
        ),
        check_vma=False,
    )
```

```python
import jax
import jax.numpy as jnp
from jax import lax
from jax.experimental import pallas as pl
from jax.experimental.pallas import tpu as pltpu
from jax.sharding import PartitionSpec as P


ITERS = 3
BF = jnp.bfloat16
F32 = jnp.float32
LANES = 128
TILE = 256
LOG2_E = 1.4426950408889634
PARAMS = pltpu.CompilerParams(vmem_limit_bytes=24 * 1024 * 1024)


def deal(x, axis):
    return lax.all_to_all(x, axis, 0, 0, tiled=True)


def tdot(a, b, a_dim, b_dim):
    return lax.dot_general(a, b, (((a_dim,), (b_dim,)), ((), ())), preferred_element_type=F32)


def fold_rows(v):
    return jnp.sum(v.reshape(v.shape[0] // 8, 8, LANES), axis=0)


def as_column(row):
    return jnp.broadcast_to(row, (LANES, LANES)).T


def lane(j):
    return slice(j * LANES, (j + 1) * LANES)


def whole(shape):
    return pl.BlockSpec(shape, lambda i, *_: (0,) * len(shape))


def rows_of(rows, width):
    return pl.BlockSpec((rows, width), lambda i, *_: (i, 0))


def pre_kernel(features_ref, w_hbm, pre_ref, msg_ref, stat_ref, w_buf, sems):
    pieces = w_buf.shape[0]
    copies = [
        pltpu.make_async_copy(w_hbm.at[:, k * TILE : (k + 1) * TILE], w_buf.at[k], sems.at[k]) for k in range(pieces)
    ]
    for copy in copies:
        copy.start()
    chunks = TILE // LANES
    half = stat_ref.shape[0] // 2
    for k in range(pieces):
        copies[k].wait()
        pre = jnp.dot(features_ref[...], w_buf[k], preferred_element_type=F32)
        pre_ref[:, k * TILE : (k + 1) * TILE] = pre
        for h in range(chunks):
            at = k * chunks + h
            part = pre[:, lane(h)]
            stat_ref[at : at + 1, :] = jnp.sum(part, axis=0, keepdims=True)
            stat_ref[half + at : half + at + 1, :] = jnp.sum(part * part, axis=0, keepdims=True)
    msg_ref[...] = jnp.broadcast_to(stat_ref[...][None], msg_ref.shape)


def relay_kernel(recv_ref, msg_ref):
    msg_ref[...] = jnp.broadcast_to(jnp.sum(recv_ref[...], axis=0, keepdims=True), msg_ref.shape)


def embed_kernel(
    total_rows, pre_hbm, recv_ref, gain_ref, bias_ref, w2_hbm, unit_ref, scale_ref, mean_ref, inv_ref, msg_ref, hid_ref,
    pre_ref, w2_ref, sems,
):
    pre_copy = pltpu.make_async_copy(pre_hbm, pre_ref, sems.at[0])
    w2_copy = pltpu.make_async_copy(w2_hbm, w2_ref, sems.at[1])
    pre_copy.start()
    w2_copy.start()
    stats = jnp.sum(recv_ref[...], axis=0)
    half = stats.shape[0] // 2
    mean = stats[:half] / total_rows
    inv = lax.rsqrt(stats[half:] / total_rows - mean * mean + 1e-05)
    mean_ref[...] = mean
    inv_ref[...] = inv
    pre_copy.wait()
    for j in range(half):
        normed = (pre_ref[:, lane(j)] - mean[j : j + 1]) * inv[j : j + 1]
        hid_ref[:, lane(j)] = jax.nn.gelu(normed * gain_ref[j : j + 1, :] + bias_ref[j : j + 1, :]).astype(BF)
    w2_copy.wait()
    embed = jnp.dot(hid_ref[...], w2_ref[...], preferred_element_type=F32)
    scale = lax.rsqrt(jnp.sum(embed * embed, axis=1, keepdims=True) + 1e-06)
    unit = embed * scale
    unit_ref[...] = unit
    scale_ref[...] = jnp.broadcast_to(scale, scale_ref.shape)
    msg_ref[...] = jnp.broadcast_to(unit.astype(BF)[None], msg_ref.shape)


def proto_kernel(raw_ref, proto_ref, proto_t_ref, raw_t_ref):
    for k in range(raw_ref.shape[0] // TILE):
        span = slice(k * TILE, (k + 1) * TILE)
        raw_t = raw_ref[span, :].T
        raw_t_ref[:, span] = raw_t
        wide = raw_t.astype(F32)
        unit = (wide * lax.rsqrt(jnp.sum(wide * wide, axis=0, keepdims=True) + 1e-06)).astype(BF)
        proto_t_ref[:, span] = unit
        proto_ref[span, :] = unit.T


def score_kernel(embed_ref, proto_t_hbm, kern_ref, msg_ref, soft_ref, acc_ref, proto_t_ref, sems):
    step = pl.program_id(0)
    rows = embed_ref.shape[0]
    cols = proto_t_ref.shape[1]

    def copy(j):
        span = slice(j * TILE, (j + 1) * TILE)
        return pltpu.make_async_copy(proto_t_hbm.at[:, span], proto_t_ref.at[:, span], sems.at[j])

    @pl.when(step == 0)
    def _():
        for j in range(cols // TILE):
            copy(j).start()
        acc_ref[...] = jnp.zeros_like(acc_ref)
        for j in range(cols // TILE):
            copy(j).wait()

    soft = [None] * (rows // LANES)
    for j in range(cols // TILE):
        span = slice(j * TILE, (j + 1) * TILE)
        scores = jnp.dot(embed_ref[...], proto_t_ref[:, span], preferred_element_type=F32)
        tempered = jnp.exp2(scores * (10.0 * LOG2_E))
        kern = tempered * tempered
        kern_ref[:, span] = kern.astype(BF)
        for h in range(TILE // LANES):
            at = (j * (TILE // LANES) + h) * 8
            acc_ref[at : at + 8, :] += fold_rows(kern[:, lane(h)])
        for b in range(rows // LANES):
            part = tempered[b * LANES : (b + 1) * LANES]
            part = part[:, :LANES] + part[:, LANES:]
            soft[b] = part if soft[b] is None else soft[b] + part
    for b in range(rows // LANES):
        soft_ref[pl.ds(step * (rows // LANES) + b, 1), :] = jnp.sum(soft[b].T, axis=0, keepdims=True)

    @pl.when(step == pl.num_programs(0) - 1)
    def _():
        total = jnp.sum(acc_ref[...].reshape(cols // LANES, 8, LANES), axis=1)
        msg_ref[...] = jnp.broadcast_to(total[None], msg_ref.shape)


def row_kernel(recv_ref, kern_ref, *rest):
    soft_ref = rest[0] if len(rest) == 3 else None
    msg_ref, scale_ref = rest[-2:]
    step = pl.program_id(0)
    rows = kern_ref.shape[0]
    copies = msg_ref.shape[0]

    @pl.when(step == 0)
    def _():
        scale_ref[...] = 1.0 / jnp.sum(recv_ref[...], axis=0)
        if soft_ref is not None:
            half = soft_ref.shape[0]
            msg_ref[:, half:, :] = jnp.broadcast_to(soft_ref[...][None], (copies, half, LANES))

    for b in range(rows // LANES):
        acc = None
        for j in range(scale_ref.shape[0]):
            part = kern_ref[b * LANES : (b + 1) * LANES, lane(j)].astype(F32) * scale_ref[j : j + 1, :]
            acc = part if acc is None else acc + part
        row = jnp.sum(acc.T, axis=0, keepdims=True)
        msg_ref[:, pl.ds(step * (rows // LANES) + b, 1), :] = jnp.broadcast_to(row[None], (copies, 1, LANES))


def col_kernel(recv_ref, kern_ref, msg_ref, acc_ref, scale_ref):
    step = pl.program_id(0)
    rows, cols = kern_ref.shape

    @pl.when(step == 0)
    def _():
        acc_ref[...] = jnp.zeros_like(acc_ref)
        scale_ref[...] = 1.0 / jnp.sum(recv_ref[:, : scale_ref.shape[0], :], axis=0)

    for b in range(rows // LANES):
        scale = as_column(scale_ref[pl.ds(step * (rows // LANES) + b, 1), :])
        for j in range(cols // LANES):
            part = kern_ref[b * LANES : (b + 1) * LANES, lane(j)].astype(F32) * scale
            acc_ref[j * 8 : (j + 1) * 8, :] += fold_rows(part)

    @pl.when(step == pl.num_programs(0) - 1)
    def _():
        total = jnp.sum(acc_ref[...].reshape(cols // LANES, 8, LANES), axis=1)
        msg_ref[...] = jnp.broadcast_to(total[None], msg_ref.shape)


def final_kernel(
    order_ref, embed_hbm, pair_ref, proto_t_hbm, proto_hbm, raw_t_hbm, recv_col_ref, recv_row_ref, recv_soft_ref,
    d_unit_ref, piece0_ref, piece1_ref, piece2_ref, piece3_ref, loss_ref,
    grad_ref, mate_ref, loss_acc_ref, col_ref, row_ref, soft_ref, embed_ref, proto_t_ref, proto_ref, raw_t_ref, term_ref, sems,
):
    pairs = ((embed_hbm, embed_ref), (proto_t_hbm, proto_t_ref), (proto_hbm, proto_ref), (raw_t_hbm, raw_t_ref))
    copies = [pltpu.make_async_copy(src, dst, sems.at[k]) for k, (src, dst) in enumerate(pairs)]
    step = pl.program_id(0)
    rows = d_unit_ref.shape[0]
    cols = proto_t_ref.shape[1]
    bands = row_ref.shape[0]
    chunks = TILE // LANES

    @pl.when(step == 0)
    def _():
        for copy in copies:
            copy.start()
        loss_acc_ref[...] = jnp.zeros_like(loss_acc_ref)
        col_ref[...] = 10.0 / jnp.sum(recv_col_ref[...], axis=0)
        row_ref[...] = 1.0 / jnp.sum(recv_row_ref[:, :bands, :], axis=0)
        soft_ref[...] = jnp.sum(recv_soft_ref[:, bands:, :], axis=0)
        loss_acc_ref[8:16, :] = jnp.log(soft_ref[...])
        copies[0].wait()
        copies[1].wait()

    base = step * (rows // LANES)
    here = pl.ds(pl.multiple_of(step * rows, rows), rows)
    spot = lax.broadcasted_iota(jnp.int32, (LANES, LANES), 1)
    scales = []
    for b in range(rows // LANES):
        pair = as_column(pair_ref[pl.ds(base + b, 1), :]).astype(jnp.int32)
        found = jnp.zeros((LANES, LANES), F32)
        for q in range(bands):
            hot = spot + q * LANES == pair
            found += jnp.where(hot, row_ref[q : q + 1, :], 0.0)
            mate_ref[b * LANES : (b + 1) * LANES, lane(q)] = jnp.where(hot, 1.0, 0.0).astype(BF)
        scales.append(jnp.broadcast_to(jnp.sum(found, axis=1, keepdims=True), (LANES, LANES)))
    mate_scale = jnp.concatenate(scales, axis=0)
    mate = jnp.dot(mate_ref[...], embed_ref[...], preferred_element_type=F32).astype(BF)
    soft = jnp.concatenate([as_column(soft_ref[pl.ds(base + b, 1), :]) for b in range(rows // LANES)], axis=0)
    inv_soft = 10.0 / soft
    loss_acc = jnp.zeros((8, LANES), F32)
    for j in range(cols // TILE):
        span = slice(j * TILE, (j + 1) * TILE)
        scores = jnp.dot(embed_ref[here, :], proto_t_ref[:, span], preferred_element_type=F32)
        mates = jnp.dot(mate, proto_t_ref[:, span], preferred_element_type=F32)
        for h in range(chunks):
            at = j * chunks + h
            target = jnp.exp2(mates[:, lane(h)] * (20.0 * LOG2_E)) * mate_scale * col_ref[at : at + 1, :]
            score = scores[:, lane(h)]
            loss_acc += fold_rows(target * score)
            grad_ref[here, lane(at)] = (jnp.exp2(score * (10.0 * LOG2_E)) * inv_soft - target).astype(BF)

    @pl.when(step == 0)
    def _():
        copies[2].wait()

    d_unit_ref[...] = jnp.dot(grad_ref[here, :], proto_ref[...], preferred_element_type=F32).astype(BF)
    loss_acc_ref[0:8, :] += loss_acc

    @pl.when(step == pl.num_programs(0) - 1)
    def _():
        copies[3].wait()
        embed_t = embed_ref[...].T
        for j in range(cols // TILE):
            span = slice(j * TILE, (j + 1) * TILE)
            raw = raw_t_ref[:, span].astype(F32)
            scale = lax.rsqrt(jnp.sum(raw * raw, axis=0, keepdims=True) + 1e-06)
            unit = raw * scale
            acc = jnp.dot(embed_t, grad_ref[:, span], preferred_element_type=F32)
            term_ref[:, span] = ((acc - unit * jnp.sum(unit * acc, axis=0, keepdims=True)) * scale).astype(BF)
        pieces = (piece0_ref, piece1_ref, piece2_ref, piece3_ref)
        for d, piece in enumerate(pieces):
            height = piece.shape[0]
            at = pl.multiple_of(lax.rem(order_ref[9] + d, len(pieces)) * height, height)
            piece[...] = term_ref[pl.ds(at, height), :]
        loss_ref[...] = loss_acc_ref[...]


def d_embed_kernel(recv_ref, unit_ref, scale_ref, msg_ref):
    d_unit = jnp.sum(recv_ref[...].astype(F32), axis=0)
    unit = unit_ref[...]
    d_embed = (d_unit - unit * jnp.sum(unit * d_unit, axis=1, keepdims=True)) * scale_ref[:, :1]
    msg_ref[...] = jnp.broadcast_to(d_embed.astype(BF)[None], msg_ref.shape)


def start_parts(parts, buf_ref, sems):
    copies = []
    at = 0
    for k, part in enumerate(parts):
        height = part.shape[0]
        copies.append(pltpu.make_async_copy(part, buf_ref.at[at : at + height], sems.at[k]))
        at += height
    for copy in copies:
        copy.start()
    return copies


def slab_kernel(order_ref, mean_ref, inv_ref, gain_ref, bias_ref, w_hbm, *rest):
    parts = rest[:-6]
    normed_ref, slope_ref, hid_ref, buf_ref, w_ref, sems = rest[-6:]
    rows, slab = normed_ref.shape
    at = pl.ds(pl.multiple_of(order_ref[0] * slab, slab), slab)
    w_copy = pltpu.make_async_copy(w_hbm.at[:, at], w_ref, sems.at[len(parts)])
    w_copy.start()
    copies = start_parts(parts, buf_ref, sems)
    w_copy.wait()
    chunks = slab // LANES
    ones = jnp.ones((LANES, LANES), F32)
    for g in range(2):
        for copy in copies[g * len(parts) // 2 : (g + 1) * len(parts) // 2]:
            copy.wait()
        start = g * rows // 2
        pre = jnp.dot(buf_ref[start : start + rows // 2, :], w_ref[...], preferred_element_type=F32)
        for h in range(chunks):
            at = pl.ds(order_ref[0] * chunks + h, 1)
            mean, inv, gain, bias = mean_ref[at, :], inv_ref[at, :], gain_ref[at, :], bias_ref[at, :]
            for b in range(rows // 2 // LANES):
                band = slice(start + b * LANES, start + (b + 1) * LANES)
                normed = (pre[b * LANES : (b + 1) * LANES, lane(h)] - mean) * inv
                hidden, back = jax.vjp(jax.nn.gelu, normed * gain + bias)
                normed_ref[band, lane(h)] = normed.astype(BF)
                slope_ref[band, lane(h)] = back(ones)[0].astype(BF)
                hid_ref[band, lane(h)] = hidden.astype(BF)


def shift_kernel(
    order_ref, d_embed_ref, w2_ref, normed_ref, slope_ref, hid_ref, loss_ref, shift_ref, msg_ref, sum_ref
):
    n_blocks, own, _ = d_embed_ref.shape
    sum_ref[...] = jnp.zeros_like(sum_ref)
    gains = biases = second = None
    for k in range(0, n_blocks, 2):
        d_embed = jnp.concatenate([d_embed_ref[order_ref[k + 1]], d_embed_ref[order_ref[k + 2]]], axis=0)
        band = slice(k * own, (k + 2) * own)
        d_shift = tdot(d_embed, w2_ref[...], 1, 1) * slope_ref[band, :].astype(F32)
        shift_ref[band, :] = d_shift
        gain = jnp.sum(d_shift * normed_ref[band, :].astype(F32), axis=0, keepdims=True)
        bias = jnp.sum(d_shift, axis=0, keepdims=True)
        part = tdot(hid_ref[band, :], d_embed, 0, 0)
        gains = gain if gains is None else gains + gain
        biases = bias if biases is None else biases + bias
        second = part if second is None else second + part
    hits = jnp.sum(loss_ref[0:8, :], axis=0, keepdims=True)
    logs = jnp.sum(loss_ref[8:16, :], axis=0, keepdims=True)
    sum_ref[0:1, :] = gains
    sum_ref[1:2, :] = biases
    sum_ref[2:3, :] = jnp.concatenate([hits, logs], axis=1)
    n, _, slab = msg_ref.shape
    share = slab // n
    sums = sum_ref[...]
    high = sums.astype(BF)
    rest = sums - high.astype(F32)
    mid = rest.astype(BF)
    low = (rest - mid.astype(F32)).astype(BF)
    row = lax.broadcasted_iota(jnp.int32, sums.shape, 0)
    lower = jnp.where(row < 4, mid.astype(F32), pltpu.roll(low.astype(F32), 4, 0))
    packed = jnp.concatenate([high.astype(F32), lower], axis=0).astype(BF)
    msg_ref[:, :share, :] = jnp.broadcast_to(packed[None], (n, share, slab))
    msg_ref[:, share:, :] = second.astype(BF).reshape(n, share, slab)


def first_kernel(total_rows, order_ref, recv_ref, shift_ref, normed_ref, inv_ref, gain_ref, *rest):
    parts = rest[:-6]
    out_ref, sums_ref, second_ref, d_pre_ref, buf_ref, sems = rest[-6:]
    copies = start_parts(parts, buf_ref, sems)
    share = second_ref.shape[0]
    second_ref[...] = jnp.sum(recv_ref[:, share:, :].astype(F32), axis=0)
    got = jnp.sum(recv_ref[:, :share, :].astype(F32), axis=0)
    got = got[0:8] + (got[8:16] + pltpu.roll(got[8:16], 4, 0))
    sums_ref[...] = got
    chunks = d_pre_ref.shape[1] // LANES
    for h in range(chunks):
        at = pl.ds(order_ref[0] * chunks + h, 1)
        factor = gain_ref[at, :] * inv_ref[at, :]
        gain_mean = got[0:1, lane(h)] / total_rows
        bias_mean = got[1:2, lane(h)] / total_rows
        for b in range(d_pre_ref.shape[0] // LANES):
            band = slice(b * LANES, (b + 1) * LANES)
            d_pre = factor * (shift_ref[band, lane(h)] - bias_mean - normed_ref[band, lane(h)].astype(F32) * gain_mean)
            d_pre_ref[band, lane(h)] = d_pre.astype(BF)
    for copy in copies:
        copy.wait()
    _, share, slab = out_ref.shape
    group = TILE // share
    for j in range(buf_ref.shape[1] // TILE):
        grad = tdot(buf_ref[:, j * TILE : (j + 1) * TILE], d_pre_ref[...], 0, 0)
        out_ref[j * group : (j + 1) * group] = grad.astype(BF).reshape(group, share, slab)


def tail_kernel(recv_ref, out_ref):
    n_batch, n_proto, _, slab = recv_ref.shape
    for p in range(n_proto):
        acc = recv_ref[0, p].astype(F32)
        for b in range(1, n_batch):
            acc += recv_ref[b, p].astype(F32)
        out_ref[:, p * slab : (p + 1) * slab] = acc


def stage_kernel(order_ref, in0_ref, in1_ref, in2_ref, in3_ref, out0_ref, out1_ref, out2_ref, out3_ref, sum_ref):
    near = in0_ref[...].astype(F32) + in1_ref[...].astype(F32)
    sum_ref[...] = (near + (in2_ref[...].astype(F32) + in3_ref[...].astype(F32))).astype(BF)
    outs = (out0_ref, out1_ref, out2_ref, out3_ref)
    for d, out in enumerate(outs):
        height = out.shape[0]
        at = pl.multiple_of(lax.rem(order_ref[10] + d, len(outs)) * height, height)
        out[...] = sum_ref[pl.ds(at, height), :]


def sums_kernel(total_rows, order_ref, *rest):
    shown = rest[:-3]
    gain_ref, bias_ref, loss_ref = rest[-3:]
    n_proto = len(shown)
    hits = jnp.zeros((1, LANES), F32)
    for d, ref in enumerate(shown):
        at = pl.ds(lax.rem(order_ref[0] + n_proto - d, n_proto), 1)
        gain_ref[at, :] = ref[0:1, :]
        bias_ref[at, :] = ref[1:2, :]
        hits += ref[2:3, :LANES]
    loss = jnp.sum(shown[0][2:3, LANES:] - hits, axis=1, keepdims=True) / total_rows
    loss_ref[...] = jnp.broadcast_to(loss, loss_ref.shape)


def shape(dims, kind=F32):
    return jax.ShapeDtypeStruct(dims, kind)


def step_of_device(features, w_first, bn_gain, bn_bias, w_second, prototypes, pair):
    n_batch = lax.axis_size("batch")
    n_proto = lax.axis_size("proto")
    own, d_in = features.shape
    d_hid, width = w_second.shape
    cols = prototypes.shape[0]
    total_rows = own * n_batch * n_proto
    rows = own * n_proto
    part = lax.axis_index("proto")
    slab = d_hid // n_proto
    col_bands = cols // LANES
    row_bands = rows // LANES
    hid_bands = d_hid // LANES
    steps = rows // TILE
    gain = bn_gain.reshape(hid_bands, LANES)
    bias = bn_bias.reshape(hid_bands, LANES)

    def hop(x, moves):
        return lax.ppermute(x, "proto", moves)

    ring = n_proto // 2
    right = [(i * 2 + c, (i + 1) % ring * 2 + c) for i in range(ring) for c in range(2)]
    left = [(t, s) for s, t in right]
    swap = [(i, i ^ 1) for i in range(n_proto)]
    from_left = hop(features, right)
    from_right = hop(features, left)
    across = lax.shift_right_logical(part, 1)
    place = lax.axis_index("batch")
    side = 4
    order = jnp.stack(
        [part]
        + [
            (lax.bitwise_and(across + d, ring - 1) * 2 + lax.bitwise_and(part, 1)) ^ o
            for o in range(2)
            for d in (0, 1, 3, 2)
        ]
        + [lax.shift_right_logical(place, 2), lax.bitwise_and(place, side - 1)]
    ).astype(jnp.int32)
    mate_row = (pair - place * rows).astype(F32).reshape(row_bands, LANES)

    anywhere = pl.BlockSpec(memory_space=pl.ANY)
    pre, msg = pl.pallas_call(
        pre_kernel,
        in_specs=[pl.BlockSpec(features.shape, lambda: (0, 0)), anywhere],
        out_shape=[shape((own, d_hid)), shape((n_batch, 2 * hid_bands, LANES))],
        scratch_shapes=[
            pltpu.VMEM((2 * hid_bands, LANES), F32),
            pltpu.VMEM((d_hid // TILE, d_in, TILE), BF),
            pltpu.SemaphoreType.DMA((d_hid // TILE,)),
        ],
        name="pre_kernel",
    )(features, w_first)
    near_left, near_right, _ = lax.optimization_barrier((from_left, from_right, pre))
    far_top = hop(near_left[: own // 2], right)
    far_low = hop(near_right[own // 2 :], left)
    got = deal(msg, "batch")
    got, far_top, far_low, mate_row, order = lax.optimization_barrier((got, far_top, far_low, mate_row, order))
    mine = [features, from_right, from_left, far_top, far_low]
    parts = mine + [hop(piece, swap) for piece in mine]
    msg = pl.pallas_call(
        relay_kernel, out_shape=shape((n_proto, 2 * hid_bands, LANES)), compiler_params=PARAMS, name="relay_kernel"
    )(got)
    raw, _ = lax.optimization_barrier((prototypes, msg))
    proto_bf, proto_t, raw_t = pl.pallas_call(
        proto_kernel,
        out_shape=[shape((cols, width), BF), shape((width, cols), BF), shape((width, cols), BF)],
        name="proto_kernel",
    )(raw)
    got, proto_bf, proto_t, raw_t = lax.optimization_barrier((deal(msg, "proto"), proto_bf, proto_t, raw_t))
    unit_embed, embed_scale, mean, inv, msg = pl.pallas_call(
        lambda *refs: embed_kernel(total_rows, *refs),
        in_specs=[anywhere, pl.BlockSpec((n_proto, 2 * hid_bands, LANES), lambda: (0, 0, 0))]
        + [pl.BlockSpec((hid_bands, LANES), lambda: (0, 0))] * 2
        + [anywhere],
        out_shape=[
            shape((own, width)),
            shape((own, LANES)),
            shape((hid_bands, LANES)),
            shape((hid_bands, LANES)),
            shape((n_proto, own, width), BF),
        ],
        scratch_shapes=[
            pltpu.VMEM((own, d_hid), BF),
            pltpu.VMEM((own, d_hid), F32),
            pltpu.VMEM((d_hid, width), BF),
            pltpu.SemaphoreType.DMA((2,)),
        ],
        name="embed_kernel",
    )(pre, got, gain, bias, w_second)
    stat_spec = whole((hid_bands, LANES))
    normed, slope, hid = pl.pallas_call(
        slab_kernel,
        grid_spec=pltpu.PrefetchScalarGridSpec(
            num_scalar_prefetch=1,
            grid=(1,),
            in_specs=[stat_spec] * 4 + [anywhere] * (1 + len(parts)),
            out_specs=[whole((rows, slab))] * 3,
            scratch_shapes=[
                pltpu.VMEM((rows, d_in), BF),
                pltpu.VMEM((d_in, slab), BF),
                pltpu.SemaphoreType.DMA((len(parts) + 1,)),
            ],
        ),
        out_shape=[shape((rows, slab), BF)] * 3,
        name="slab_kernel",
    )(order, mean, inv, gain, bias, w_first, *parts)
    block_embed, normed, slope, hid = lax.optimization_barrier((deal(msg, "proto"), normed, slope, hid))
    block_embed = block_embed.reshape(rows, width)

    kern, col_msg, soft = pl.pallas_call(
        score_kernel,
        grid=(steps,),
        in_specs=[rows_of(TILE, width), anywhere],
        out_specs=[rows_of(TILE, cols), whole((n_batch, col_bands, LANES)), whole((row_bands, LANES))],
        out_shape=[shape((rows, cols), BF), shape((n_batch, col_bands, LANES)), shape((row_bands, LANES))],
        scratch_shapes=[
            pltpu.VMEM((col_bands * 8, LANES), F32),
            pltpu.VMEM((width, cols), BF),
            pltpu.SemaphoreType.DMA((cols // TILE,)),
        ],
        compiler_params=PARAMS,
        name="score_kernel",
    )(block_embed, proto_t)

    def row_pass(recv, extra):
        height = row_bands * (2 if extra else 1)
        return pl.pallas_call(
            row_kernel,
            grid=(steps,),
            in_specs=[whole((n_batch, col_bands, LANES)), rows_of(TILE, cols)]
            + [whole((row_bands, LANES)) for _ in extra],
            out_specs=whole((n_proto, height, LANES)),
            out_shape=shape((n_proto, height, LANES)),
            scratch_shapes=[pltpu.VMEM((col_bands, LANES), F32)],
            compiler_params=PARAMS,
        name="row_kernel",
        )(recv, kern, *extra)

    def col_pass(recv):
        return pl.pallas_call(
            col_kernel,
            grid=(steps,),
            in_specs=[whole(recv.shape), rows_of(TILE, cols)],
            out_specs=whole((n_batch, col_bands, LANES)),
            out_shape=shape((n_batch, col_bands, LANES)),
            scratch_shapes=[pltpu.VMEM((col_bands * 8, LANES), F32), pltpu.VMEM((row_bands, LANES), F32)],
            compiler_params=PARAMS,
        name="col_kernel",
        )(recv, kern)

    recv_soft = None
    for step in range(ITERS):
        recv_col = deal(col_msg, "batch")
        recv_row = deal(row_pass(recv_col, () if step else (soft,)), "proto")
        recv_soft = recv_row if recv_soft is None else recv_soft
        if step + 1 < ITERS:
            col_msg = col_pass(recv_row)

    d_unit, *pieces, loss_tile = pl.pallas_call(
        final_kernel,
        grid=(steps,),
        in_specs=[
            pl.BlockSpec(memory_space=pltpu.SMEM),
            anywhere,
            whole((row_bands, LANES)),
            anywhere,
            anywhere,
            anywhere,
            whole(recv_col.shape),
            whole(recv_row.shape),
            whole(recv_soft.shape),
        ],
        out_specs=[rows_of(TILE, width)] + [whole((width // side, cols))] * side + [whole((16, LANES))],
        out_shape=[shape((rows, width), BF)] + [shape((width // side, cols), BF)] * side + [shape((16, LANES))],
        scratch_shapes=[
            pltpu.VMEM((rows, cols), BF),
            pltpu.VMEM((TILE, rows), BF),
            pltpu.VMEM((16, LANES), F32),
            pltpu.VMEM((col_bands, LANES), F32),
            pltpu.VMEM((row_bands, LANES), F32),
            pltpu.VMEM((row_bands, LANES), F32),
            pltpu.VMEM((rows, width), BF),
            pltpu.VMEM((width, cols), BF),
            pltpu.VMEM((cols, width), BF),
            pltpu.VMEM((width, cols), BF),
            pltpu.VMEM((width, cols), BF),
            pltpu.SemaphoreType.DMA((4,)),
        ],
        name="final_kernel",
    )(order, block_embed, mate_row, proto_t, proto_bf, raw_t, recv_col, recv_row, recv_soft)


    def shifted(axis, d):
        moves = []
        for b in range(n_batch):
            y, z = divmod(b, side)
            moves.append((b, (y + d) % side * side + z if axis == 0 else y * side + (z + d) % side))
        return moves

    pieces = [pieces[0]] + [lax.ppermute(pieces[d], "batch", shifted(0, d)) for d in range(1, side)]
    d_unit = deal(d_unit.reshape(n_proto, own, width), "proto")
    d_embed = pl.pallas_call(
        d_embed_kernel, out_shape=shape((n_proto, own, width), BF), compiler_params=PARAMS, name="d_embed_kernel"
    )(d_unit, unit_embed, embed_scale)
    d_embed = deal(d_embed, "proto")

    shift, msg = pl.pallas_call(
        shift_kernel,
        grid_spec=pltpu.PrefetchScalarGridSpec(
            num_scalar_prefetch=1,
            grid=(1,),
            in_specs=[
                whole((n_proto, own, width)),
                pl.BlockSpec((slab, width), lambda i, s: (s[0], 0)),
                whole((rows, slab)),
                whole((rows, slab)),
                whole((rows, slab)),
                whole((16, LANES)),
            ],
            out_specs=[whole((rows, slab)), whole((n_batch, 2 * slab // n_batch, width))],
            scratch_shapes=[pltpu.VMEM((8, slab), F32)],
        ),
        out_shape=[shape((rows, slab)), shape((n_batch, 2 * slab // n_batch, width), BF)],
        compiler_params=PARAMS,
        name="shift_kernel",
    )(order, d_embed, w_second, normed, slope, hid, loss_tile)
    recv = deal(msg, "batch")

    share = d_in // (n_batch * n_proto)
    first, sums, second = pl.pallas_call(
        lambda *refs: first_kernel(total_rows, *refs),
        grid_spec=pltpu.PrefetchScalarGridSpec(
            num_scalar_prefetch=1,
            grid=(1,),
            in_specs=[whole(recv.shape), whole((rows, slab)), whole((rows, slab)), stat_spec, stat_spec]
            + [anywhere] * len(parts),
            out_specs=[
                whole((n_batch * n_proto, share, slab)),
                whole((8, slab)),
                whole((slab // n_batch, width)),
            ],
            scratch_shapes=[
                pltpu.VMEM((rows, slab), BF),
                pltpu.VMEM((rows, d_in), BF),
                pltpu.SemaphoreType.DMA((len(parts),)),
            ],
        ),
        out_shape=[
            shape((n_batch * n_proto, share, slab), BF),
            shape((8, slab)),
            shape((slab // n_batch, width)),
        ],
        name="first_kernel",
    )(order, recv, shift, normed, inv, gain, *parts)

    first, *pieces = lax.optimization_barrier((first, *pieces))
    pieces = pl.pallas_call(
        stage_kernel,
        in_specs=[pl.BlockSpec(memory_space=pltpu.SMEM)] + [pl.BlockSpec((width // side, cols), lambda: (0, 0))] * side,
        out_shape=[shape((width // n_batch, cols), BF)] * side,
        scratch_shapes=[pltpu.VMEM((width // side, cols), BF)],
        name="stage_kernel",
    )(order, *pieces)
    pieces = [pieces[0]] + [lax.ppermute(pieces[d], "batch", shifted(1, d)) for d in range(1, side)]
    grad_proto = sum(piece.astype(F32) for piece in pieces).T
    first = deal(first, ("batch", "proto")).reshape(n_batch, n_proto, share, slab)
    grad_first = pl.pallas_call(
        tail_kernel, out_shape=shape((share, d_hid)), compiler_params=PARAMS, name="tail_kernel"
    )(first)
    grad_second = lax.ppermute(
        second,
        ("batch", "proto"),
        [(b * n_proto + p, p * n_batch + b) for b in range(n_batch) for p in range(n_proto)],
    )
    shown = [sums] + [
        hop(sums, [(i, (i + d) % n_proto) for i in range(n_proto)]) for d in range(1, n_proto)
    ]
    grad_gain, grad_bias, loss = pl.pallas_call(
        lambda *refs: sums_kernel(total_rows, *refs),
        in_specs=[pl.BlockSpec(memory_space=pltpu.SMEM)] + [pl.BlockSpec((8, slab), lambda: (0, 0))] * n_proto,
        out_shape=[shape((n_proto, slab)), shape((n_proto, slab)), shape((1, LANES))],
        compiler_params=PARAMS,
        name="sums_kernel",
    )(order, *shown)
    grad_gain = grad_gain.reshape(-1)
    grad_bias = grad_bias.reshape(-1)
    loss = loss[0, 0]
    return (grad_first, grad_second, grad_gain, grad_bias, grad_proto, loss)


def solution(mesh):
    return jax.shard_map(
        step_of_device,
        mesh=mesh,
        in_specs=(P(("batch", "proto"), None), P(), P(), P(), P(), P("proto", None), P("batch")),
        out_specs=(
            P(("batch", "proto"), None),
            P(("batch", "proto"), None),
            P(),
            P(),
            P("proto", "batch"),
            P(),
        ),
        check_vma=False,
    )
```

```python
import jax
import jax.numpy as jnp
from jax import lax
from jax.experimental import pallas as pl
from jax.experimental.pallas import tpu as pltpu
from jax.sharding import PartitionSpec as P


ITERS = 3
BF = jnp.bfloat16
F32 = jnp.float32
LANES = 128
TILE = 256
LOG2_E = 1.4426950408889634
PARAMS = pltpu.CompilerParams(vmem_limit_bytes=24 * 1024 * 1024)


def deal(x, axis):
    return lax.all_to_all(x, axis, 0, 0, tiled=True)


def tdot(a, b, a_dim, b_dim):
    return lax.dot_general(a, b, (((a_dim,), (b_dim,)), ((), ())), preferred_element_type=F32)


def fold_rows(v):
    return jnp.sum(v.reshape(v.shape[0] // 8, 8, LANES), axis=0)


def as_column(row):
    return jnp.broadcast_to(row, (LANES, LANES)).T


def lane(j):
    return slice(j * LANES, (j + 1) * LANES)


def whole(shape):
    return pl.BlockSpec(shape, lambda i, *_: (0,) * len(shape))


def rows_of(rows, width):
    return pl.BlockSpec((rows, width), lambda i, *_: (i, 0))


def pre_kernel(features_ref, w_hbm, pre_ref, msg_ref, stat_ref, w_buf, sems):
    pieces = w_buf.shape[0]
    copies = [
        pltpu.make_async_copy(w_hbm.at[:, k * TILE : (k + 1) * TILE], w_buf.at[k], sems.at[k]) for k in range(pieces)
    ]
    for copy in copies:
        copy.start()
    chunks = TILE // LANES
    half = stat_ref.shape[0] // 2
    for k in range(pieces):
        copies[k].wait()
        pre = jnp.dot(features_ref[...], w_buf[k], preferred_element_type=F32)
        pre_ref[:, k * TILE : (k + 1) * TILE] = pre
        for h in range(chunks):
            at = k * chunks + h
            part = pre[:, lane(h)]
            stat_ref[at : at + 1, :] = jnp.sum(part, axis=0, keepdims=True)
            stat_ref[half + at : half + at + 1, :] = jnp.sum(part * part, axis=0, keepdims=True)
    msg_ref[...] = jnp.broadcast_to(stat_ref[...][None], msg_ref.shape)


def relay_kernel(recv_ref, msg_ref):
    msg_ref[...] = jnp.broadcast_to(jnp.sum(recv_ref[...], axis=0, keepdims=True), msg_ref.shape)


def embed_kernel(
    total_rows, pre_hbm, recv_ref, gain_ref, bias_ref, w2_hbm, unit_ref, scale_ref, mean_ref, inv_ref, msg_ref, hid_ref,
    pre_ref, w2_ref, sems,
):
    pre_copy = pltpu.make_async_copy(pre_hbm, pre_ref, sems.at[0])
    w2_copy = pltpu.make_async_copy(w2_hbm, w2_ref, sems.at[1])
    pre_copy.start()
    w2_copy.start()
    stats = jnp.sum(recv_ref[...], axis=0)
    half = stats.shape[0] // 2
    mean = stats[:half] / total_rows
    inv = lax.rsqrt(stats[half:] / total_rows - mean * mean + 1e-05)
    mean_ref[...] = mean
    inv_ref[...] = inv
    pre_copy.wait()
    for j in range(half):
        normed = (pre_ref[:, lane(j)] - mean[j : j + 1]) * inv[j : j + 1]
        hid_ref[:, lane(j)] = jax.nn.gelu(normed * gain_ref[j : j + 1, :] + bias_ref[j : j + 1, :]).astype(BF)
    w2_copy.wait()
    embed = jnp.dot(hid_ref[...], w2_ref[...], preferred_element_type=F32)
    scale = lax.rsqrt(jnp.sum(embed * embed, axis=1, keepdims=True) + 1e-06)
    unit = embed * scale
    unit_ref[...] = unit
    scale_ref[...] = jnp.broadcast_to(scale, scale_ref.shape)
    msg_ref[...] = jnp.broadcast_to(unit.astype(BF)[None], msg_ref.shape)


def proto_kernel(raw_ref, proto_ref, proto_t_ref, raw_t_ref):
    for k in range(raw_ref.shape[0] // TILE):
        span = slice(k * TILE, (k + 1) * TILE)
        raw_t = raw_ref[span, :].T
        raw_t_ref[:, span] = raw_t
        wide = raw_t.astype(F32)
        unit = (wide * lax.rsqrt(jnp.sum(wide * wide, axis=0, keepdims=True) + 1e-06)).astype(BF)
        proto_t_ref[:, span] = unit
        proto_ref[span, :] = unit.T


def score_kernel(embed_ref, proto_t_hbm, kern_ref, msg_ref, soft_ref, acc_ref, proto_t_ref, sems):
    step = pl.program_id(0)
    rows = embed_ref.shape[0]
    cols = proto_t_ref.shape[1]

    def copy(j):
        span = slice(j * TILE, (j + 1) * TILE)
        return pltpu.make_async_copy(proto_t_hbm.at[:, span], proto_t_ref.at[:, span], sems.at[j])

    @pl.when(step == 0)
    def _():
        for j in range(cols // TILE):
            copy(j).start()
        acc_ref[...] = jnp.zeros_like(acc_ref)
        for j in range(cols // TILE):
            copy(j).wait()

    soft = [None] * (rows // LANES)
    for j in range(cols // TILE):
        span = slice(j * TILE, (j + 1) * TILE)
        scores = jnp.dot(embed_ref[...], proto_t_ref[:, span], preferred_element_type=F32)
        tempered = jnp.exp2(scores * (10.0 * LOG2_E))
        kern = tempered * tempered
        kern_ref[:, span] = kern.astype(BF)
        for h in range(TILE // LANES):
            at = (j * (TILE // LANES) + h) * 8
            acc_ref[at : at + 8, :] += fold_rows(kern[:, lane(h)])
        for b in range(rows // LANES):
            part = tempered[b * LANES : (b + 1) * LANES]
            part = part[:, :LANES] + part[:, LANES:]
            soft[b] = part if soft[b] is None else soft[b] + part
    for b in range(rows // LANES):
        soft_ref[pl.ds(step * (rows // LANES) + b, 1), :] = jnp.sum(soft[b].T, axis=0, keepdims=True)

    @pl.when(step == pl.num_programs(0) - 1)
    def _():
        total = jnp.sum(acc_ref[...].reshape(cols // LANES, 8, LANES), axis=1)
        msg_ref[...] = jnp.broadcast_to(total[None], msg_ref.shape)


def row_kernel(recv_ref, kern_ref, *rest):
    soft_ref = rest[0] if len(rest) == 3 else None
    msg_ref, scale_ref = rest[-2:]
    step = pl.program_id(0)
    rows = kern_ref.shape[0]
    copies = msg_ref.shape[0]

    @pl.when(step == 0)
    def _():
        scale_ref[...] = 1.0 / jnp.sum(recv_ref[...], axis=0)
        if soft_ref is not None:
            half = soft_ref.shape[0]
            msg_ref[:, half:, :] = jnp.broadcast_to(soft_ref[...][None], (copies, half, LANES))

    for b in range(rows // LANES):
        acc = None
        for j in range(scale_ref.shape[0]):
            part = kern_ref[b * LANES : (b + 1) * LANES, lane(j)].astype(F32) * scale_ref[j : j + 1, :]
            acc = part if acc is None else acc + part
        row = jnp.sum(acc.T, axis=0, keepdims=True)
        msg_ref[:, pl.ds(step * (rows // LANES) + b, 1), :] = jnp.broadcast_to(row[None], (copies, 1, LANES))


def col_kernel(recv_ref, kern_ref, msg_ref, acc_ref, scale_ref):
    step = pl.program_id(0)
    rows, cols = kern_ref.shape

    @pl.when(step == 0)
    def _():
        acc_ref[...] = jnp.zeros_like(acc_ref)
        scale_ref[...] = 1.0 / jnp.sum(recv_ref[:, : scale_ref.shape[0], :], axis=0)

    for b in range(rows // LANES):
        scale = as_column(scale_ref[pl.ds(step * (rows // LANES) + b, 1), :])
        for j in range(cols // LANES):
            part = kern_ref[b * LANES : (b + 1) * LANES, lane(j)].astype(F32) * scale
            acc_ref[j * 8 : (j + 1) * 8, :] += fold_rows(part)

    @pl.when(step == pl.num_programs(0) - 1)
    def _():
        total = jnp.sum(acc_ref[...].reshape(cols // LANES, 8, LANES), axis=1)
        msg_ref[...] = jnp.broadcast_to(total[None], msg_ref.shape)


def final_kernel(
    order_ref, embed_hbm, pair_ref, proto_t_hbm, proto_hbm, raw_t_hbm, recv_col_ref, recv_row_ref, recv_soft_ref,
    d_unit_ref, piece0_ref, piece1_ref, piece2_ref, piece3_ref, loss_ref,
    grad_ref, mate_ref, loss_acc_ref, col_ref, row_ref, soft_ref, embed_ref, proto_t_ref, proto_ref, raw_t_ref, term_ref, both_ref, sems,
):
    pairs = ((embed_hbm, embed_ref), (proto_t_hbm, proto_t_ref), (proto_hbm, proto_ref), (raw_t_hbm, raw_t_ref))
    copies = [pltpu.make_async_copy(src, dst, sems.at[k]) for k, (src, dst) in enumerate(pairs)]
    step = pl.program_id(0)
    rows = d_unit_ref.shape[0]
    cols = proto_t_ref.shape[1]
    bands = row_ref.shape[0]
    chunks = TILE // LANES

    @pl.when(step == 0)
    def _():
        for copy in copies:
            copy.start()
        loss_acc_ref[...] = jnp.zeros_like(loss_acc_ref)
        col_ref[...] = 10.0 / jnp.sum(recv_col_ref[...], axis=0)
        row_ref[...] = 1.0 / jnp.sum(recv_row_ref[:, :bands, :], axis=0)
        soft_ref[...] = jnp.sum(recv_soft_ref[:, bands:, :], axis=0)
        loss_acc_ref[8:16, :] = jnp.log(soft_ref[...])
        copies[0].wait()
        copies[1].wait()

    base = step * (rows // LANES)
    here = pl.ds(pl.multiple_of(step * rows, rows), rows)
    spot = lax.broadcasted_iota(jnp.int32, (LANES, LANES), 1)
    scales = []
    for b in range(rows // LANES):
        pair = as_column(pair_ref[pl.ds(base + b, 1), :]).astype(jnp.int32)
        found = jnp.zeros((LANES, LANES), F32)
        for q in range(bands):
            hot = spot + q * LANES == pair
            found += jnp.where(hot, row_ref[q : q + 1, :], 0.0)
            mate_ref[b * LANES : (b + 1) * LANES, lane(q)] = jnp.where(hot, 1.0, 0.0).astype(BF)
        scales.append(jnp.broadcast_to(jnp.sum(found, axis=1, keepdims=True), (LANES, LANES)))
    mate_scale = jnp.concatenate(scales, axis=0)
    both_ref[0:rows, :] = embed_ref[here, :]
    both_ref[rows:, :] = jnp.dot(mate_ref[...], embed_ref[...], preferred_element_type=F32).astype(BF)
    soft = jnp.concatenate([as_column(soft_ref[pl.ds(base + b, 1), :]) for b in range(rows // LANES)], axis=0)
    inv_soft = 10.0 / soft
    loss_acc = jnp.zeros((8, LANES), F32)
    for j in range(cols // TILE):
        span = slice(j * TILE, (j + 1) * TILE)
        both = jnp.dot(both_ref[...], proto_t_ref[:, span], preferred_element_type=F32)
        scores, mates = both[:rows], both[rows:]
        for h in range(chunks):
            at = j * chunks + h
            target = jnp.exp2(mates[:, lane(h)] * (20.0 * LOG2_E)) * mate_scale * col_ref[at : at + 1, :]
            score = scores[:, lane(h)]
            loss_acc += fold_rows(target * score)
            grad_ref[here, lane(at)] = (jnp.exp2(score * (10.0 * LOG2_E)) * inv_soft - target).astype(BF)

    @pl.when(step == 0)
    def _():
        copies[2].wait()

    d_unit_ref[...] = jnp.dot(grad_ref[here, :], proto_ref[...], preferred_element_type=F32).astype(BF)
    loss_acc_ref[0:8, :] += loss_acc

    @pl.when(step == pl.num_programs(0) - 1)
    def _():
        copies[3].wait()
        embed_t = embed_ref[...].T
        for j in range(cols // TILE):
            span = slice(j * TILE, (j + 1) * TILE)
            raw = raw_t_ref[:, span].astype(F32)
            scale = lax.rsqrt(jnp.sum(raw * raw, axis=0, keepdims=True) + 1e-06)
            unit = raw * scale
            acc = jnp.dot(embed_t, grad_ref[:, span], preferred_element_type=F32)
            term_ref[:, span] = ((acc - unit * jnp.sum(unit * acc, axis=0, keepdims=True)) * scale).astype(BF)
        pieces = (piece0_ref, piece1_ref, piece2_ref, piece3_ref)
        for d, piece in enumerate(pieces):
            height = piece.shape[0]
            at = pl.multiple_of(lax.rem(order_ref[9] + d, len(pieces)) * height, height)
            piece[...] = term_ref[pl.ds(at, height), :]
        loss_ref[...] = loss_acc_ref[...]


def d_embed_kernel(recv_ref, unit_ref, scale_ref, msg_ref):
    d_unit = jnp.sum(recv_ref[...].astype(F32), axis=0)
    unit = unit_ref[...]
    d_embed = (d_unit - unit * jnp.sum(unit * d_unit, axis=1, keepdims=True)) * scale_ref[:, :1]
    msg_ref[...] = jnp.broadcast_to(d_embed.astype(BF)[None], msg_ref.shape)


def start_parts(parts, buf_ref, sems):
    copies = []
    at = 0
    for k, part in enumerate(parts):
        height = part.shape[0]
        copies.append(pltpu.make_async_copy(part, buf_ref.at[at : at + height], sems.at[k]))
        at += height
    for copy in copies:
        copy.start()
    return copies


def slab_kernel(order_ref, mean_ref, inv_ref, gain_ref, bias_ref, w_hbm, *rest):
    parts = rest[:-6]
    normed_ref, slope_ref, hid_ref, buf_ref, w_ref, sems = rest[-6:]
    rows, slab = normed_ref.shape
    at = pl.ds(pl.multiple_of(order_ref[0] * slab, slab), slab)
    w_copy = pltpu.make_async_copy(w_hbm.at[:, at], w_ref, sems.at[len(parts)])
    w_copy.start()
    copies = start_parts(parts, buf_ref, sems)
    w_copy.wait()
    chunks = slab // LANES
    ones = jnp.ones((LANES, LANES), F32)
    for g in range(2):
        for copy in copies[g * len(parts) // 2 : (g + 1) * len(parts) // 2]:
            copy.wait()
        start = g * rows // 2
        pre = jnp.dot(buf_ref[start : start + rows // 2, :], w_ref[...], preferred_element_type=F32)
        for h in range(chunks):
            at = pl.ds(order_ref[0] * chunks + h, 1)
            mean, inv, gain, bias = mean_ref[at, :], inv_ref[at, :], gain_ref[at, :], bias_ref[at, :]
            for b in range(rows // 2 // LANES):
                band = slice(start + b * LANES, start + (b + 1) * LANES)
                normed = (pre[b * LANES : (b + 1) * LANES, lane(h)] - mean) * inv
                hidden, back = jax.vjp(jax.nn.gelu, normed * gain + bias)
                normed_ref[band, lane(h)] = normed.astype(BF)
                slope_ref[band, lane(h)] = back(ones)[0].astype(BF)
                hid_ref[band, lane(h)] = hidden.astype(BF)


def shift_kernel(
    order_ref, d_embed_ref, w2_ref, normed_ref, slope_ref, hid_ref, loss_hbm, shift_ref, msg_ref, sum_ref, loss_ref, sems
):
    loss_copy = pltpu.make_async_copy(loss_hbm, loss_ref, sems.at[0])
    loss_copy.start()
    n_blocks, own, _ = d_embed_ref.shape
    sum_ref[...] = jnp.zeros_like(sum_ref)
    gains = biases = second = None
    for k in range(0, n_blocks, 2):
        d_embed = jnp.concatenate([d_embed_ref[order_ref[k + 1]], d_embed_ref[order_ref[k + 2]]], axis=0)
        band = slice(k * own, (k + 2) * own)
        d_shift = tdot(d_embed, w2_ref[...], 1, 1) * slope_ref[band, :].astype(F32)
        shift_ref[band, :] = d_shift
        gain = jnp.sum(d_shift * normed_ref[band, :].astype(F32), axis=0, keepdims=True)
        bias = jnp.sum(d_shift, axis=0, keepdims=True)
        part = tdot(hid_ref[band, :], d_embed, 0, 0)
        gains = gain if gains is None else gains + gain
        biases = bias if biases is None else biases + bias
        second = part if second is None else second + part
    loss_copy.wait()
    hits = jnp.sum(loss_ref[0:8, :], axis=0, keepdims=True)
    logs = jnp.sum(loss_ref[8:16, :], axis=0, keepdims=True)
    sum_ref[0:1, :] = gains
    sum_ref[1:2, :] = biases
    sum_ref[2:3, :] = jnp.concatenate([hits, logs], axis=1)
    n, _, slab = msg_ref.shape
    share = slab // n
    sums = sum_ref[...]
    high = sums.astype(BF)
    rest = sums - high.astype(F32)
    mid = rest.astype(BF)
    low = (rest - mid.astype(F32)).astype(BF)
    row = lax.broadcasted_iota(jnp.int32, sums.shape, 0)
    lower = jnp.where(row < 4, mid.astype(F32), pltpu.roll(low.astype(F32), 4, 0))
    packed = jnp.concatenate([high.astype(F32), lower], axis=0).astype(BF)
    msg_ref[:, :share, :] = jnp.broadcast_to(packed[None], (n, share, slab))
    msg_ref[:, share:, :] = second.astype(BF).reshape(n, share, slab)


def halves(v):
    high = v.astype(BF)
    return high, (v - high.astype(F32)).astype(BF)


def first_kernel(total_rows, order_ref, recv_ref, shift_ref, normed_ref, inv_ref, gain_ref, *rest):
    parts = rest[:-5]
    out_hbm, second_ref, d_pre_ref, out_ref, sems = rest[-5:]
    n, _, _ = out_ref.shape
    slab = d_pre_ref.shape[1]
    share = second_ref.shape[0]
    second_ref[...] = jnp.sum(recv_ref[:, share:, :].astype(F32), axis=0)
    got = jnp.sum(recv_ref[:, :share, :].astype(F32), axis=0)
    got = got[0:8] + (got[8:16] + pltpu.roll(got[8:16], 4, 0))
    chunks = slab // LANES
    for h in range(chunks):
        at = pl.ds(order_ref[0] * chunks + h, 1)
        factor = gain_ref[at, :] * inv_ref[at, :]
        gain_mean = got[0:1, lane(h)] / total_rows
        bias_mean = got[1:2, lane(h)] / total_rows
        for b in range(d_pre_ref.shape[0] // LANES):
            band = slice(b * LANES, (b + 1) * LANES)
            d_pre = factor * (shift_ref[band, lane(h)] - bias_mean - normed_ref[band, lane(h)].astype(F32) * gain_mean)
            d_pre_ref[band, lane(h)] = d_pre.astype(BF)
    high, low = halves(got[0:2])
    sums = [piece[k : k + 1, lane(h)] for k in range(2) for piece in (high, low) for h in range(chunks)]
    high, rest_of = got[2:3].astype(BF), got[2:3] - got[2:3].astype(BF).astype(F32)
    losses = [piece[:, lane(h)] for piece in (high,) + halves(rest_of) for h in range(chunks)]
    losses += [jnp.zeros((1, LANES), BF)] * (8 - len(losses))
    odd = lax.rem(order_ref[10], 2) == 1
    extra = jnp.where(
        odd,
        jnp.concatenate([v.astype(F32) for v in losses], axis=0),
        jnp.concatenate([v.astype(F32) for v in sums], axis=0),
    ).astype(BF)
    out_ref[:, chunks * share :, :] = jnp.broadcast_to(extra[None], (n, 8, LANES))
    group = TILE // share
    copies = []
    for j in range(n // group):
        tile = jnp.concatenate([part[:, j * TILE : (j + 1) * TILE] for part in parts], axis=0)
        grad = tdot(tile, d_pre_ref[...], 0, 0).astype(BF)
        span = slice(j * group, (j + 1) * group)
        for h in range(chunks):
            out_ref[span, h * share : (h + 1) * share, :] = grad[:, lane(h)].reshape(group, share, LANES)
        copies.append(pltpu.make_async_copy(out_ref.at[span], out_hbm.at[span], sems.at[j]))
        copies[-1].start()
    for copy in copies:
        copy.wait()


def tail_kernel(total_rows, recv_ref, out_ref, gain_ref, bias_ref, loss_ref):
    n_batch, n_proto, height, _ = recv_ref.shape
    share = out_ref.shape[0]
    chunks = height // share
    lines = jnp.zeros((8, LANES), F32)
    for p in range(n_proto):
        acc = recv_ref[0, p].astype(F32)
        for b in range(1, n_batch):
            acc += recv_ref[b, p].astype(F32)
        for h in range(chunks):
            at = (p * chunks + h) * LANES
            out_ref[:, at : at + LANES] = acc[h * share : (h + 1) * share, :]
        sums = recv_ref[0, p, chunks * share :, :].astype(F32)
        for h in range(chunks):
            at = p * chunks + h
            gain_ref[at : at + 1, :] = sums[h : h + 1] + sums[chunks + h : chunks + h + 1]
            bias_ref[at : at + 1, :] = sums[2 * chunks + h : 2 * chunks + h + 1] + sums[3 * chunks + h : 3 * chunks + h + 1]
        lines += recv_ref[1, p, chunks * share :, :].astype(F32)
    hits = lines[0:1] + (lines[2:3] + lines[4:5])
    logs = (lines[1:2] + (lines[3:4] + lines[5:6])) / n_proto
    loss = jnp.sum(logs - hits, axis=1, keepdims=True) / total_rows
    loss_ref[...] = jnp.broadcast_to(loss, loss_ref.shape)


def stage_kernel(order_ref, in0_ref, in1_ref, in2_ref, in3_ref, out0_ref, out1_ref, out2_ref, out3_ref, sum_ref):
    near = in0_ref[...].astype(F32) + in1_ref[...].astype(F32)
    sum_ref[...] = (near + (in2_ref[...].astype(F32) + in3_ref[...].astype(F32))).astype(BF)
    outs = (out0_ref, out1_ref, out2_ref, out3_ref)
    for d, out in enumerate(outs):
        height = out.shape[0]
        at = pl.multiple_of(lax.rem(order_ref[10] + d, len(outs)) * height, height)
        out[...] = sum_ref[pl.ds(at, height), :]


def shape(dims, kind=F32):
    return jax.ShapeDtypeStruct(dims, kind)


def step_of_device(features, w_first, bn_gain, bn_bias, w_second, prototypes, pair):
    n_batch = lax.axis_size("batch")
    n_proto = lax.axis_size("proto")
    own, d_in = features.shape
    d_hid, width = w_second.shape
    cols = prototypes.shape[0]
    total_rows = own * n_batch * n_proto
    rows = own * n_proto
    part = lax.axis_index("proto")
    slab = d_hid // n_proto
    col_bands = cols // LANES
    row_bands = rows // LANES
    hid_bands = d_hid // LANES
    steps = rows // TILE
    gain = bn_gain.reshape(hid_bands, LANES)
    bias = bn_bias.reshape(hid_bands, LANES)

    def hop(x, moves):
        return lax.ppermute(x, "proto", moves)

    ring = n_proto // 2
    right = [(i * 2 + c, (i + 1) % ring * 2 + c) for i in range(ring) for c in range(2)]
    left = [(t, s) for s, t in right]
    swap = [(i, i ^ 1) for i in range(n_proto)]
    from_left = hop(features, right)
    from_right = hop(features, left)
    across = lax.shift_right_logical(part, 1)
    place = lax.axis_index("batch")
    side = 4
    order = jnp.stack(
        [part]
        + [
            (lax.bitwise_and(across + d, ring - 1) * 2 + lax.bitwise_and(part, 1)) ^ o
            for o in range(2)
            for d in (0, 1, 3, 2)
        ]
        + [lax.shift_right_logical(place, 2), lax.bitwise_and(place, side - 1)]
    ).astype(jnp.int32)
    mate_row = (pair - place * rows).astype(F32).reshape(row_bands, LANES)

    anywhere = pl.BlockSpec(memory_space=pl.ANY)
    pre, msg = pl.pallas_call(
        pre_kernel,
        in_specs=[pl.BlockSpec(features.shape, lambda: (0, 0)), anywhere],
        out_shape=[shape((own, d_hid)), shape((n_batch, 2 * hid_bands, LANES))],
        scratch_shapes=[
            pltpu.VMEM((2 * hid_bands, LANES), F32),
            pltpu.VMEM((d_hid // TILE, d_in, TILE), BF),
            pltpu.SemaphoreType.DMA((d_hid // TILE,)),
        ],
        name="pre_kernel",
    )(features, w_first)
    near_left, near_right, _ = lax.optimization_barrier((from_left, from_right, pre))
    far_top = hop(near_left[: own // 2], right)
    far_low = hop(near_right[own // 2 :], left)
    got = deal(msg, "batch")
    got, far_top, far_low, mate_row, order = lax.optimization_barrier((got, far_top, far_low, mate_row, order))
    mine = [features, from_right, from_left, far_top, far_low]
    parts = mine + [hop(piece, swap) for piece in mine]
    msg = pl.pallas_call(
        relay_kernel, out_shape=shape((n_proto, 2 * hid_bands, LANES)), compiler_params=PARAMS, name="relay_kernel"
    )(got)
    raw, _ = lax.optimization_barrier((prototypes, msg))
    proto_bf, proto_t, raw_t = pl.pallas_call(
        proto_kernel,
        out_shape=[shape((cols, width), BF), shape((width, cols), BF), shape((width, cols), BF)],
        name="proto_kernel",
    )(raw)
    got, proto_bf, proto_t, raw_t = lax.optimization_barrier((deal(msg, "proto"), proto_bf, proto_t, raw_t))
    unit_embed, embed_scale, mean, inv, msg = pl.pallas_call(
        lambda *refs: embed_kernel(total_rows, *refs),
        in_specs=[anywhere, pl.BlockSpec((n_proto, 2 * hid_bands, LANES), lambda: (0, 0, 0))]
        + [pl.BlockSpec((hid_bands, LANES), lambda: (0, 0))] * 2
        + [anywhere],
        out_shape=[
            shape((own, width)),
            shape((own, LANES)),
            shape((hid_bands, LANES)),
            shape((hid_bands, LANES)),
            shape((n_proto, own, width), BF),
        ],
        scratch_shapes=[
            pltpu.VMEM((own, d_hid), BF),
            pltpu.VMEM((own, d_hid), F32),
            pltpu.VMEM((d_hid, width), BF),
            pltpu.SemaphoreType.DMA((2,)),
        ],
        name="embed_kernel",
    )(pre, got, gain, bias, w_second)
    stat_spec = whole((hid_bands, LANES))
    normed, slope, hid = pl.pallas_call(
        slab_kernel,
        grid_spec=pltpu.PrefetchScalarGridSpec(
            num_scalar_prefetch=1,
            grid=(1,),
            in_specs=[stat_spec] * 4 + [anywhere] * (1 + len(parts)),
            out_specs=[whole((rows, slab))] * 3,
            scratch_shapes=[
                pltpu.VMEM((rows, d_in), BF),
                pltpu.VMEM((d_in, slab), BF),
                pltpu.SemaphoreType.DMA((len(parts) + 1,)),
            ],
        ),
        out_shape=[shape((rows, slab), BF)] * 3,
        name="slab_kernel",
    )(order, mean, inv, gain, bias, w_first, *parts)
    block_embed, normed, slope, hid = lax.optimization_barrier((deal(msg, "proto"), normed, slope, hid))
    block_embed = block_embed.reshape(rows, width)

    kern, col_msg, soft = pl.pallas_call(
        score_kernel,
        grid=(steps,),
        in_specs=[rows_of(TILE, width), anywhere],
        out_specs=[rows_of(TILE, cols), whole((n_batch, col_bands, LANES)), whole((row_bands, LANES))],
        out_shape=[shape((rows, cols), BF), shape((n_batch, col_bands, LANES)), shape((row_bands, LANES))],
        scratch_shapes=[
            pltpu.VMEM((col_bands * 8, LANES), F32),
            pltpu.VMEM((width, cols), BF),
            pltpu.SemaphoreType.DMA((cols // TILE,)),
        ],
        compiler_params=PARAMS,
        name="score_kernel",
    )(block_embed, proto_t)

    def row_pass(recv, extra):
        height = row_bands * (2 if extra else 1)
        return pl.pallas_call(
            row_kernel,
            grid=(steps,),
            in_specs=[whole((n_batch, col_bands, LANES)), rows_of(TILE, cols)]
            + [whole((row_bands, LANES)) for _ in extra],
            out_specs=whole((n_proto, height, LANES)),
            out_shape=shape((n_proto, height, LANES)),
            scratch_shapes=[pltpu.VMEM((col_bands, LANES), F32)],
            compiler_params=PARAMS,
        name="row_kernel",
        )(recv, kern, *extra)

    def col_pass(recv):
        return pl.pallas_call(
            col_kernel,
            grid=(steps,),
            in_specs=[whole(recv.shape), rows_of(TILE, cols)],
            out_specs=whole((n_batch, col_bands, LANES)),
            out_shape=shape((n_batch, col_bands, LANES)),
            scratch_shapes=[pltpu.VMEM((col_bands * 8, LANES), F32), pltpu.VMEM((row_bands, LANES), F32)],
            compiler_params=PARAMS,
        name="col_kernel",
        )(recv, kern)

    recv_soft = None
    for step in range(ITERS):
        recv_col = deal(col_msg, "batch")
        recv_row = deal(row_pass(recv_col, () if step else (soft,)), "proto")
        recv_soft = recv_row if recv_soft is None else recv_soft
        if step + 1 < ITERS:
            col_msg = col_pass(recv_row)

    d_unit, *pieces, loss_tile = pl.pallas_call(
        final_kernel,
        grid=(steps,),
        in_specs=[
            pl.BlockSpec(memory_space=pltpu.SMEM),
            anywhere,
            whole((row_bands, LANES)),
            anywhere,
            anywhere,
            anywhere,
            whole(recv_col.shape),
            whole(recv_row.shape),
            whole(recv_soft.shape),
        ],
        out_specs=[rows_of(TILE, width)] + [whole((width // side, cols))] * side + [whole((16, LANES))],
        out_shape=[shape((rows, width), BF)] + [shape((width // side, cols), BF)] * side + [shape((16, LANES))],
        scratch_shapes=[
            pltpu.VMEM((rows, cols), BF),
            pltpu.VMEM((TILE, rows), BF),
            pltpu.VMEM((16, LANES), F32),
            pltpu.VMEM((col_bands, LANES), F32),
            pltpu.VMEM((row_bands, LANES), F32),
            pltpu.VMEM((row_bands, LANES), F32),
            pltpu.VMEM((rows, width), BF),
            pltpu.VMEM((width, cols), BF),
            pltpu.VMEM((cols, width), BF),
            pltpu.VMEM((width, cols), BF),
            pltpu.VMEM((width, cols), BF),
            pltpu.VMEM((2 * TILE, width), BF),
            pltpu.SemaphoreType.DMA((4,)),
        ],
        name="final_kernel",
    )(order, block_embed, mate_row, proto_t, proto_bf, raw_t, recv_col, recv_row, recv_soft)


    def shifted(axis, d):
        moves = []
        for b in range(n_batch):
            y, z = divmod(b, side)
            moves.append((b, (y + d) % side * side + z if axis == 0 else y * side + (z + d) % side))
        return moves

    pieces = [pieces[0]] + [lax.ppermute(pieces[d], "batch", shifted(0, d)) for d in range(1, side)]
    d_unit = deal(d_unit.reshape(n_proto, own, width), "proto")
    d_embed = pl.pallas_call(
        d_embed_kernel, out_shape=shape((n_proto, own, width), BF), compiler_params=PARAMS, name="d_embed_kernel"
    )(d_unit, unit_embed, embed_scale)
    d_embed = deal(d_embed, "proto")

    shift, msg = pl.pallas_call(
        shift_kernel,
        grid_spec=pltpu.PrefetchScalarGridSpec(
            num_scalar_prefetch=1,
            grid=(1,),
            in_specs=[
                whole((n_proto, own, width)),
                pl.BlockSpec((slab, width), lambda i, s: (s[0], 0)),
                whole((rows, slab)),
                whole((rows, slab)),
                whole((rows, slab)),
                pl.BlockSpec(memory_space=pltpu.HBM),
            ],
            out_specs=[whole((rows, slab)), whole((n_batch, 2 * slab // n_batch, width))],
            scratch_shapes=[pltpu.VMEM((8, slab), F32), pltpu.VMEM((16, LANES), F32), pltpu.SemaphoreType.DMA((1,))],
        ),
        out_shape=[shape((rows, slab)), shape((n_batch, 2 * slab // n_batch, width), BF)],
        compiler_params=PARAMS,
        name="shift_kernel",
    )(order, d_embed, w_second, normed, slope, hid, loss_tile)
    recv = deal(msg, "batch")

    share = d_in // (n_batch * n_proto)
    lines = slab // LANES * share + 8
    first, second = pl.pallas_call(
        lambda *refs: first_kernel(total_rows, *refs),
        grid_spec=pltpu.PrefetchScalarGridSpec(
            num_scalar_prefetch=1,
            grid=(1,),
            in_specs=[whole(recv.shape), whole((rows, slab)), whole((rows, slab)), stat_spec, stat_spec]
            + [whole(piece.shape) for piece in parts],
            out_specs=[pl.BlockSpec(memory_space=pltpu.HBM), whole((slab // n_batch, width))],
            scratch_shapes=[
                pltpu.VMEM((rows, slab), BF),
                pltpu.VMEM((n_batch * n_proto, lines, LANES), BF),
                pltpu.SemaphoreType.DMA((d_in // TILE,)),
            ],
        ),
        out_shape=[shape((n_batch * n_proto, lines, LANES), BF), shape((slab // n_batch, width))],
        compiler_params=PARAMS,
        name="first_kernel",
    )(order, recv, shift, normed, inv, gain, *parts)

    first, *pieces = lax.optimization_barrier((first, *pieces))
    pieces = pl.pallas_call(
        stage_kernel,
        in_specs=[pl.BlockSpec(memory_space=pltpu.SMEM)] + [pl.BlockSpec((width // side, cols), lambda: (0, 0))] * side,
        out_shape=[shape((width // n_batch, cols), BF)] * side,
        scratch_shapes=[pltpu.VMEM((width // side, cols), BF)],
        name="stage_kernel",
    )(order, *pieces)
    pieces = [pieces[0]] + [lax.ppermute(pieces[d], "batch", shifted(1, d)) for d in range(1, side)]
    grad_proto = sum(piece.astype(F32) for piece in pieces).T
    first = deal(first, ("batch", "proto")).reshape(n_batch, n_proto, lines, LANES)
    grad_first, grad_gain, grad_bias, loss = pl.pallas_call(
        lambda *refs: tail_kernel(total_rows, *refs),
        out_shape=[shape((share, d_hid)), shape((hid_bands, LANES)), shape((hid_bands, LANES)), shape((1, LANES))],
        compiler_params=PARAMS,
        name="tail_kernel",
    )(first)
    grad_second = lax.ppermute(
        second,
        ("batch", "proto"),
        [(b * n_proto + p, p * n_batch + b) for b in range(n_batch) for p in range(n_proto)],
    )
    grad_gain = grad_gain.reshape(-1)
    grad_bias = grad_bias.reshape(-1)
    loss = loss[0, 0]
    return (grad_first, grad_second, grad_gain, grad_bias, grad_proto, loss)


def solution(mesh):
    return jax.shard_map(
        step_of_device,
        mesh=mesh,
        in_specs=(P(("batch", "proto"), None), P(), P(), P(), P(), P("proto", None), P("batch")),
        out_specs=(
            P(("batch", "proto"), None),
            P(("batch", "proto"), None),
            P(),
            P(),
            P("proto", "batch"),
            P(),
        ),
        check_vma=False,
    )
```

```python
import jax
import jax.numpy as jnp
from jax import lax
from jax.experimental import pallas as pl
from jax.experimental.pallas import tpu as pltpu
from jax.sharding import PartitionSpec as P


ITERS = 3
BF = jnp.bfloat16
F32 = jnp.float32
LANES = 128
TILE = 256
LOG2_E = 1.4426950408889634
PARAMS = pltpu.CompilerParams(vmem_limit_bytes=24 * 1024 * 1024)


def deal(x, axis):
    return lax.all_to_all(x, axis, 0, 0, tiled=True)


def tdot(a, b, a_dim, b_dim):
    return lax.dot_general(a, b, (((a_dim,), (b_dim,)), ((), ())), preferred_element_type=F32)


def fold_rows(v):
    return jnp.sum(v.reshape(v.shape[0] // 8, 8, LANES), axis=0)


def as_column(row):
    return jnp.broadcast_to(row, (LANES, LANES)).T


def lane(j):
    return slice(j * LANES, (j + 1) * LANES)


def whole(shape):
    return pl.BlockSpec(shape, lambda i, *_: (0,) * len(shape))


def rows_of(rows, width):
    return pl.BlockSpec((rows, width), lambda i, *_: (i, 0))


def pre_kernel(features_ref, w_hbm, pre_ref, msg_ref, stat_ref, w_buf, sems):
    pieces = w_buf.shape[0]
    copies = [
        pltpu.make_async_copy(w_hbm.at[:, k * TILE : (k + 1) * TILE], w_buf.at[k], sems.at[k]) for k in range(pieces)
    ]
    for copy in copies:
        copy.start()
    chunks = TILE // LANES
    half = stat_ref.shape[0] // 2
    for k in range(pieces):
        copies[k].wait()
        pre = jnp.dot(features_ref[...], w_buf[k], preferred_element_type=F32)
        pre_ref[:, k * TILE : (k + 1) * TILE] = pre
        for h in range(chunks):
            at = k * chunks + h
            part = pre[:, lane(h)]
            stat_ref[at : at + 1, :] = jnp.sum(part, axis=0, keepdims=True)
            stat_ref[half + at : half + at + 1, :] = jnp.sum(part * part, axis=0, keepdims=True)
    msg_ref[...] = jnp.broadcast_to(stat_ref[...][None], msg_ref.shape)


def relay_kernel(recv_ref, msg_ref):
    msg_ref[...] = jnp.broadcast_to(jnp.sum(recv_ref[...], axis=0, keepdims=True), msg_ref.shape)


def embed_kernel(
    total_rows, pre_ref, recv_ref, gain_ref, bias_ref, w2_ref, unit_hbm, scale_hbm, mean_hbm, inv_hbm, msg_hbm,
    hid_ref, unit_ref, scale_ref, mean_ref, inv_ref, bf_ref, sems,
):
    stats = jnp.sum(recv_ref[...], axis=0)
    half = stats.shape[0] // 2
    mean = stats[:half] / total_rows
    inv = lax.rsqrt(stats[half:] / total_rows - mean * mean + 1e-05)
    mean_ref[...] = mean
    inv_ref[...] = inv
    for j in range(half):
        normed = (pre_ref[:, lane(j)] - mean[j : j + 1]) * inv[j : j + 1]
        hid_ref[:, lane(j)] = jax.nn.gelu(normed * gain_ref[j : j + 1, :] + bias_ref[j : j + 1, :]).astype(BF)
    embed = jnp.dot(hid_ref[...], w2_ref[...], preferred_element_type=F32)
    scale = lax.rsqrt(jnp.sum(embed * embed, axis=1, keepdims=True) + 1e-06)
    unit = embed * scale
    bf_ref[...] = unit.astype(BF)
    unit_ref[...] = unit
    scale_ref[...] = jnp.broadcast_to(scale, scale_ref.shape)
    moves = [(bf_ref, msg_hbm.at[k]) for k in range(msg_hbm.shape[0])]
    moves += [(unit_ref, unit_hbm), (scale_ref, scale_hbm), (mean_ref, mean_hbm), (inv_ref, inv_hbm)]
    copies = [pltpu.make_async_copy(src, dst, sems.at[k]) for k, (src, dst) in enumerate(moves)]
    for copy in copies:
        copy.start()
    for copy in copies:
        copy.wait()


def proto_kernel(raw_ref, proto_ref, proto_t_ref, raw_t_ref, norm_ref):
    for k in range(raw_ref.shape[0] // TILE):
        span = slice(k * TILE, (k + 1) * TILE)
        raw_t = raw_ref[span, :].T
        raw_t_ref[:, span] = raw_t
        wide = raw_t.astype(F32)
        scale = lax.rsqrt(jnp.sum(wide * wide, axis=0, keepdims=True) + 1e-06)
        norm_ref[:, span] = jnp.broadcast_to(scale, (8, TILE))
        unit = (wide * scale).astype(BF)
        proto_t_ref[:, span] = unit
        proto_ref[span, :] = unit.T


def score_kernel(embed_ref, proto_t_hbm, kern_ref, msg_ref, soft_ref, acc_ref, proto_t_ref, sems):
    step = pl.program_id(0)
    rows = embed_ref.shape[0]
    cols = proto_t_ref.shape[1]

    def copy(j):
        span = slice(j * TILE, (j + 1) * TILE)
        return pltpu.make_async_copy(proto_t_hbm.at[:, span], proto_t_ref.at[:, span], sems.at[j])

    @pl.when(step == 0)
    def _():
        for j in range(cols // TILE):
            copy(j).start()
        acc_ref[...] = jnp.zeros_like(acc_ref)
        for j in range(cols // TILE):
            copy(j).wait()

    soft = [None] * (rows // LANES)
    for j in range(cols // TILE):
        span = slice(j * TILE, (j + 1) * TILE)
        scores = jnp.dot(embed_ref[...], proto_t_ref[:, span], preferred_element_type=F32)
        tempered = jnp.exp2(scores * (10.0 * LOG2_E))
        kern = tempered * tempered
        kern_ref[:, span] = kern.astype(BF)
        for h in range(TILE // LANES):
            at = (j * (TILE // LANES) + h) * 8
            acc_ref[at : at + 8, :] += fold_rows(kern[:, lane(h)])
        for b in range(rows // LANES):
            part = tempered[b * LANES : (b + 1) * LANES]
            part = part[:, :LANES] + part[:, LANES:]
            soft[b] = part if soft[b] is None else soft[b] + part
    for b in range(rows // LANES):
        soft_ref[pl.ds(step * (rows // LANES) + b, 1), :] = jnp.sum(soft[b].T, axis=0, keepdims=True)

    @pl.when(step == pl.num_programs(0) - 1)
    def _():
        total = jnp.sum(acc_ref[...].reshape(cols // LANES, 8, LANES), axis=1)
        msg_ref[...] = jnp.broadcast_to(total[None], msg_ref.shape)


def row_kernel(recv_ref, kern_ref, *rest):
    soft_ref = rest[0] if len(rest) == 3 else None
    msg_ref, scale_ref = rest[-2:]
    step = pl.program_id(0)
    rows = kern_ref.shape[0]
    copies = msg_ref.shape[0]

    @pl.when(step == 0)
    def _():
        scale_ref[...] = 1.0 / jnp.sum(recv_ref[...], axis=0)
        if soft_ref is not None:
            half = soft_ref.shape[0]
            msg_ref[:, half:, :] = jnp.broadcast_to(soft_ref[...][None], (copies, half, LANES))

    for b in range(rows // LANES):
        acc = None
        for j in range(scale_ref.shape[0]):
            part = kern_ref[b * LANES : (b + 1) * LANES, lane(j)].astype(F32) * scale_ref[j : j + 1, :]
            acc = part if acc is None else acc + part
        row = jnp.sum(acc.T, axis=0, keepdims=True)
        msg_ref[:, pl.ds(step * (rows // LANES) + b, 1), :] = jnp.broadcast_to(row[None], (copies, 1, LANES))


def col_kernel(recv_ref, kern_ref, msg_ref, acc_ref, scale_ref):
    step = pl.program_id(0)
    rows, cols = kern_ref.shape

    @pl.when(step == 0)
    def _():
        acc_ref[...] = jnp.zeros_like(acc_ref)
        scale_ref[...] = 1.0 / jnp.sum(recv_ref[:, : scale_ref.shape[0], :], axis=0)

    for b in range(rows // LANES):
        scale = as_column(scale_ref[pl.ds(step * (rows // LANES) + b, 1), :])
        for j in range(cols // LANES):
            part = kern_ref[b * LANES : (b + 1) * LANES, lane(j)].astype(F32) * scale
            acc_ref[j * 8 : (j + 1) * 8, :] += fold_rows(part)

    @pl.when(step == pl.num_programs(0) - 1)
    def _():
        total = jnp.sum(acc_ref[...].reshape(cols // LANES, 8, LANES), axis=1)
        msg_ref[...] = jnp.broadcast_to(total[None], msg_ref.shape)


def final_kernel(
    order_ref, embed_ref, pair_ref, proto_t_ref, proto_ref, raw_t_ref, norm_ref, recv_col_ref, recv_row_ref, recv_soft_ref,
    d_unit_ref, piece0_ref, piece1_ref, piece2_ref, piece3_ref, loss_ref,
    grad_ref, mate_ref, loss_acc_ref, col_ref, row_ref, soft_ref, term_ref, both_ref,
):
    step = pl.program_id(0)
    rows = d_unit_ref.shape[0]
    cols = proto_t_ref.shape[1]
    bands = row_ref.shape[0]
    chunks = TILE // LANES

    @pl.when(step == 0)
    def _():
        loss_acc_ref[...] = jnp.zeros_like(loss_acc_ref)
        col_ref[...] = 10.0 / jnp.sum(recv_col_ref[...], axis=0)
        row_ref[...] = 1.0 / jnp.sum(recv_row_ref[:, :bands, :], axis=0)
        soft_ref[...] = jnp.sum(recv_soft_ref[:, bands:, :], axis=0)
        loss_acc_ref[8:16, :] = jnp.log(soft_ref[...])

    base = step * (rows // LANES)
    here = pl.ds(pl.multiple_of(step * rows, rows), rows)
    spot = lax.broadcasted_iota(jnp.int32, (LANES, LANES), 1)
    scales = []
    for b in range(rows // LANES):
        pair = as_column(pair_ref[pl.ds(base + b, 1), :]).astype(jnp.int32)
        found = jnp.zeros((LANES, LANES), F32)
        for q in range(bands):
            hot = spot + q * LANES == pair
            found += jnp.where(hot, row_ref[q : q + 1, :], 0.0)
            mate_ref[b * LANES : (b + 1) * LANES, lane(q)] = jnp.where(hot, 1.0, 0.0).astype(BF)
        scales.append(jnp.broadcast_to(jnp.sum(found, axis=1, keepdims=True), (LANES, LANES)))
    mate_scale = jnp.concatenate(scales, axis=0)
    both_ref[0:rows, :] = embed_ref[here, :]
    both_ref[rows:, :] = jnp.dot(mate_ref[...], embed_ref[...], preferred_element_type=F32).astype(BF)
    soft = jnp.concatenate([as_column(soft_ref[pl.ds(base + b, 1), :]) for b in range(rows // LANES)], axis=0)
    inv_soft = 10.0 / soft
    loss_acc = jnp.zeros((8, LANES), F32)
    for j in range(cols // TILE):
        span = slice(j * TILE, (j + 1) * TILE)
        both = jnp.dot(both_ref[...], proto_t_ref[:, span], preferred_element_type=F32)
        scores, mates = both[:rows], both[rows:]
        for h in range(chunks):
            at = j * chunks + h
            target = jnp.exp2(mates[:, lane(h)] * (20.0 * LOG2_E)) * mate_scale * col_ref[at : at + 1, :]
            score = scores[:, lane(h)]
            loss_acc += fold_rows(target * score)
            grad_ref[here, lane(at)] = (jnp.exp2(score * (10.0 * LOG2_E)) * inv_soft - target).astype(BF)
    d_unit_ref[...] = jnp.dot(grad_ref[here, :], proto_ref[...], preferred_element_type=F32).astype(BF)
    loss_acc_ref[0:8, :] += loss_acc

    @pl.when(step == pl.num_programs(0) - 1)
    def _():
        embed_t = embed_ref[...].T
        for j in range(cols // TILE):
            span = slice(j * TILE, (j + 1) * TILE)
            raw = raw_t_ref[:, span].astype(F32)
            scale = norm_ref[0:1, span]
            acc = jnp.dot(embed_t, grad_ref[:, span], preferred_element_type=F32)
            along = scale * scale * jnp.sum(raw * acc, axis=0, keepdims=True)
            term_ref[:, span] = ((acc - raw * along) * scale).astype(BF)
        pieces = (piece0_ref, piece1_ref, piece2_ref, piece3_ref)
        for d, piece in enumerate(pieces):
            height = piece.shape[0]
            at = pl.multiple_of(lax.rem(order_ref[9] + d, len(pieces)) * height, height)
            piece[...] = term_ref[pl.ds(at, height), :]
        loss_ref[...] = loss_acc_ref[...]


def d_embed_kernel(recv_ref, unit_ref, scale_ref, msg_ref):
    d_unit = jnp.sum(recv_ref[...].astype(F32), axis=0)
    unit = unit_ref[...]
    d_embed = (d_unit - unit * jnp.sum(unit * d_unit, axis=1, keepdims=True)) * scale_ref[:, :1]
    msg_ref[...] = jnp.broadcast_to(d_embed.astype(BF)[None], msg_ref.shape)


def start_parts(parts, buf_ref, sems):
    copies = []
    at = 0
    for k, part in enumerate(parts):
        height = part.shape[0]
        copies.append(pltpu.make_async_copy(part, buf_ref.at[at : at + height], sems.at[k]))
        at += height
    for copy in copies:
        copy.start()
    return copies


def slab_kernel(order_ref, mean_ref, inv_ref, gain_ref, bias_ref, w_hbm, *rest):
    parts = rest[:-9]
    outs, bufs = rest[-9:-6], rest[-6:-3]
    buf_ref, w_ref, sems = rest[-3:]
    normed_ref, slope_ref, hid_ref = bufs
    rows, slab = normed_ref.shape
    at = pl.ds(pl.multiple_of(order_ref[0] * slab, slab), slab)
    w_copy = pltpu.make_async_copy(w_hbm.at[:, at], w_ref, sems.at[len(parts)])
    w_copy.start()
    copies = start_parts(parts, buf_ref, sems)
    stops = [sum(part.shape[0] for part in parts[: k + 1]) for k in range(len(parts))]
    w_copy.wait()
    chunks = slab // LANES
    ones = jnp.ones((LANES, LANES), F32)
    done = 0
    sends = []
    for g in range(rows // TILE):
        start = g * TILE
        while done < len(parts) and (stops[done - 1] if done else 0) < start + TILE:
            copies[done].wait()
            done += 1
        pre = jnp.dot(buf_ref[start : start + TILE, :], w_ref[...], preferred_element_type=F32)
        for h in range(chunks):
            at = pl.ds(order_ref[0] * chunks + h, 1)
            mean, inv, gain, bias = mean_ref[at, :], inv_ref[at, :], gain_ref[at, :], bias_ref[at, :]
            for b in range(TILE // LANES):
                band = slice(start + b * LANES, start + (b + 1) * LANES)
                normed = (pre[b * LANES : (b + 1) * LANES, lane(h)] - mean) * inv
                hidden, back = jax.vjp(jax.nn.gelu, normed * gain + bias)
                normed_ref[band, lane(h)] = normed.astype(BF)
                slope_ref[band, lane(h)] = back(ones)[0].astype(BF)
                hid_ref[band, lane(h)] = hidden.astype(BF)
        span = slice(start, start + TILE)
        for k, (buf, out) in enumerate(zip(bufs, outs)):
            sends.append(
                pltpu.make_async_copy(buf.at[span], out.at[span], sems.at[len(parts) + 1 + g * len(outs) + k])
            )
            sends[-1].start()
    for send in sends:
        send.wait()


def shift_kernel(
    order_ref, d_embed_ref, w2_ref, normed_hbm, slope_hbm, hid_hbm, loss_hbm, shift_ref, msg_ref, sum_ref, loss_ref,
    normed_ref, slope_ref, hid_ref, sems,
):
    moves = ((slope_hbm, slope_ref), (normed_hbm, normed_ref), (hid_hbm, hid_ref), (loss_hbm, loss_ref))
    copies = [pltpu.make_async_copy(src, dst, sems.at[k]) for k, (src, dst) in enumerate(moves)]
    for copy in copies:
        copy.start()
    n_blocks, own, _ = d_embed_ref.shape
    sum_ref[...] = jnp.zeros_like(sum_ref)
    gains = biases = second = None
    for copy in copies:
        copy.wait()
    for k in range(0, n_blocks, 2):
        d_embed = jnp.concatenate([d_embed_ref[order_ref[k + 1]], d_embed_ref[order_ref[k + 2]]], axis=0)
        band = slice(k * own, (k + 2) * own)
        d_shift = tdot(d_embed, w2_ref[...], 1, 1) * slope_ref[band, :].astype(F32)
        shift_ref[band, :] = d_shift
        gain = jnp.sum(d_shift * normed_ref[band, :].astype(F32), axis=0, keepdims=True)
        bias = jnp.sum(d_shift, axis=0, keepdims=True)
        part = tdot(hid_ref[band, :], d_embed, 0, 0)
        gains = gain if gains is None else gains + gain
        biases = bias if biases is None else biases + bias
        second = part if second is None else second + part
    hits = jnp.sum(loss_ref[0:8, :], axis=0, keepdims=True)
    logs = jnp.sum(loss_ref[8:16, :], axis=0, keepdims=True)
    sum_ref[0:1, :] = gains
    sum_ref[1:2, :] = biases
    sum_ref[2:3, :] = jnp.concatenate([hits, logs], axis=1)
    n, _, slab = msg_ref.shape
    share = slab // n
    sums = sum_ref[...]
    high = sums.astype(BF)
    rest = sums - high.astype(F32)
    mid = rest.astype(BF)
    low = (rest - mid.astype(F32)).astype(BF)
    row = lax.broadcasted_iota(jnp.int32, sums.shape, 0)
    lower = jnp.where(row < 4, mid.astype(F32), pltpu.roll(low.astype(F32), 4, 0))
    packed = jnp.concatenate([high.astype(F32), lower], axis=0).astype(BF)
    msg_ref[:, :share, :] = jnp.broadcast_to(packed[None], (n, share, slab))
    msg_ref[:, share:, :] = second.astype(BF).reshape(n, share, slab)


def halves(v):
    high = v.astype(BF)
    return high, (v - high.astype(F32)).astype(BF)


def first_kernel(total_rows, order_ref, recv_ref, shift_ref, normed_ref, inv_ref, gain_ref, *rest):
    parts = rest[:-5]
    out_hbm, second_ref, d_pre_ref, out_ref, sems = rest[-5:]
    n, _, _ = out_ref.shape
    slab = d_pre_ref.shape[1]
    share = second_ref.shape[0]
    second_ref[...] = jnp.sum(recv_ref[:, share:, :].astype(F32), axis=0)
    got = jnp.sum(recv_ref[:, :share, :].astype(F32), axis=0)
    got = got[0:8] + (got[8:16] + pltpu.roll(got[8:16], 4, 0))
    chunks = slab // LANES
    for h in range(chunks):
        at = pl.ds(order_ref[0] * chunks + h, 1)
        factor = gain_ref[at, :] * inv_ref[at, :]
        gain_mean = got[0:1, lane(h)] / total_rows
        bias_mean = got[1:2, lane(h)] / total_rows
        for b in range(d_pre_ref.shape[0] // LANES):
            band = slice(b * LANES, (b + 1) * LANES)
            d_pre = factor * (shift_ref[band, lane(h)] - bias_mean - normed_ref[band, lane(h)].astype(F32) * gain_mean)
            d_pre_ref[band, lane(h)] = d_pre.astype(BF)
    high, low = halves(got[0:2])
    sums = [piece[k : k + 1, lane(h)] for k in range(2) for piece in (high, low) for h in range(chunks)]
    high, rest_of = got[2:3].astype(BF), got[2:3] - got[2:3].astype(BF).astype(F32)
    losses = [piece[:, lane(h)] for piece in (high,) + halves(rest_of) for h in range(chunks)]
    losses += [jnp.zeros((1, LANES), BF)] * (8 - len(losses))
    odd = lax.rem(order_ref[10], 2) == 1
    extra = jnp.where(
        odd,
        jnp.concatenate([v.astype(F32) for v in losses], axis=0),
        jnp.concatenate([v.astype(F32) for v in sums], axis=0),
    ).astype(BF)
    out_ref[:, chunks * share :, :] = jnp.broadcast_to(extra[None], (n, 8, LANES))
    group = TILE // share
    copies = []
    for j in range(n // group):
        tile = jnp.concatenate([part[:, j * TILE : (j + 1) * TILE] for part in parts], axis=0)
        grad = tdot(tile, d_pre_ref[...], 0, 0).astype(BF)
        span = slice(j * group, (j + 1) * group)
        for h in range(chunks):
            out_ref[span, h * share : (h + 1) * share, :] = grad[:, lane(h)].reshape(group, share, LANES)
        copies.append(pltpu.make_async_copy(out_ref.at[span], out_hbm.at[span], sems.at[j]))
        copies[-1].start()
    for copy in copies:
        copy.wait()


def tail_kernel(total_rows, recv_ref, out_ref, gain_ref, bias_ref, loss_ref):
    n_batch, n_proto, height, _ = recv_ref.shape
    share = out_ref.shape[0]
    chunks = height // share
    lines = jnp.zeros((8, LANES), F32)
    for p in range(n_proto):
        acc = recv_ref[0, p].astype(F32)
        for b in range(1, n_batch):
            acc += recv_ref[b, p].astype(F32)
        for h in range(chunks):
            at = (p * chunks + h) * LANES
            out_ref[:, at : at + LANES] = acc[h * share : (h + 1) * share, :]
        sums = recv_ref[0, p, chunks * share :, :].astype(F32)
        for h in range(chunks):
            at = p * chunks + h
            gain_ref[at : at + 1, :] = sums[h : h + 1] + sums[chunks + h : chunks + h + 1]
            bias_ref[at : at + 1, :] = sums[2 * chunks + h : 2 * chunks + h + 1] + sums[3 * chunks + h : 3 * chunks + h + 1]
        lines += recv_ref[1, p, chunks * share :, :].astype(F32)
    hits = lines[0:1] + (lines[2:3] + lines[4:5])
    logs = (lines[1:2] + (lines[3:4] + lines[5:6])) / n_proto
    loss = jnp.sum(logs - hits, axis=1, keepdims=True) / total_rows
    loss_ref[...] = jnp.broadcast_to(loss, loss_ref.shape)


def stage_kernel(order_ref, in0_ref, in1_ref, in2_ref, in3_ref, out0_ref, out1_ref, out2_ref, out3_ref, sum_ref):
    near = in0_ref[...].astype(F32) + in1_ref[...].astype(F32)
    sum_ref[...] = (near + (in2_ref[...].astype(F32) + in3_ref[...].astype(F32))).astype(BF)
    outs = (out0_ref, out1_ref, out2_ref, out3_ref)
    for d, out in enumerate(outs):
        height = out.shape[0]
        at = pl.multiple_of(lax.rem(order_ref[10] + d, len(outs)) * height, height)
        out[...] = sum_ref[pl.ds(at, height), :]


def shape(dims, kind=F32):
    return jax.ShapeDtypeStruct(dims, kind)


def far_shape(dims, kind=F32):
    return pltpu.HBM(dims, kind)


def far(x):
    return pltpu.with_memory_space_constraint(x, pltpu.HBM)


def step_of_device(features, w_first, bn_gain, bn_bias, w_second, prototypes, pair):
    n_batch = lax.axis_size("batch")
    n_proto = lax.axis_size("proto")
    own, d_in = features.shape
    d_hid, width = w_second.shape
    cols = prototypes.shape[0]
    total_rows = own * n_batch * n_proto
    rows = own * n_proto
    part = lax.axis_index("proto")
    slab = d_hid // n_proto
    col_bands = cols // LANES
    row_bands = rows // LANES
    hid_bands = d_hid // LANES
    steps = rows // TILE
    gain = bn_gain.reshape(hid_bands, LANES)
    bias = bn_bias.reshape(hid_bands, LANES)

    def hop(x, moves):
        return lax.ppermute(x, "proto", moves)

    ring = n_proto // 2
    right = [(i * 2 + c, (i + 1) % ring * 2 + c) for i in range(ring) for c in range(2)]
    left = [(t, s) for s, t in right]
    swap = [(i, i ^ 1) for i in range(n_proto)]
    from_left = hop(features, right)
    from_right = hop(features, left)
    across = lax.shift_right_logical(part, 1)
    place = lax.axis_index("batch")
    side = 4
    order = jnp.stack(
        [part]
        + [
            (lax.bitwise_and(across + d, ring - 1) * 2 + lax.bitwise_and(part, 1)) ^ o
            for o in range(2)
            for d in (0, 1, 3, 2)
        ]
        + [lax.shift_right_logical(place, 2), lax.bitwise_and(place, side - 1)]
    ).astype(jnp.int32)
    mate_row = (pair - place * rows).astype(F32).reshape(row_bands, LANES)

    anywhere = pl.BlockSpec(memory_space=pl.ANY)
    pre, msg = pl.pallas_call(
        pre_kernel,
        in_specs=[pl.BlockSpec(features.shape, lambda: (0, 0)), anywhere],
        out_shape=[shape((own, d_hid)), shape((n_batch, 2 * hid_bands, LANES))],
        scratch_shapes=[
            pltpu.VMEM((2 * hid_bands, LANES), F32),
            pltpu.VMEM((d_hid // TILE, d_in, TILE), BF),
            pltpu.SemaphoreType.DMA((d_hid // TILE,)),
        ],
        name="pre_kernel",
    )(features, w_first)
    near_left, near_right, _ = lax.optimization_barrier((from_left, from_right, pre))
    far_top = hop(near_left[: own // 2], right)
    far_low = hop(near_right[own // 2 :], left)
    got = deal(msg, "batch")
    got, mate_row, order = lax.optimization_barrier((got, mate_row, order))
    msg = pl.pallas_call(
        relay_kernel, out_shape=shape((n_proto, 2 * hid_bands, LANES)), compiler_params=PARAMS, name="relay_kernel"
    )(got)
    got = deal(msg, "proto")
    unit_embed, embed_scale, mean, inv, msg = pl.pallas_call(
        lambda *refs: embed_kernel(total_rows, *refs),
        out_specs=[pl.BlockSpec(memory_space=pltpu.HBM)] * 5,
        out_shape=[
            far_shape((own, width)),
            far_shape((own, LANES)),
            far_shape((hid_bands, LANES)),
            far_shape((hid_bands, LANES)),
            far_shape((n_proto, own, width), BF),
        ],
        scratch_shapes=[
            pltpu.VMEM((own, d_hid), BF),
            pltpu.VMEM((own, width), F32),
            pltpu.VMEM((own, LANES), F32),
            pltpu.VMEM((hid_bands, LANES), F32),
            pltpu.VMEM((hid_bands, LANES), F32),
            pltpu.VMEM((own, width), BF),
            pltpu.SemaphoreType.DMA((n_proto + 4,)),
        ],
        compiler_params=PARAMS,
        name="embed_kernel",
    )(pre, got, gain, bias, w_second)
    raw, *mine, _ = lax.optimization_barrier((prototypes, features, from_right, from_left, far_top, far_low, msg))
    parts = mine + [hop(piece, swap) for piece in mine]
    proto_bf, proto_t, raw_t, norm = pl.pallas_call(
        proto_kernel,
        out_shape=[shape((cols, width), BF), shape((width, cols), BF), shape((width, cols), BF), shape((8, cols))],
        name="proto_kernel",
    )(raw)
    block_embed, proto_bf, proto_t, raw_t, norm, *parts = lax.optimization_barrier(
        (deal(msg, "proto"), proto_bf, proto_t, raw_t, norm, *parts)
    )
    block_embed = block_embed.reshape(rows, width)

    kern, col_msg, soft = pl.pallas_call(
        score_kernel,
        grid=(steps,),
        in_specs=[rows_of(TILE, width), anywhere],
        out_specs=[rows_of(TILE, cols), whole((n_batch, col_bands, LANES)), whole((row_bands, LANES))],
        out_shape=[shape((rows, cols), BF), shape((n_batch, col_bands, LANES)), shape((row_bands, LANES))],
        scratch_shapes=[
            pltpu.VMEM((col_bands * 8, LANES), F32),
            pltpu.VMEM((width, cols), BF),
            pltpu.SemaphoreType.DMA((cols // TILE,)),
        ],
        compiler_params=PARAMS,
        name="score_kernel",
    )(block_embed, far(proto_t))

    def row_pass(recv, extra):
        height = row_bands * (2 if extra else 1)
        return pl.pallas_call(
            row_kernel,
            grid=(steps,),
            in_specs=[whole((n_batch, col_bands, LANES)), rows_of(TILE, cols)]
            + [whole((row_bands, LANES)) for _ in extra],
            out_specs=whole((n_proto, height, LANES)),
            out_shape=shape((n_proto, height, LANES)),
            scratch_shapes=[pltpu.VMEM((col_bands, LANES), F32)],
            compiler_params=PARAMS,
        name="row_kernel",
        )(recv, kern, *extra)

    def col_pass(recv):
        return pl.pallas_call(
            col_kernel,
            grid=(steps,),
            in_specs=[whole(recv.shape), rows_of(TILE, cols)],
            out_specs=whole((n_batch, col_bands, LANES)),
            out_shape=shape((n_batch, col_bands, LANES)),
            scratch_shapes=[pltpu.VMEM((col_bands * 8, LANES), F32), pltpu.VMEM((row_bands, LANES), F32)],
            compiler_params=PARAMS,
        name="col_kernel",
        )(recv, kern)

    recv_soft = None
    for step in range(ITERS):
        recv_col = deal(col_msg, "batch")
        recv_row = deal(row_pass(recv_col, () if step else (soft,)), "proto")
        recv_soft = recv_row if recv_soft is None else recv_soft
        if step + 1 < ITERS:
            col_msg = col_pass(recv_row)

    d_unit, *pieces, loss_tile = pl.pallas_call(
        final_kernel,
        grid=(steps,),
        in_specs=[
            pl.BlockSpec(memory_space=pltpu.SMEM),
            whole((rows, width)),
            whole((row_bands, LANES)),
            whole((width, cols)),
            whole((cols, width)),
            whole((width, cols)),
            whole((8, cols)),
            whole(recv_col.shape),
            whole(recv_row.shape),
            whole(recv_soft.shape),
        ],
        out_specs=[rows_of(TILE, width)] + [whole((width // side, cols))] * side + [whole((16, LANES))],
        out_shape=[far_shape((rows, width), BF)]
        + [far_shape((width // side, cols), BF)] * side
        + [far_shape((16, LANES))],
        scratch_shapes=[
            pltpu.VMEM((rows, cols), BF),
            pltpu.VMEM((TILE, rows), BF),
            pltpu.VMEM((16, LANES), F32),
            pltpu.VMEM((col_bands, LANES), F32),
            pltpu.VMEM((row_bands, LANES), F32),
            pltpu.VMEM((row_bands, LANES), F32),
            pltpu.VMEM((width, cols), BF),
            pltpu.VMEM((2 * TILE, width), BF),
        ],
        compiler_params=PARAMS,
        name="final_kernel",
    )(order, block_embed, mate_row, proto_t, proto_bf, raw_t, norm, recv_col, recv_row, recv_soft)


    def shifted(axis, d):
        moves = []
        for b in range(n_batch):
            y, z = divmod(b, side)
            moves.append((b, (y + d) % side * side + z if axis == 0 else y * side + (z + d) % side))
        return moves

    pieces = [pieces[0]] + [lax.ppermute(pieces[d], "batch", shifted(0, d)) for d in range(1, side)]
    d_unit_got = deal(d_unit.reshape(n_proto, own, width), "proto")
    stat_spec = whole((hid_bands, LANES))
    mean_late, inv, _ = lax.optimization_barrier((mean, inv, d_unit))
    normed, slope, hid = pl.pallas_call(
        slab_kernel,
        grid_spec=pltpu.PrefetchScalarGridSpec(
            num_scalar_prefetch=1,
            grid=(1,),
            in_specs=[stat_spec] * 4 + [anywhere] * (1 + len(parts)),
            out_specs=[pl.BlockSpec(memory_space=pltpu.HBM)] * 3,
            scratch_shapes=[pltpu.VMEM((rows, slab), BF)] * 3
            + [
                pltpu.VMEM((rows, d_in), BF),
                pltpu.VMEM((d_in, slab), BF),
                pltpu.SemaphoreType.DMA((len(parts) + 1 + 3 * (rows // TILE),)),
            ],
        ),
        out_shape=[shape((rows, slab), BF)] * 3,
        name="slab_kernel",
    )(order, mean_late, inv, gain, bias, w_first, *parts)
    d_unit, normed, slope, hid = lax.optimization_barrier((d_unit_got, normed, slope, hid))
    d_embed = pl.pallas_call(
        d_embed_kernel, out_shape=shape((n_proto, own, width), BF), compiler_params=PARAMS, name="d_embed_kernel"
    )(d_unit, unit_embed, embed_scale)
    d_embed = deal(d_embed, "proto")

    shift, msg = pl.pallas_call(
        shift_kernel,
        grid_spec=pltpu.PrefetchScalarGridSpec(
            num_scalar_prefetch=1,
            grid=(1,),
            in_specs=[
                whole((n_proto, own, width)),
                pl.BlockSpec((slab, width), lambda i, s: (s[0], 0)),
                anywhere,
                anywhere,
                anywhere,
                anywhere,
            ],
            out_specs=[whole((rows, slab)), whole((n_batch, 2 * slab // n_batch, width))],
            scratch_shapes=[pltpu.VMEM((8, slab), F32), pltpu.VMEM((16, LANES), F32)]
            + [pltpu.VMEM((rows, slab), BF)] * 3
            + [pltpu.SemaphoreType.DMA((4,))],
        ),
        out_shape=[shape((rows, slab)), shape((n_batch, 2 * slab // n_batch, width), BF)],
        compiler_params=PARAMS,
        name="shift_kernel",
    )(order, d_embed, w_second, far(normed), far(slope), far(hid), far(loss_tile))
    recv = deal(msg, "batch")

    share = d_in // (n_batch * n_proto)
    lines = slab // LANES * share + 8
    first, second = pl.pallas_call(
        lambda *refs: first_kernel(total_rows, *refs),
        grid_spec=pltpu.PrefetchScalarGridSpec(
            num_scalar_prefetch=1,
            grid=(1,),
            in_specs=[whole(recv.shape), whole((rows, slab)), whole((rows, slab)), stat_spec, stat_spec]
            + [whole(piece.shape) for piece in parts],
            out_specs=[pl.BlockSpec(memory_space=pltpu.HBM), whole((slab // n_batch, width))],
            scratch_shapes=[
                pltpu.VMEM((rows, slab), BF),
                pltpu.VMEM((n_batch * n_proto, lines, LANES), BF),
                pltpu.SemaphoreType.DMA((d_in // TILE,)),
            ],
        ),
        out_shape=[far_shape((n_batch * n_proto, lines, LANES), BF), shape((slab // n_batch, width))],
        compiler_params=PARAMS,
        name="first_kernel",
    )(order, recv, shift, normed, inv, gain, *parts)

    first, *pieces = lax.optimization_barrier((first, *pieces))
    pieces = pl.pallas_call(
        stage_kernel,
        in_specs=[pl.BlockSpec(memory_space=pltpu.SMEM)] + [pl.BlockSpec((width // side, cols), lambda: (0, 0))] * side,
        out_shape=[shape((width // n_batch, cols), BF)] * side,
        scratch_shapes=[pltpu.VMEM((width // side, cols), BF)],
        name="stage_kernel",
    )(order, *pieces)
    pieces = [pieces[0]] + [lax.ppermute(pieces[d], "batch", shifted(1, d)) for d in range(1, side)]
    grad_proto = sum(piece.astype(F32) for piece in pieces).T
    first = deal(first, ("batch", "proto")).reshape(n_batch, n_proto, lines, LANES)
    grad_first, grad_gain, grad_bias, loss = pl.pallas_call(
        lambda *refs: tail_kernel(total_rows, *refs),
        out_shape=[shape((share, d_hid)), shape((hid_bands, LANES)), shape((hid_bands, LANES)), shape((1, LANES))],
        compiler_params=PARAMS,
        name="tail_kernel",
    )(first)
    grad_second = lax.ppermute(
        second,
        ("batch", "proto"),
        [(b * n_proto + p, p * n_batch + b) for b in range(n_batch) for p in range(n_proto)],
    )
    grad_gain = grad_gain.reshape(-1)
    grad_bias = grad_bias.reshape(-1)
    loss = loss[0, 0]
    return (grad_first, grad_second, grad_gain, grad_bias, grad_proto, loss)


def solution(mesh):
    return jax.shard_map(
        step_of_device,
        mesh=mesh,
        in_specs=(P(("batch", "proto"), None), P(), P(), P(), P(), P("proto", None), P("batch")),
        out_specs=(
            P(("batch", "proto"), None),
            P(("batch", "proto"), None),
            P(),
            P(),
            P("proto", "batch"),
            P(),
        ),
        check_vma=False,
    )
```

```python
import jax
import jax.numpy as jnp
from jax import lax
from jax.experimental import pallas as pl
from jax.experimental.pallas import tpu as pltpu
from jax.sharding import PartitionSpec as P


ITERS = 3
BF = jnp.bfloat16
F32 = jnp.float32
LANES = 128
TILE = 256
LOG2_E = 1.4426950408889634
PARAMS = pltpu.CompilerParams(vmem_limit_bytes=24 * 1024 * 1024)


def deal(x, axis):
    return lax.all_to_all(x, axis, 0, 0, tiled=True)


def tdot(a, b, a_dim, b_dim):
    return lax.dot_general(a, b, (((a_dim,), (b_dim,)), ((), ())), preferred_element_type=F32)


def fold_rows(v):
    return jnp.sum(v.reshape(v.shape[0] // 8, 8, LANES), axis=0)


def as_column(row):
    return jnp.broadcast_to(row, (LANES, LANES)).T


def lane(j):
    return slice(j * LANES, (j + 1) * LANES)


def whole(shape):
    return pl.BlockSpec(shape, lambda i, *_: (0,) * len(shape))


def rows_of(rows, width):
    return pl.BlockSpec((rows, width), lambda i, *_: (i, 0))


def pre_kernel(features_ref, w_hbm, pre_ref, msg_ref, stat_ref, w_buf, sems):
    pieces, depth, width = w_buf.shape
    copies = [
        pltpu.make_async_copy(w_hbm.at[k * depth : (k + 1) * depth], w_buf.at[k], sems.at[k]) for k in range(pieces)
    ]
    for copy in copies:
        copy.start()
    half = stat_ref.shape[0] // 2
    for k in range(pieces):
        copies[k].wait()
        for j in range(width // TILE):
            span = slice(j * TILE, (j + 1) * TILE)
            part = jnp.dot(features_ref[:, k * depth : (k + 1) * depth], w_buf[k, :, span], preferred_element_type=F32)
            pre = part if k == 0 else pre_ref[:, span] + part
            pre_ref[:, span] = pre
            if k == pieces - 1:
                for h in range(TILE // LANES):
                    at = j * (TILE // LANES) + h
                    piece = pre[:, lane(h)]
                    stat_ref[at : at + 1, :] = jnp.sum(piece, axis=0, keepdims=True)
                    stat_ref[half + at : half + at + 1, :] = jnp.sum(piece * piece, axis=0, keepdims=True)
    msg_ref[...] = jnp.broadcast_to(stat_ref[...][None], msg_ref.shape)


def relay_kernel(recv_ref, msg_ref):
    msg_ref[...] = jnp.broadcast_to(jnp.sum(recv_ref[...], axis=0, keepdims=True), msg_ref.shape)


def embed_kernel(
    total_rows, pre_ref, recv_ref, gain_ref, bias_ref, w2_ref, unit_hbm, mean_hbm, inv_hbm, msg_hbm,
    hid_ref, unit_ref, mean_ref, inv_ref, bf_ref, sems,
):
    stats = jnp.sum(recv_ref[...], axis=0)
    half = stats.shape[0] // 2
    mean = stats[:half] / total_rows
    inv = lax.rsqrt(stats[half:] / total_rows - mean * mean + 1e-05)
    mean_ref[...] = mean
    inv_ref[...] = inv
    for j in range(half):
        normed = (pre_ref[:, lane(j)] - mean[j : j + 1]) * inv[j : j + 1]
        hid_ref[:, lane(j)] = jax.nn.gelu(normed * gain_ref[j : j + 1, :] + bias_ref[j : j + 1, :]).astype(BF)
    embed = jnp.dot(hid_ref[...], w2_ref[...], preferred_element_type=F32)
    scale = lax.rsqrt(jnp.sum(embed * embed, axis=1, keepdims=True) + 1e-06)
    unit = embed * scale
    bf_ref[...] = unit.astype(BF)
    width = unit.shape[1]
    unit_ref[:, :width] = unit
    unit_ref[:, width:] = jnp.broadcast_to(scale, (unit.shape[0], LANES))
    moves = [(bf_ref, msg_hbm.at[k]) for k in range(msg_hbm.shape[0])]
    moves += [(unit_ref, unit_hbm), (mean_ref, mean_hbm), (inv_ref, inv_hbm)]
    copies = [pltpu.make_async_copy(src, dst, sems.at[k]) for k, (src, dst) in enumerate(moves)]
    for copy in copies:
        copy.start()
    for copy in copies:
        copy.wait()


def proto_kernel(order_ref, raw_ref, w_hbm, proto_ref, proto_t_ref, raw_t_ref, norm_ref, slab_hbm, slab_ref, sem):
    slab = slab_ref.shape[1]
    at = pl.ds(pl.multiple_of(order_ref[0] * slab, slab), slab)
    fetch = pltpu.make_async_copy(w_hbm.at[:, at], slab_ref, sem)
    store = pltpu.make_async_copy(slab_ref, slab_hbm, sem)
    fetch.start()
    for k in range(raw_ref.shape[0] // TILE):
        span = slice(k * TILE, (k + 1) * TILE)
        raw_t = raw_ref[span, :].T
        raw_t_ref[:, span] = raw_t
        wide = raw_t.astype(F32)
        scale = lax.rsqrt(jnp.sum(wide * wide, axis=0, keepdims=True) + 1e-06)
        norm_ref[:, span] = jnp.broadcast_to(scale, (8, TILE))
        unit = (wide * scale).astype(BF)
        proto_t_ref[:, span] = unit
        proto_ref[span, :] = unit.T
        if k == 3:
            fetch.wait()
            store.start()
    store.wait()


def score_kernel(embed_ref, proto_t_hbm, kern_ref, msg_ref, soft_ref, acc_ref, proto_t_ref, sems):
    step = pl.program_id(0)
    rows = embed_ref.shape[0]
    cols = proto_t_ref.shape[1]

    def copy(j):
        span = slice(j * TILE, (j + 1) * TILE)
        return pltpu.make_async_copy(proto_t_hbm.at[:, span], proto_t_ref.at[:, span], sems.at[j])

    @pl.when(step == 0)
    def _():
        for j in range(cols // TILE):
            copy(j).start()
        acc_ref[...] = jnp.zeros_like(acc_ref)

    soft = [None] * (rows // LANES)
    for j in range(cols // TILE):
        span = slice(j * TILE, (j + 1) * TILE)
        if j % 2 == 0:

            @pl.when(step == 0)
            def _():
                copy(j).wait()
                copy(j + 1).wait()

        scores = jnp.dot(embed_ref[...], proto_t_ref[:, span], preferred_element_type=F32)
        tempered = jnp.exp2(scores * (10.0 * LOG2_E))
        kern = tempered * tempered
        kern_ref[:, span] = kern.astype(BF)
        for h in range(TILE // LANES):
            at = (j * (TILE // LANES) + h) * 8
            acc_ref[at : at + 8, :] += fold_rows(kern[:, lane(h)])
        for b in range(rows // LANES):
            part = tempered[b * LANES : (b + 1) * LANES]
            part = part[:, :LANES] + part[:, LANES:]
            soft[b] = part if soft[b] is None else soft[b] + part
    for b in range(rows // LANES):
        soft_ref[pl.ds(step * (rows // LANES) + b, 1), :] = jnp.sum(soft[b].T, axis=0, keepdims=True)

    @pl.when(step == pl.num_programs(0) - 1)
    def _():
        total = jnp.sum(acc_ref[...].reshape(cols // LANES, 8, LANES), axis=1)
        msg_ref[...] = jnp.broadcast_to(total[None], msg_ref.shape)


def row_kernel(recv_ref, kern_ref, *rest):
    soft_ref = rest[0] if len(rest) == 3 else None
    msg_ref, scale_ref = rest[-2:]
    step = pl.program_id(0)
    rows = kern_ref.shape[0]
    copies = msg_ref.shape[0]

    @pl.when(step == 0)
    def _():
        scale_ref[...] = 1.0 / jnp.sum(recv_ref[...], axis=0)
        if soft_ref is not None:
            half = soft_ref.shape[0]
            msg_ref[:, half:, :] = jnp.broadcast_to(soft_ref[...][None], (copies, half, LANES))

    for b in range(rows // LANES):
        acc = None
        for j in range(scale_ref.shape[0]):
            part = kern_ref[b * LANES : (b + 1) * LANES, lane(j)].astype(F32) * scale_ref[j : j + 1, :]
            acc = part if acc is None else acc + part
        row = jnp.sum(acc.T, axis=0, keepdims=True)
        msg_ref[:, pl.ds(step * (rows // LANES) + b, 1), :] = jnp.broadcast_to(row[None], (copies, 1, LANES))


def col_kernel(recv_ref, kern_ref, msg_ref, acc_ref, scale_ref):
    step = pl.program_id(0)
    rows, cols = kern_ref.shape

    @pl.when(step == 0)
    def _():
        acc_ref[...] = jnp.zeros_like(acc_ref)
        scale_ref[...] = 1.0 / jnp.sum(recv_ref[:, : scale_ref.shape[0], :], axis=0)

    for b in range(rows // LANES):
        scale = as_column(scale_ref[pl.ds(step * (rows // LANES) + b, 1), :])
        for j in range(cols // LANES):
            part = kern_ref[b * LANES : (b + 1) * LANES, lane(j)].astype(F32) * scale
            acc_ref[j * 8 : (j + 1) * 8, :] += fold_rows(part)

    @pl.when(step == pl.num_programs(0) - 1)
    def _():
        total = jnp.sum(acc_ref[...].reshape(cols // LANES, 8, LANES), axis=1)
        msg_ref[...] = jnp.broadcast_to(total[None], msg_ref.shape)


def final_kernel(
    order_ref, embed_ref, pair_ref, proto_t_ref, proto_ref, raw_t_ref, norm_ref, recv_col_ref, recv_row_ref, recv_soft_ref,
    d_unit_ref, piece0_ref, piece1_ref, piece2_ref, piece3_ref, loss_ref,
    grad_ref, mate_ref, loss_acc_ref, col_ref, row_ref, soft_ref, term_ref, both_ref,
):
    step = pl.program_id(0)
    rows = d_unit_ref.shape[0]
    cols = proto_t_ref.shape[1]
    bands = row_ref.shape[0]
    chunks = TILE // LANES

    @pl.when(step == 0)
    def _():
        loss_acc_ref[...] = jnp.zeros_like(loss_acc_ref)
        col_ref[...] = 10.0 / jnp.sum(recv_col_ref[...], axis=0)
        row_ref[...] = 1.0 / jnp.sum(recv_row_ref[:, :bands, :], axis=0)
        soft_ref[...] = jnp.sum(recv_soft_ref[:, bands:, :], axis=0)
        loss_acc_ref[8:16, :] = jnp.log(soft_ref[...])

    base = step * (rows // LANES)
    here = pl.ds(pl.multiple_of(step * rows, rows), rows)
    spot = lax.broadcasted_iota(jnp.int32, (LANES, LANES), 1)
    scales = []
    for b in range(rows // LANES):
        pair = as_column(pair_ref[pl.ds(base + b, 1), :]).astype(jnp.int32)
        found = jnp.zeros((LANES, LANES), F32)
        for q in range(bands):
            hot = spot + q * LANES == pair
            found += jnp.where(hot, row_ref[q : q + 1, :], 0.0)
            mate_ref[b * LANES : (b + 1) * LANES, lane(q)] = jnp.where(hot, 1.0, 0.0).astype(BF)
        scales.append(jnp.broadcast_to(jnp.sum(found, axis=1, keepdims=True), (LANES, LANES)))
    mate_scale = jnp.concatenate(scales, axis=0)
    both_ref[0:rows, :] = embed_ref[here, :]
    both_ref[rows:, :] = jnp.dot(mate_ref[...], embed_ref[...], preferred_element_type=F32).astype(BF)
    soft = jnp.concatenate([as_column(soft_ref[pl.ds(base + b, 1), :]) for b in range(rows // LANES)], axis=0)
    inv_soft = 10.0 / soft
    loss_acc = jnp.zeros((8, LANES), F32)
    for j in range(cols // TILE):
        span = slice(j * TILE, (j + 1) * TILE)
        both = jnp.dot(both_ref[...], proto_t_ref[:, span], preferred_element_type=F32)
        scores, mates = both[:rows], both[rows:]
        for h in range(chunks):
            at = j * chunks + h
            target = jnp.exp2(mates[:, lane(h)] * (20.0 * LOG2_E)) * mate_scale * col_ref[at : at + 1, :]
            score = scores[:, lane(h)]
            loss_acc += fold_rows(target * score)
            grad_ref[here, lane(at)] = (jnp.exp2(score * (10.0 * LOG2_E)) * inv_soft - target).astype(BF)
    d_unit_ref[...] = jnp.dot(grad_ref[here, :], proto_ref[...], preferred_element_type=F32).astype(BF)
    loss_acc_ref[0:8, :] += loss_acc

    @pl.when(step == pl.num_programs(0) - 1)
    def _():
        embed_t = embed_ref[...].T
        for j in range(cols // TILE):
            span = slice(j * TILE, (j + 1) * TILE)
            raw = raw_t_ref[:, span].astype(F32)
            scale = norm_ref[0:1, span]
            acc = jnp.dot(embed_t, grad_ref[:, span], preferred_element_type=F32)
            along = scale * scale * jnp.sum(raw * acc, axis=0, keepdims=True)
            term_ref[:, span] = ((acc - raw * along) * scale).astype(BF)
        pieces = (piece0_ref, piece1_ref, piece2_ref, piece3_ref)
        for d, piece in enumerate(pieces):
            height = piece.shape[0]
            at = pl.multiple_of(lax.rem(order_ref[9] + d, len(pieces)) * height, height)
            piece[...] = term_ref[pl.ds(at, height), :]
        loss_ref[...] = loss_acc_ref[...]


def d_embed_kernel(recv_ref, unit_ref, msg_ref):
    d_unit = jnp.sum(recv_ref[...].astype(F32), axis=0)
    width = d_unit.shape[1]
    unit = unit_ref[:, :width]
    d_embed = (d_unit - unit * jnp.sum(unit * d_unit, axis=1, keepdims=True)) * unit_ref[:, width : width + 1]
    msg_ref[...] = jnp.broadcast_to(d_embed.astype(BF)[None], msg_ref.shape)


def start_parts(parts, buf_ref, sems):
    copies = []
    at = 0
    for k, part in enumerate(parts):
        height = part.shape[0]
        copies.append(pltpu.make_async_copy(part, buf_ref.at[at : at + height], sems.at[k]))
        at += height
    for copy in copies:
        copy.start()
    return copies


def slab_kernel(order_ref, mean_ref, inv_ref, gain_ref, bias_ref, w_hbm, *rest):
    parts = rest[:-9]
    outs, bufs = rest[-9:-6], rest[-6:-3]
    buf_ref, w_ref, sems = rest[-3:]
    normed_ref, slope_ref, hid_ref = bufs
    rows, slab = normed_ref.shape
    w_copy = pltpu.make_async_copy(w_hbm, w_ref, sems.at[len(parts)])
    w_copy.start()
    copies = start_parts(parts, buf_ref, sems)
    stops = [sum(part.shape[0] for part in parts[: k + 1]) for k in range(len(parts))]
    w_copy.wait()
    chunks = slab // LANES
    ones = jnp.ones((LANES, LANES), F32)
    done = 0
    sends = []
    for g in range(rows // TILE):
        start = g * TILE
        while done < len(parts) and (stops[done - 1] if done else 0) < start + TILE:
            copies[done].wait()
            done += 1
        pre = jnp.dot(buf_ref[start : start + TILE, :], w_ref[...], preferred_element_type=F32)
        for h in range(chunks):
            at = pl.ds(order_ref[0] * chunks + h, 1)
            mean, inv, gain, bias = mean_ref[at, :], inv_ref[at, :], gain_ref[at, :], bias_ref[at, :]
            for b in range(TILE // LANES):
                band = slice(start + b * LANES, start + (b + 1) * LANES)
                normed = (pre[b * LANES : (b + 1) * LANES, lane(h)] - mean) * inv
                hidden, back = jax.vjp(jax.nn.gelu, normed * gain + bias)
                normed_ref[band, lane(h)] = normed.astype(BF)
                slope_ref[band, lane(h)] = back(ones)[0].astype(BF)
                hid_ref[band, lane(h)] = hidden.astype(BF)
        span = slice(start, start + TILE)
        for k, (buf, out) in enumerate(zip(bufs, outs)):
            sends.append(
                pltpu.make_async_copy(buf.at[span], out.at[span], sems.at[len(parts) + 1 + g * len(outs) + k])
            )
            sends[-1].start()
    for send in sends:
        send.wait()


def shift_kernel(
    order_ref, d_embed_ref, w2_ref, normed_hbm, slope_hbm, hid_hbm, loss_hbm, shift_ref, msg_ref, sum_ref, loss_ref,
    normed_ref, slope_ref, hid_ref, sems,
):
    moves = ((slope_hbm, slope_ref), (normed_hbm, normed_ref), (hid_hbm, hid_ref), (loss_hbm, loss_ref))
    copies = [pltpu.make_async_copy(src, dst, sems.at[k]) for k, (src, dst) in enumerate(moves)]
    for copy in copies:
        copy.start()
    n_blocks, own, _ = d_embed_ref.shape
    sum_ref[...] = jnp.zeros_like(sum_ref)
    gains = biases = second = None
    for copy in copies:
        copy.wait()
    for k in range(0, n_blocks, 2):
        d_embed = jnp.concatenate([d_embed_ref[order_ref[k + 1]], d_embed_ref[order_ref[k + 2]]], axis=0)
        band = slice(k * own, (k + 2) * own)
        d_shift = tdot(d_embed, w2_ref[...], 1, 1) * slope_ref[band, :].astype(F32)
        shift_ref[band, :] = d_shift
        gain = jnp.sum(d_shift * normed_ref[band, :].astype(F32), axis=0, keepdims=True)
        bias = jnp.sum(d_shift, axis=0, keepdims=True)
        part = tdot(hid_ref[band, :], d_embed, 0, 0)
        gains = gain if gains is None else gains + gain
        biases = bias if biases is None else biases + bias
        second = part if second is None else second + part
    hits = jnp.sum(loss_ref[0:8, :], axis=0, keepdims=True)
    logs = jnp.sum(loss_ref[8:16, :], axis=0, keepdims=True)
    sum_ref[0:1, :] = gains
    sum_ref[1:2, :] = biases
    sum_ref[2:3, :] = jnp.concatenate([hits, logs], axis=1)
    n, _, slab = msg_ref.shape
    share = slab // n
    sums = sum_ref[...]
    high = sums.astype(BF)
    rest = sums - high.astype(F32)
    mid = rest.astype(BF)
    low = (rest - mid.astype(F32)).astype(BF)
    row = lax.broadcasted_iota(jnp.int32, sums.shape, 0)
    lower = jnp.where(row < 4, mid.astype(F32), pltpu.roll(low.astype(F32), 4, 0))
    packed = jnp.concatenate([high.astype(F32), lower], axis=0).astype(BF)
    msg_ref[:, :share, :] = jnp.broadcast_to(packed[None], (n, share, slab))
    msg_ref[:, share:, :] = second.astype(BF).reshape(n, share, slab)


def halves(v):
    high = v.astype(BF)
    return high, (v - high.astype(F32)).astype(BF)


def first_kernel(total_rows, order_ref, recv_ref, shift_ref, normed_ref, inv_ref, gain_ref, *rest):
    parts = rest[:-5]
    out_hbm, second_ref, d_pre_ref, out_ref, sems = rest[-5:]
    n, _, _ = out_ref.shape
    slab = d_pre_ref.shape[1]
    share = second_ref.shape[0]
    second_ref[...] = jnp.sum(recv_ref[:, share:, :].astype(F32), axis=0)
    got = jnp.sum(recv_ref[:, :share, :].astype(F32), axis=0)
    got = got[0:8] + (got[8:16] + pltpu.roll(got[8:16], 4, 0))
    chunks = slab // LANES
    for h in range(chunks):
        at = pl.ds(order_ref[0] * chunks + h, 1)
        factor = gain_ref[at, :] * inv_ref[at, :]
        gain_mean = got[0:1, lane(h)] / total_rows
        bias_mean = got[1:2, lane(h)] / total_rows
        for b in range(d_pre_ref.shape[0] // LANES):
            band = slice(b * LANES, (b + 1) * LANES)
            d_pre = factor * (shift_ref[band, lane(h)] - bias_mean - normed_ref[band, lane(h)].astype(F32) * gain_mean)
            d_pre_ref[band, lane(h)] = d_pre.astype(BF)
    high, low = halves(got[0:2])
    sums = [piece[k : k + 1, lane(h)] for k in range(2) for piece in (high, low) for h in range(chunks)]
    high, rest_of = got[2:3].astype(BF), got[2:3] - got[2:3].astype(BF).astype(F32)
    losses = [piece[:, lane(h)] for piece in (high,) + halves(rest_of) for h in range(chunks)]
    losses += [jnp.zeros((1, LANES), BF)] * (8 - len(losses))
    odd = lax.rem(order_ref[10], 2) == 1
    extra = jnp.where(
        odd,
        jnp.concatenate([v.astype(F32) for v in losses], axis=0),
        jnp.concatenate([v.astype(F32) for v in sums], axis=0),
    ).astype(BF)
    out_ref[:, chunks * share :, :] = jnp.broadcast_to(extra[None], (n, 8, LANES))
    group = TILE // share
    copies = []
    for j in range(n // group):
        tile = jnp.concatenate([part[:, j * TILE : (j + 1) * TILE] for part in parts], axis=0)
        grad = tdot(tile, d_pre_ref[...], 0, 0).astype(BF)
        span = slice(j * group, (j + 1) * group)
        for h in range(chunks):
            out_ref[span, h * share : (h + 1) * share, :] = grad[:, lane(h)].reshape(group, share, LANES)
        copies.append(pltpu.make_async_copy(out_ref.at[span], out_hbm.at[span], sems.at[j]))
        copies[-1].start()
    for copy in copies:
        copy.wait()


def tail_kernel(total_rows, recv_ref, out_ref, gain_ref, bias_ref, loss_ref):
    n_batch, n_proto, height, _ = recv_ref.shape
    share = out_ref.shape[0]
    chunks = height // share
    lines = jnp.zeros((8, LANES), F32)
    for p in range(n_proto):
        acc = recv_ref[0, p].astype(F32)
        for b in range(1, n_batch):
            acc += recv_ref[b, p].astype(F32)
        for h in range(chunks):
            at = (p * chunks + h) * LANES
            out_ref[:, at : at + LANES] = acc[h * share : (h + 1) * share, :]
        sums = recv_ref[0, p, chunks * share :, :].astype(F32)
        for h in range(chunks):
            at = p * chunks + h
            gain_ref[at : at + 1, :] = sums[h : h + 1] + sums[chunks + h : chunks + h + 1]
            bias_ref[at : at + 1, :] = sums[2 * chunks + h : 2 * chunks + h + 1] + sums[3 * chunks + h : 3 * chunks + h + 1]
        lines += recv_ref[1, p, chunks * share :, :].astype(F32)
    hits = lines[0:1] + (lines[2:3] + lines[4:5])
    logs = (lines[1:2] + (lines[3:4] + lines[5:6])) / n_proto
    loss = jnp.sum(logs - hits, axis=1, keepdims=True) / total_rows
    loss_ref[...] = jnp.broadcast_to(loss, loss_ref.shape)


def stage_kernel(order_ref, in0_ref, in1_ref, in2_ref, in3_ref, out0_ref, out1_ref, out2_ref, out3_ref, sum_ref):
    near = in0_ref[...].astype(F32) + in1_ref[...].astype(F32)
    sum_ref[...] = (near + (in2_ref[...].astype(F32) + in3_ref[...].astype(F32))).astype(BF)
    outs = (out0_ref, out1_ref, out2_ref, out3_ref)
    for d, out in enumerate(outs):
        height = out.shape[0]
        at = pl.multiple_of(lax.rem(order_ref[10] + d, len(outs)) * height, height)
        out[...] = sum_ref[pl.ds(at, height), :]


def shape(dims, kind=F32):
    return jax.ShapeDtypeStruct(dims, kind)


def far_shape(dims, kind=F32):
    return pltpu.HBM(dims, kind)


def far(x):
    return pltpu.with_memory_space_constraint(x, pltpu.HBM)


def step_of_device(features, w_first, bn_gain, bn_bias, w_second, prototypes, pair):
    n_batch = lax.axis_size("batch")
    n_proto = lax.axis_size("proto")
    own, d_in = features.shape
    d_hid, width = w_second.shape
    cols = prototypes.shape[0]
    total_rows = own * n_batch * n_proto
    rows = own * n_proto
    part = lax.axis_index("proto")
    slab = d_hid // n_proto
    col_bands = cols // LANES
    row_bands = rows // LANES
    hid_bands = d_hid // LANES
    steps = rows // TILE
    gain = bn_gain.reshape(hid_bands, LANES)
    bias = bn_bias.reshape(hid_bands, LANES)

    def hop(x, moves):
        return lax.ppermute(x, "proto", moves)

    ring = n_proto // 2
    right = [(i * 2 + c, (i + 1) % ring * 2 + c) for i in range(ring) for c in range(2)]
    left = [(t, s) for s, t in right]
    swap = [(i, i ^ 1) for i in range(n_proto)]
    from_left = hop(features, right)
    from_right = hop(features, left)
    across = lax.shift_right_logical(part, 1)
    place = lax.axis_index("batch")
    side = 4
    order = jnp.stack(
        [part]
        + [
            (lax.bitwise_and(across + d, ring - 1) * 2 + lax.bitwise_and(part, 1)) ^ o
            for o in range(2)
            for d in (0, 1, 3, 2)
        ]
        + [lax.shift_right_logical(place, 2), lax.bitwise_and(place, side - 1)]
    ).astype(jnp.int32)
    mate_row = (pair - place * rows).astype(F32).reshape(row_bands, LANES)

    anywhere = pl.BlockSpec(memory_space=pl.ANY)
    pre, msg = pl.pallas_call(
        pre_kernel,
        in_specs=[pl.BlockSpec(features.shape, lambda: (0, 0)), anywhere],
        out_shape=[shape((own, d_hid)), shape((n_batch, 2 * hid_bands, LANES))],
        scratch_shapes=[
            pltpu.VMEM((2 * hid_bands, LANES), F32),
            pltpu.VMEM((4, d_in // 4, d_hid), BF),
            pltpu.SemaphoreType.DMA((4,)),
        ],
        name="pre_kernel",
    )(features, w_first)
    near_left, near_right, _ = lax.optimization_barrier((from_left, from_right, pre))
    far_top = hop(near_left[: own // 2], right)
    far_low = hop(near_right[own // 2 :], left)
    got = deal(msg, "batch")
    got, mate_row, order = lax.optimization_barrier((got, mate_row, order))
    msg = pl.pallas_call(
        relay_kernel, out_shape=shape((n_proto, 2 * hid_bands, LANES)), compiler_params=PARAMS, name="relay_kernel"
    )(got)
    got = deal(msg, "proto")
    unit_embed, mean, inv, msg = pl.pallas_call(
        lambda *refs: embed_kernel(total_rows, *refs),
        out_specs=[pl.BlockSpec(memory_space=pltpu.HBM)] * 4,
        out_shape=[
            far_shape((own, width + LANES)),
            far_shape((hid_bands, LANES)),
            far_shape((hid_bands, LANES)),
            far_shape((n_proto, own, width), BF),
        ],
        scratch_shapes=[
            pltpu.VMEM((own, d_hid), BF),
            pltpu.VMEM((own, width + LANES), F32),
            pltpu.VMEM((hid_bands, LANES), F32),
            pltpu.VMEM((hid_bands, LANES), F32),
            pltpu.VMEM((own, width), BF),
            pltpu.SemaphoreType.DMA((n_proto + 3,)),
        ],
        compiler_params=PARAMS,
        name="embed_kernel",
    )(pre, got, gain, bias, w_second)
    raw, *mine, _ = lax.optimization_barrier((prototypes, features, from_right, from_left, far_top, far_low, msg))
    parts = mine + [hop(piece, swap) for piece in mine]
    proto_bf, proto_t, raw_t, norm, w_slab = pl.pallas_call(
        proto_kernel,
        in_specs=[pl.BlockSpec(memory_space=pltpu.SMEM), pl.BlockSpec((cols, width), lambda: (0, 0)), anywhere],
        out_specs=[
            pl.BlockSpec((cols, width), lambda: (0, 0)),
            pl.BlockSpec((width, cols), lambda: (0, 0)),
            pl.BlockSpec((width, cols), lambda: (0, 0)),
            pl.BlockSpec((8, cols), lambda: (0, 0)),
            anywhere,
        ],
        out_shape=[
            shape((cols, width), BF),
            shape((width, cols), BF),
            shape((width, cols), BF),
            shape((8, cols)),
            far_shape((d_in, slab), BF),
        ],
        scratch_shapes=[pltpu.VMEM((d_in, slab), BF), pltpu.SemaphoreType.DMA],
        name="proto_kernel",
    )(order, raw, w_first)
    block_embed, proto_bf, proto_t, raw_t, norm, w_slab, *parts = lax.optimization_barrier(
        (deal(msg, "proto"), proto_bf, proto_t, raw_t, norm, w_slab, *parts)
    )
    block_embed = block_embed.reshape(rows, width)

    kern, col_msg, soft = pl.pallas_call(
        score_kernel,
        grid=(steps,),
        in_specs=[rows_of(TILE, width), anywhere],
        out_specs=[rows_of(TILE, cols), whole((n_batch, col_bands, LANES)), whole((row_bands, LANES))],
        out_shape=[shape((rows, cols), BF), shape((n_batch, col_bands, LANES)), shape((row_bands, LANES))],
        scratch_shapes=[
            pltpu.VMEM((col_bands * 8, LANES), F32),
            pltpu.VMEM((width, cols), BF),
            pltpu.SemaphoreType.DMA((cols // TILE,)),
        ],
        compiler_params=PARAMS,
        name="score_kernel",
    )(block_embed, far(proto_t))

    def row_pass(recv, extra):
        height = row_bands * (2 if extra else 1)
        return pl.pallas_call(
            row_kernel,
            grid=(steps,),
            in_specs=[whole((n_batch, col_bands, LANES)), rows_of(TILE, cols)]
            + [whole((row_bands, LANES)) for _ in extra],
            out_specs=whole((n_proto, height, LANES)),
            out_shape=shape((n_proto, height, LANES)),
            scratch_shapes=[pltpu.VMEM((col_bands, LANES), F32)],
            compiler_params=PARAMS,
        name="row_kernel",
        )(recv, kern, *extra)

    def col_pass(recv):
        return pl.pallas_call(
            col_kernel,
            grid=(steps,),
            in_specs=[whole(recv.shape), rows_of(TILE, cols)],
            out_specs=whole((n_batch, col_bands, LANES)),
            out_shape=shape((n_batch, col_bands, LANES)),
            scratch_shapes=[pltpu.VMEM((col_bands * 8, LANES), F32), pltpu.VMEM((row_bands, LANES), F32)],
            compiler_params=PARAMS,
        name="col_kernel",
        )(recv, kern)

    recv_soft = None
    for step in range(ITERS):
        recv_col = deal(col_msg, "batch")
        recv_row = deal(row_pass(recv_col, () if step else (soft,)), "proto")
        recv_soft = recv_row if recv_soft is None else recv_soft
        if step + 1 < ITERS:
            col_msg = col_pass(recv_row)

    d_unit, *pieces, loss_tile = pl.pallas_call(
        final_kernel,
        grid=(steps // 2,),
        in_specs=[
            pl.BlockSpec(memory_space=pltpu.SMEM),
            whole((rows, width)),
            whole((row_bands, LANES)),
            whole((width, cols)),
            whole((cols, width)),
            whole((width, cols)),
            whole((8, cols)),
            whole(recv_col.shape),
            whole(recv_row.shape),
            whole(recv_soft.shape),
        ],
        out_specs=[rows_of(2 * TILE, width)] + [whole((width // side, cols))] * side + [whole((16, LANES))],
        out_shape=[far_shape((rows, width), BF)]
        + [far_shape((width // side, cols), BF)] * side
        + [far_shape((16, LANES))],
        scratch_shapes=[
            pltpu.VMEM((rows, cols), BF),
            pltpu.VMEM((2 * TILE, rows), BF),
            pltpu.VMEM((16, LANES), F32),
            pltpu.VMEM((col_bands, LANES), F32),
            pltpu.VMEM((row_bands, LANES), F32),
            pltpu.VMEM((row_bands, LANES), F32),
            pltpu.VMEM((width, cols), BF),
            pltpu.VMEM((4 * TILE, width), BF),
        ],
        compiler_params=PARAMS,
        name="final_kernel",
    )(order, block_embed, mate_row, proto_t, proto_bf, raw_t, norm, recv_col, recv_row, recv_soft)


    def shifted(axis, d):
        moves = []
        for b in range(n_batch):
            y, z = divmod(b, side)
            moves.append((b, (y + d) % side * side + z if axis == 0 else y * side + (z + d) % side))
        return moves

    pieces = [pieces[0]] + [lax.ppermute(pieces[d], "batch", shifted(0, d)) for d in range(1, side)]
    d_unit_got = deal(d_unit.reshape(n_proto, own, width), "proto")
    stat_spec = whole((hid_bands, LANES))
    mean_late, inv, _ = lax.optimization_barrier((mean, inv, d_unit))
    normed, slope, hid = pl.pallas_call(
        slab_kernel,
        grid_spec=pltpu.PrefetchScalarGridSpec(
            num_scalar_prefetch=1,
            grid=(1,),
            in_specs=[stat_spec] * 4 + [anywhere] * (1 + len(parts)),
            out_specs=[pl.BlockSpec(memory_space=pltpu.HBM)] * 3,
            scratch_shapes=[pltpu.VMEM((rows, slab), BF)] * 3
            + [
                pltpu.VMEM((rows, d_in), BF),
                pltpu.VMEM((d_in, slab), BF),
                pltpu.SemaphoreType.DMA((len(parts) + 1 + 3 * (rows // TILE),)),
            ],
        ),
        out_shape=[shape((rows, slab), BF)] * 3,
        name="slab_kernel",
    )(order, mean_late, inv, gain, bias, w_slab, *parts)
    d_unit, normed, slope, hid = lax.optimization_barrier((d_unit_got, normed, slope, hid))
    d_embed = pl.pallas_call(
        d_embed_kernel, out_shape=shape((n_proto, own, width), BF), compiler_params=PARAMS, name="d_embed_kernel"
    )(d_unit, unit_embed)
    d_embed = deal(d_embed, "proto")

    shift, msg = pl.pallas_call(
        shift_kernel,
        grid_spec=pltpu.PrefetchScalarGridSpec(
            num_scalar_prefetch=1,
            grid=(1,),
            in_specs=[
                whole((n_proto, own, width)),
                pl.BlockSpec((slab, width), lambda i, s: (s[0], 0)),
                anywhere,
                anywhere,
                anywhere,
                anywhere,
            ],
            out_specs=[whole((rows, slab)), whole((n_batch, 2 * slab // n_batch, width))],
            scratch_shapes=[pltpu.VMEM((8, slab), F32), pltpu.VMEM((16, LANES), F32)]
            + [pltpu.VMEM((rows, slab), BF)] * 3
            + [pltpu.SemaphoreType.DMA((4,))],
        ),
        out_shape=[shape((rows, slab)), shape((n_batch, 2 * slab // n_batch, width), BF)],
        compiler_params=PARAMS,
        name="shift_kernel",
    )(order, d_embed, w_second, far(normed), far(slope), far(hid), far(loss_tile))
    recv = deal(msg, "batch")

    share = d_in // (n_batch * n_proto)
    lines = slab // LANES * share + 8
    first, second = pl.pallas_call(
        lambda *refs: first_kernel(total_rows, *refs),
        grid_spec=pltpu.PrefetchScalarGridSpec(
            num_scalar_prefetch=1,
            grid=(1,),
            in_specs=[whole(recv.shape), whole((rows, slab)), whole((rows, slab)), stat_spec, stat_spec]
            + [whole(piece.shape) for piece in parts],
            out_specs=[pl.BlockSpec(memory_space=pltpu.HBM), whole((slab // n_batch, width))],
            scratch_shapes=[
                pltpu.VMEM((rows, slab), BF),
                pltpu.VMEM((n_batch * n_proto, lines, LANES), BF),
                pltpu.SemaphoreType.DMA((d_in // TILE,)),
            ],
        ),
        out_shape=[far_shape((n_batch * n_proto, lines, LANES), BF), shape((slab // n_batch, width))],
        compiler_params=PARAMS,
        name="first_kernel",
    )(order, recv, shift, normed, inv, gain, *parts)

    first, *pieces = lax.optimization_barrier((first, *pieces))
    pieces = pl.pallas_call(
        stage_kernel,
        in_specs=[pl.BlockSpec(memory_space=pltpu.SMEM)] + [pl.BlockSpec((width // side, cols), lambda: (0, 0))] * side,
        out_shape=[shape((width // n_batch, cols), BF)] * side,
        scratch_shapes=[pltpu.VMEM((width // side, cols), BF)],
        name="stage_kernel",
    )(order, *pieces)
    pieces = [pieces[0]] + [lax.ppermute(pieces[d], "batch", shifted(1, d)) for d in range(1, side)]
    grad_proto = sum(piece.astype(F32) for piece in pieces).T
    first = deal(first, ("batch", "proto")).reshape(n_batch, n_proto, lines, LANES)
    grad_first, grad_gain, grad_bias, loss = pl.pallas_call(
        lambda *refs: tail_kernel(total_rows, *refs),
        out_shape=[shape((share, d_hid)), shape((hid_bands, LANES)), shape((hid_bands, LANES)), shape((1, LANES))],
        compiler_params=PARAMS,
        name="tail_kernel",
    )(first)
    grad_second = lax.ppermute(
        second,
        ("batch", "proto"),
        [(b * n_proto + p, p * n_batch + b) for b in range(n_batch) for p in range(n_proto)],
    )
    grad_gain = grad_gain.reshape(-1)
    grad_bias = grad_bias.reshape(-1)
    loss = loss[0, 0]
    return (grad_first, grad_second, grad_gain, grad_bias, grad_proto, loss)


def solution(mesh):
    return jax.shard_map(
        step_of_device,
        mesh=mesh,
        in_specs=(P(("batch", "proto"), None), P(), P(), P(), P(), P("proto", None), P("batch")),
        out_specs=(
            P(("batch", "proto"), None),
            P(("batch", "proto"), None),
            P(),
            P(),
            P("proto", "batch"),
            P(),
        ),
        check_vma=False,
    )
```

```python
import jax
import jax.numpy as jnp
from jax import lax
from jax.experimental import pallas as pl
from jax.experimental.pallas import tpu as pltpu
from jax.sharding import PartitionSpec as P


ITERS = 3
BF = jnp.bfloat16
F32 = jnp.float32
LANES = 128
TILE = 256
LOG2_E = 1.4426950408889634
PARAMS = pltpu.CompilerParams(vmem_limit_bytes=24 * 1024 * 1024)


def deal(x, axis):
    return lax.all_to_all(x, axis, 0, 0, tiled=True)


def tdot(a, b, a_dim, b_dim):
    return lax.dot_general(a, b, (((a_dim,), (b_dim,)), ((), ())), preferred_element_type=F32)


def fold_rows(v):
    return jnp.sum(v.reshape(v.shape[0] // 8, 8, LANES), axis=0)


def as_column(row):
    return jnp.broadcast_to(row, (LANES, LANES)).T


def lane(j):
    return slice(j * LANES, (j + 1) * LANES)


def whole(shape):
    return pl.BlockSpec(shape, lambda i, *_: (0,) * len(shape))


def rows_of(rows, width):
    return pl.BlockSpec((rows, width), lambda i, *_: (i, 0))


def pre_kernel(features_ref, w_hbm, pre_ref, msg_ref, stat_ref, w_buf, sems):
    pieces, depth, width = w_buf.shape
    copies = [
        pltpu.make_async_copy(w_hbm.at[k * depth : (k + 1) * depth], w_buf.at[k], sems.at[k]) for k in range(pieces)
    ]
    for copy in copies:
        copy.start()
    half = stat_ref.shape[0] // 2
    for k in range(pieces):
        copies[k].wait()
        for j in range(width // TILE):
            span = slice(j * TILE, (j + 1) * TILE)
            part = jnp.dot(features_ref[:, k * depth : (k + 1) * depth], w_buf[k, :, span], preferred_element_type=F32)
            pre = part if k == 0 else pre_ref[:, span] + part
            pre_ref[:, span] = pre
            if k == pieces - 1:
                for h in range(TILE // LANES):
                    at = j * (TILE // LANES) + h
                    piece = pre[:, lane(h)]
                    stat_ref[at : at + 1, :] = jnp.sum(piece, axis=0, keepdims=True)
                    stat_ref[half + at : half + at + 1, :] = jnp.sum(piece * piece, axis=0, keepdims=True)
    msg_ref[...] = jnp.broadcast_to(stat_ref[...][None], msg_ref.shape)


def relay_kernel(recv_ref, msg_ref):
    msg_ref[...] = jnp.broadcast_to(jnp.sum(recv_ref[...], axis=0, keepdims=True), msg_ref.shape)


def embed_kernel(
    total_rows, pre_ref, recv_ref, gain_ref, bias_ref, w2_ref, unit_hbm, mean_hbm, inv_hbm, msg_hbm,
    hid_ref, unit_ref, mean_ref, inv_ref, bf_ref, sems,
):
    stats = jnp.sum(recv_ref[...], axis=0)
    half = stats.shape[0] // 2
    mean = stats[:half] / total_rows
    inv = lax.rsqrt(stats[half:] / total_rows - mean * mean + 1e-05)
    mean_ref[...] = mean
    inv_ref[...] = inv
    for j in range(half):
        normed = (pre_ref[:, lane(j)] - mean[j : j + 1]) * inv[j : j + 1]
        hid_ref[:, lane(j)] = jax.nn.gelu(normed * gain_ref[j : j + 1, :] + bias_ref[j : j + 1, :]).astype(BF)
    embed = jnp.dot(hid_ref[...], w2_ref[...], preferred_element_type=F32)
    scale = lax.rsqrt(jnp.sum(embed * embed, axis=1, keepdims=True) + 1e-06)
    unit = embed * scale
    bf_ref[...] = unit.astype(BF)
    width = unit.shape[1]
    unit_ref[:, :width] = unit
    unit_ref[:, width:] = jnp.broadcast_to(scale, (unit.shape[0], LANES))
    moves = [(bf_ref, msg_hbm.at[k]) for k in range(msg_hbm.shape[0])]
    moves += [(unit_ref, unit_hbm), (mean_ref, mean_hbm), (inv_ref, inv_hbm)]
    copies = [pltpu.make_async_copy(src, dst, sems.at[k]) for k, (src, dst) in enumerate(moves)]
    for copy in copies:
        copy.start()
    for copy in copies:
        copy.wait()


def proto_kernel(order_ref, raw_ref, w_hbm, proto_ref, proto_t_ref, raw_t_ref, norm_ref, slab_hbm, slab_ref, sem):
    slab = slab_ref.shape[1]
    at = pl.ds(pl.multiple_of(order_ref[0] * slab, slab), slab)
    fetch = pltpu.make_async_copy(w_hbm.at[:, at], slab_ref, sem)
    store = pltpu.make_async_copy(slab_ref, slab_hbm, sem)
    fetch.start()
    for k in range(raw_ref.shape[0] // TILE):
        span = slice(k * TILE, (k + 1) * TILE)
        raw_t = raw_ref[span, :].T
        raw_t_ref[:, span] = raw_t
        wide = raw_t.astype(F32)
        scale = lax.rsqrt(jnp.sum(wide * wide, axis=0, keepdims=True) + 1e-06)
        norm_ref[:, span] = jnp.broadcast_to(scale, (8, TILE))
        unit = (wide * scale).astype(BF)
        proto_t_ref[:, span] = unit
        proto_ref[span, :] = unit.T
        if k == 3:
            fetch.wait()
            store.start()
    store.wait()


def score_kernel(embed_ref, proto_t_hbm, kern_ref, msg_ref, soft_ref, acc_ref, proto_t_ref, sems):
    total, cols = kern_ref.shape
    copies = []
    for j in range(cols // TILE):
        span = slice(j * TILE, (j + 1) * TILE)
        copies.append(pltpu.make_async_copy(proto_t_hbm.at[:, span], proto_t_ref.at[:, span], sems.at[j]))
        copies[-1].start()
    acc_ref[...] = jnp.zeros_like(acc_ref)
    for step in range(total // TILE):
        band = slice(step * TILE, (step + 1) * TILE)
        soft = [None] * (TILE // LANES)
        for j in range(cols // TILE):
            span = slice(j * TILE, (j + 1) * TILE)
            if step == 0:
                copies[j].wait()
            scores = jnp.dot(embed_ref[band, :], proto_t_ref[:, span], preferred_element_type=F32)
            tempered = jnp.exp2(scores * (10.0 * LOG2_E))
            kern = tempered * tempered
            kern_ref[band, span] = kern.astype(BF)
            for h in range(TILE // LANES):
                at = (j * (TILE // LANES) + h) * 8
                acc_ref[at : at + 8, :] += fold_rows(kern[:, lane(h)])
            for b in range(TILE // LANES):
                part = tempered[b * LANES : (b + 1) * LANES]
                part = part[:, :LANES] + part[:, LANES:]
                soft[b] = part if soft[b] is None else soft[b] + part
        for b in range(TILE // LANES):
            at = step * (TILE // LANES) + b
            soft_ref[at : at + 1, :] = jnp.sum(soft[b].T, axis=0, keepdims=True)
    sums = jnp.sum(acc_ref[...].reshape(cols // LANES, 8, LANES), axis=1)
    msg_ref[...] = jnp.broadcast_to(sums[None], msg_ref.shape)


def row_kernel(recv_ref, kern_ref, *rest):
    soft_ref = rest[0] if len(rest) == 3 else None
    msg_ref, scale_ref = rest[-2:]
    step = pl.program_id(0)
    rows = kern_ref.shape[0]
    copies = msg_ref.shape[0]

    @pl.when(step == 0)
    def _():
        scale_ref[...] = 1.0 / jnp.sum(recv_ref[...], axis=0)
        if soft_ref is not None:
            half = soft_ref.shape[0]
            msg_ref[:, half:, :] = jnp.broadcast_to(soft_ref[...][None], (copies, half, LANES))

    for b in range(rows // LANES):
        acc = None
        for j in range(scale_ref.shape[0]):
            part = kern_ref[b * LANES : (b + 1) * LANES, lane(j)].astype(F32) * scale_ref[j : j + 1, :]
            acc = part if acc is None else acc + part
        row = jnp.sum(acc.T, axis=0, keepdims=True)
        msg_ref[:, pl.ds(step * (rows // LANES) + b, 1), :] = jnp.broadcast_to(row[None], (copies, 1, LANES))


def col_kernel(recv_ref, kern_ref, msg_ref, acc_ref, scale_ref):
    step = pl.program_id(0)
    rows, cols = kern_ref.shape

    @pl.when(step == 0)
    def _():
        acc_ref[...] = jnp.zeros_like(acc_ref)
        scale_ref[...] = 1.0 / jnp.sum(recv_ref[:, : scale_ref.shape[0], :], axis=0)

    for b in range(rows // LANES):
        scale = as_column(scale_ref[pl.ds(step * (rows // LANES) + b, 1), :])
        for j in range(cols // LANES):
            part = kern_ref[b * LANES : (b + 1) * LANES, lane(j)].astype(F32) * scale
            acc_ref[j * 8 : (j + 1) * 8, :] += fold_rows(part)

    @pl.when(step == pl.num_programs(0) - 1)
    def _():
        total = jnp.sum(acc_ref[...].reshape(cols // LANES, 8, LANES), axis=1)
        msg_ref[...] = jnp.broadcast_to(total[None], msg_ref.shape)


def final_kernel(
    order_ref, embed_ref, pair_ref, proto_t_ref, proto_ref, raw_t_ref, norm_ref, recv_col_ref, recv_row_ref, recv_soft_ref,
    d_unit_ref, piece0_ref, piece1_ref, piece2_ref, piece3_ref, loss_ref,
    grad_ref, mate_ref, loss_acc_ref, col_ref, row_ref, soft_ref, term_ref, both_ref,
):
    step = pl.program_id(0)
    rows = d_unit_ref.shape[0]
    cols = proto_t_ref.shape[1]
    bands = row_ref.shape[0]
    chunks = TILE // LANES

    @pl.when(step == 0)
    def _():
        loss_acc_ref[...] = jnp.zeros_like(loss_acc_ref)
        col_ref[...] = 10.0 / jnp.sum(recv_col_ref[...], axis=0)
        row_ref[...] = 1.0 / jnp.sum(recv_row_ref[:, :bands, :], axis=0)
        soft_ref[...] = jnp.sum(recv_soft_ref[:, bands:, :], axis=0)
        loss_acc_ref[8:16, :] = jnp.log(soft_ref[...])

    base = step * (rows // LANES)
    here = pl.ds(pl.multiple_of(step * rows, rows), rows)
    spot = lax.broadcasted_iota(jnp.int32, (LANES, LANES), 1)
    scales = []
    for b in range(rows // LANES):
        pair = as_column(pair_ref[pl.ds(base + b, 1), :]).astype(jnp.int32)
        found = jnp.zeros((LANES, LANES), F32)
        for q in range(bands):
            hot = spot + q * LANES == pair
            found += jnp.where(hot, row_ref[q : q + 1, :], 0.0)
            mate_ref[b * LANES : (b + 1) * LANES, lane(q)] = jnp.where(hot, 1.0, 0.0).astype(BF)
        scales.append(jnp.broadcast_to(jnp.sum(found, axis=1, keepdims=True), (LANES, LANES)))
    mate_scale = jnp.concatenate(scales, axis=0)
    both_ref[0:rows, :] = embed_ref[here, :]
    both_ref[rows:, :] = jnp.dot(mate_ref[...], embed_ref[...], preferred_element_type=F32).astype(BF)
    soft = jnp.concatenate([as_column(soft_ref[pl.ds(base + b, 1), :]) for b in range(rows // LANES)], axis=0)
    inv_soft = 10.0 / soft
    loss_acc = jnp.zeros((8, LANES), F32)
    for j in range(cols // TILE):
        span = slice(j * TILE, (j + 1) * TILE)
        both = jnp.dot(both_ref[...], proto_t_ref[:, span], preferred_element_type=F32)
        scores, mates = both[:rows], both[rows:]
        for h in range(chunks):
            at = j * chunks + h
            target = jnp.exp2(mates[:, lane(h)] * (20.0 * LOG2_E)) * mate_scale * col_ref[at : at + 1, :]
            score = scores[:, lane(h)]
            loss_acc += fold_rows(target * score)
            grad_ref[here, lane(at)] = (jnp.exp2(score * (10.0 * LOG2_E)) * inv_soft - target).astype(BF)
    d_unit_ref[...] = jnp.dot(grad_ref[here, :], proto_ref[...], preferred_element_type=F32).astype(BF)
    loss_acc_ref[0:8, :] += loss_acc

    @pl.when(step == pl.num_programs(0) - 1)
    def _():
        embed_t = embed_ref[...].T
        for j in range(cols // TILE):
            span = slice(j * TILE, (j + 1) * TILE)
            raw = raw_t_ref[:, span].astype(F32)
            scale = norm_ref[0:1, span]
            acc = jnp.dot(embed_t, grad_ref[:, span], preferred_element_type=F32)
            along = scale * scale * jnp.sum(raw * acc, axis=0, keepdims=True)
            term_ref[:, span] = ((acc - raw * along) * scale).astype(BF)
        pieces = (piece0_ref, piece1_ref, piece2_ref, piece3_ref)
        for d, piece in enumerate(pieces):
            height = piece.shape[0]
            at = pl.multiple_of(lax.rem(order_ref[9] + d, len(pieces)) * height, height)
            piece[...] = term_ref[pl.ds(at, height), :]
        loss_ref[...] = loss_acc_ref[...]


def d_embed_kernel(recv_hbm, unit_hbm, msg_ref, recv_ref, unit_ref, sems):
    copies = [pltpu.make_async_copy(recv_hbm, recv_ref, sems.at[0]), pltpu.make_async_copy(unit_hbm, unit_ref, sems.at[1])]
    for copy in copies:
        copy.start()
    for copy in copies:
        copy.wait()
    d_unit = jnp.sum(recv_ref[...].astype(F32), axis=0)
    width = d_unit.shape[1]
    unit = unit_ref[:, :width]
    d_embed = (d_unit - unit * jnp.sum(unit * d_unit, axis=1, keepdims=True)) * unit_ref[:, width : width + 1]
    msg_ref[...] = jnp.broadcast_to(d_embed.astype(BF)[None], msg_ref.shape)


def start_parts(parts, buf_ref, sems):
    copies = []
    at = 0
    for k, part in enumerate(parts):
        height = part.shape[0]
        copies.append(pltpu.make_async_copy(part, buf_ref.at[at : at + height], sems.at[k]))
        at += height
    for copy in copies:
        copy.start()
    return copies


def slab_kernel(order_ref, mean_hbm, inv_hbm, gain_hbm, bias_hbm, w_hbm, *rest):
    parts = rest[:-13]
    outs, bufs = rest[-13:-10], rest[-10:-7]
    mean_ref, inv_ref, gain_ref, bias_ref, buf_ref, w_ref, sems = rest[-7:]
    normed_ref, slope_ref, hid_ref = bufs
    rows, slab = normed_ref.shape
    w_copy = pltpu.make_async_copy(w_hbm, w_ref, sems.at[len(parts)])
    w_copy.start()
    copies = start_parts(parts, buf_ref, sems)
    stops = [sum(part.shape[0] for part in parts[: k + 1]) for k in range(len(parts))]
    moves = ((mean_hbm, mean_ref), (inv_hbm, inv_ref), (gain_hbm, gain_ref), (bias_hbm, bias_ref))
    base = sems.shape[0] - len(moves)
    stats = [pltpu.make_async_copy(src, dst, sems.at[base + k]) for k, (src, dst) in enumerate(moves)]
    for copy in stats:
        copy.start()
    w_copy.wait()
    for copy in stats:
        copy.wait()
    chunks = slab // LANES
    ones = jnp.ones((LANES, LANES), F32)
    done = 0
    sends = []
    for g in range(rows // TILE):
        start = g * TILE
        while done < len(parts) and (stops[done - 1] if done else 0) < start + TILE:
            copies[done].wait()
            done += 1
        pre = jnp.dot(buf_ref[start : start + TILE, :], w_ref[...], preferred_element_type=F32)
        for h in range(chunks):
            at = pl.ds(order_ref[0] * chunks + h, 1)
            mean, inv, gain, bias = mean_ref[at, :], inv_ref[at, :], gain_ref[at, :], bias_ref[at, :]
            for b in range(TILE // LANES):
                band = slice(start + b * LANES, start + (b + 1) * LANES)
                normed = (pre[b * LANES : (b + 1) * LANES, lane(h)] - mean) * inv
                hidden, back = jax.vjp(jax.nn.gelu, normed * gain + bias)
                normed_ref[band, lane(h)] = normed.astype(BF)
                slope_ref[band, lane(h)] = back(ones)[0].astype(BF)
                hid_ref[band, lane(h)] = hidden.astype(BF)
        span = slice(start, start + TILE)
        for k, (buf, out) in enumerate(zip(bufs, outs)):
            sends.append(
                pltpu.make_async_copy(buf.at[span], out.at[span], sems.at[len(parts) + 1 + g * len(outs) + k])
            )
            sends[-1].start()
    for send in sends:
        send.wait()


def shift_kernel(
    order_ref, d_embed_hbm, w2_hbm, normed_hbm, slope_hbm, hid_hbm, loss_hbm, shift_ref, msg_ref, sum_ref, loss_ref,
    normed_ref, slope_ref, hid_ref, d_embed_ref, w2_ref, sems,
):
    slab = w2_ref.shape[0]
    at = pl.ds(pl.multiple_of(order_ref[0] * slab, slab), slab)
    moves = ((d_embed_hbm, d_embed_ref), (w2_hbm.at[at], w2_ref))
    moves += ((slope_hbm, slope_ref), (normed_hbm, normed_ref), (hid_hbm, hid_ref), (loss_hbm, loss_ref))
    copies = [pltpu.make_async_copy(src, dst, sems.at[k]) for k, (src, dst) in enumerate(moves)]
    for copy in copies:
        copy.start()
    n_blocks, own, _ = d_embed_ref.shape
    sum_ref[...] = jnp.zeros_like(sum_ref)
    gains = biases = second = None
    for copy in copies:
        copy.wait()
    for k in range(0, n_blocks, 2):
        d_embed = jnp.concatenate([d_embed_ref[order_ref[k + 1]], d_embed_ref[order_ref[k + 2]]], axis=0)
        band = slice(k * own, (k + 2) * own)
        d_shift = tdot(d_embed, w2_ref[...], 1, 1) * slope_ref[band, :].astype(F32)
        shift_ref[band, :] = d_shift
        gain = jnp.sum(d_shift * normed_ref[band, :].astype(F32), axis=0, keepdims=True)
        bias = jnp.sum(d_shift, axis=0, keepdims=True)
        part = tdot(hid_ref[band, :], d_embed, 0, 0)
        gains = gain if gains is None else gains + gain
        biases = bias if biases is None else biases + bias
        second = part if second is None else second + part
    hits = jnp.sum(loss_ref[0:8, :], axis=0, keepdims=True)
    logs = jnp.sum(loss_ref[8:16, :], axis=0, keepdims=True)
    sum_ref[0:1, :] = gains
    sum_ref[1:2, :] = biases
    sum_ref[2:3, :] = jnp.concatenate([hits, logs], axis=1)
    n, _, slab = msg_ref.shape
    share = slab // n
    sums = sum_ref[...]
    high = sums.astype(BF)
    rest = sums - high.astype(F32)
    mid = rest.astype(BF)
    low = (rest - mid.astype(F32)).astype(BF)
    row = lax.broadcasted_iota(jnp.int32, sums.shape, 0)
    lower = jnp.where(row < 4, mid.astype(F32), pltpu.roll(low.astype(F32), 4, 0))
    packed = jnp.concatenate([high.astype(F32), lower], axis=0).astype(BF)
    msg_ref[:, :share, :] = jnp.broadcast_to(packed[None], (n, share, slab))
    msg_ref[:, share:, :] = second.astype(BF).reshape(n, share, slab)


def halves(v):
    high = v.astype(BF)
    return high, (v - high.astype(F32)).astype(BF)


def first_kernel(total_rows, order_ref, recv_ref, shift_ref, normed_ref, inv_ref, gain_ref, *rest):
    parts = rest[:-5]
    out_hbm, second_ref, d_pre_ref, out_ref, sems = rest[-5:]
    n, _, _ = out_ref.shape
    slab = d_pre_ref.shape[1]
    share = second_ref.shape[0]
    second_ref[...] = jnp.sum(recv_ref[:, share:, :].astype(F32), axis=0)
    got = jnp.sum(recv_ref[:, :share, :].astype(F32), axis=0)
    got = got[0:8] + (got[8:16] + pltpu.roll(got[8:16], 4, 0))
    chunks = slab // LANES
    for h in range(chunks):
        at = pl.ds(order_ref[0] * chunks + h, 1)
        factor = gain_ref[at, :] * inv_ref[at, :]
        gain_mean = got[0:1, lane(h)] / total_rows
        bias_mean = got[1:2, lane(h)] / total_rows
        for b in range(d_pre_ref.shape[0] // LANES):
            band = slice(b * LANES, (b + 1) * LANES)
            d_pre = factor * (shift_ref[band, lane(h)] - bias_mean - normed_ref[band, lane(h)].astype(F32) * gain_mean)
            d_pre_ref[band, lane(h)] = d_pre.astype(BF)
    high, low = halves(got[0:2])
    sums = [piece[k : k + 1, lane(h)] for k in range(2) for piece in (high, low) for h in range(chunks)]
    high, rest_of = got[2:3].astype(BF), got[2:3] - got[2:3].astype(BF).astype(F32)
    losses = [piece[:, lane(h)] for piece in (high,) + halves(rest_of) for h in range(chunks)]
    losses += [jnp.zeros((1, LANES), BF)] * (8 - len(losses))
    odd = lax.rem(order_ref[10], 2) == 1
    extra = jnp.where(
        odd,
        jnp.concatenate([v.astype(F32) for v in losses], axis=0),
        jnp.concatenate([v.astype(F32) for v in sums], axis=0),
    ).astype(BF)
    out_ref[:, chunks * share :, :] = jnp.broadcast_to(extra[None], (n, 8, LANES))
    group = TILE // share
    copies = []
    for j in range(n // group):
        tile = jnp.concatenate([part[:, j * TILE : (j + 1) * TILE] for part in parts], axis=0)
        grad = tdot(tile, d_pre_ref[...], 0, 0).astype(BF)
        span = slice(j * group, (j + 1) * group)
        for h in range(chunks):
            out_ref[span, h * share : (h + 1) * share, :] = grad[:, lane(h)].reshape(group, share, LANES)
        copies.append(pltpu.make_async_copy(out_ref.at[span], out_hbm.at[span], sems.at[j]))
        copies[-1].start()
    for copy in copies:
        copy.wait()


def tail_kernel(total_rows, recv_ref, out_ref, gain_ref, bias_ref, loss_ref):
    n_batch, n_proto, height, _ = recv_ref.shape
    share = out_ref.shape[0]
    chunks = height // share
    lines = jnp.zeros((8, LANES), F32)
    for p in range(n_proto):
        acc = recv_ref[0, p].astype(F32)
        for b in range(1, n_batch):
            acc += recv_ref[b, p].astype(F32)
        for h in range(chunks):
            at = (p * chunks + h) * LANES
            out_ref[:, at : at + LANES] = acc[h * share : (h + 1) * share, :]
        sums = recv_ref[0, p, chunks * share :, :].astype(F32)
        for h in range(chunks):
            at = p * chunks + h
            gain_ref[at : at + 1, :] = sums[h : h + 1] + sums[chunks + h : chunks + h + 1]
            bias_ref[at : at + 1, :] = sums[2 * chunks + h : 2 * chunks + h + 1] + sums[3 * chunks + h : 3 * chunks + h + 1]
        lines += recv_ref[1, p, chunks * share :, :].astype(F32)
    hits = lines[0:1] + (lines[2:3] + lines[4:5])
    logs = (lines[1:2] + (lines[3:4] + lines[5:6])) / n_proto
    loss = jnp.sum(logs - hits, axis=1, keepdims=True) / total_rows
    loss_ref[...] = jnp.broadcast_to(loss, loss_ref.shape)


def stage_kernel(order_ref, in0_ref, in1_ref, in2_ref, in3_ref, out0_ref, out1_ref, out2_ref, out3_ref, sum_ref):
    near = in0_ref[...].astype(F32) + in1_ref[...].astype(F32)
    sum_ref[...] = (near + (in2_ref[...].astype(F32) + in3_ref[...].astype(F32))).astype(BF)
    outs = (out0_ref, out1_ref, out2_ref, out3_ref)
    for d, out in enumerate(outs):
        height = out.shape[0]
        at = pl.multiple_of(lax.rem(order_ref[10] + d, len(outs)) * height, height)
        out[...] = sum_ref[pl.ds(at, height), :]


def shape(dims, kind=F32):
    return jax.ShapeDtypeStruct(dims, kind)


def far_shape(dims, kind=F32):
    return pltpu.HBM(dims, kind)


def far(x):
    return pltpu.with_memory_space_constraint(x, pltpu.HBM)


def step_of_device(features, w_first, bn_gain, bn_bias, w_second, prototypes, pair):
    n_batch = lax.axis_size("batch")
    n_proto = lax.axis_size("proto")
    own, d_in = features.shape
    d_hid, width = w_second.shape
    cols = prototypes.shape[0]
    total_rows = own * n_batch * n_proto
    rows = own * n_proto
    part = lax.axis_index("proto")
    slab = d_hid // n_proto
    col_bands = cols // LANES
    row_bands = rows // LANES
    hid_bands = d_hid // LANES
    steps = rows // TILE
    gain = bn_gain.reshape(hid_bands, LANES)
    bias = bn_bias.reshape(hid_bands, LANES)

    def hop(x, moves):
        return lax.ppermute(x, "proto", moves)

    ring = n_proto // 2
    right = [(i * 2 + c, (i + 1) % ring * 2 + c) for i in range(ring) for c in range(2)]
    left = [(t, s) for s, t in right]
    swap = [(i, i ^ 1) for i in range(n_proto)]
    from_left = hop(features, right)
    from_right = hop(features, left)
    across = lax.shift_right_logical(part, 1)
    place = lax.axis_index("batch")
    side = 4
    order = jnp.stack(
        [part]
        + [
            (lax.bitwise_and(across + d, ring - 1) * 2 + lax.bitwise_and(part, 1)) ^ o
            for o in range(2)
            for d in (0, 1, 3, 2)
        ]
        + [lax.shift_right_logical(place, 2), lax.bitwise_and(place, side - 1)]
    ).astype(jnp.int32)
    mate_row = (pair - place * rows).astype(F32).reshape(row_bands, LANES)

    anywhere = pl.BlockSpec(memory_space=pl.ANY)
    pre, msg = pl.pallas_call(
        pre_kernel,
        in_specs=[pl.BlockSpec(features.shape, lambda: (0, 0)), anywhere],
        out_shape=[shape((own, d_hid)), shape((n_batch, 2 * hid_bands, LANES))],
        scratch_shapes=[
            pltpu.VMEM((2 * hid_bands, LANES), F32),
            pltpu.VMEM((4, d_in // 4, d_hid), BF),
            pltpu.SemaphoreType.DMA((4,)),
        ],
        name="pre_kernel",
    )(features, w_first)
    near_left, near_right, _ = lax.optimization_barrier((from_left, from_right, pre))
    far_top = hop(near_left[: own // 2], right)
    far_low = hop(near_right[own // 2 :], left)
    got = deal(msg, "batch")
    got, mate_row, order = lax.optimization_barrier((got, mate_row, order))
    msg = pl.pallas_call(
        relay_kernel, out_shape=shape((n_proto, 2 * hid_bands, LANES)), compiler_params=PARAMS, name="relay_kernel"
    )(got)
    got = deal(msg, "proto")
    unit_embed, mean, inv, msg = pl.pallas_call(
        lambda *refs: embed_kernel(total_rows, *refs),
        out_specs=[pl.BlockSpec(memory_space=pltpu.HBM)] * 4,
        out_shape=[
            far_shape((own, width + LANES)),
            far_shape((hid_bands, LANES)),
            far_shape((hid_bands, LANES)),
            far_shape((n_proto, own, width), BF),
        ],
        scratch_shapes=[
            pltpu.VMEM((own, d_hid), BF),
            pltpu.VMEM((own, width + LANES), F32),
            pltpu.VMEM((hid_bands, LANES), F32),
            pltpu.VMEM((hid_bands, LANES), F32),
            pltpu.VMEM((own, width), BF),
            pltpu.SemaphoreType.DMA((n_proto + 3,)),
        ],
        compiler_params=PARAMS,
        name="embed_kernel",
    )(pre, got, gain, bias, w_second)
    raw, *mine, _ = lax.optimization_barrier((prototypes, features, from_right, from_left, far_top, far_low, msg))
    parts = mine + [hop(piece, swap) for piece in mine]
    proto_bf, proto_t, raw_t, norm, w_slab = pl.pallas_call(
        proto_kernel,
        in_specs=[pl.BlockSpec(memory_space=pltpu.SMEM), pl.BlockSpec((cols, width), lambda: (0, 0)), anywhere],
        out_specs=[
            pl.BlockSpec((cols, width), lambda: (0, 0)),
            pl.BlockSpec((width, cols), lambda: (0, 0)),
            pl.BlockSpec((width, cols), lambda: (0, 0)),
            pl.BlockSpec((8, cols), lambda: (0, 0)),
            anywhere,
        ],
        out_shape=[
            shape((cols, width), BF),
            shape((width, cols), BF),
            shape((width, cols), BF),
            shape((8, cols)),
            far_shape((d_in, slab), BF),
        ],
        scratch_shapes=[pltpu.VMEM((d_in, slab), BF), pltpu.SemaphoreType.DMA],
        name="proto_kernel",
    )(order, raw, w_first)
    block_embed, proto_bf, proto_t, raw_t, norm, w_slab, *parts = lax.optimization_barrier(
        (deal(msg, "proto"), proto_bf, proto_t, raw_t, norm, w_slab, *parts)
    )
    block_embed = block_embed.reshape(rows, width)

    kern, col_msg, soft = pl.pallas_call(
        score_kernel,
        in_specs=[pl.BlockSpec((rows, width), lambda: (0, 0)), anywhere],
        out_shape=[shape((rows, cols), BF), shape((n_batch, col_bands, LANES)), shape((row_bands, LANES))],
        scratch_shapes=[
            pltpu.VMEM((col_bands * 8, LANES), F32),
            pltpu.VMEM((width, cols), BF),
            pltpu.SemaphoreType.DMA((cols // TILE,)),
        ],
        compiler_params=PARAMS,
        name="score_kernel",
    )(block_embed, far(proto_t))

    def row_pass(recv, extra):
        height = row_bands * (2 if extra else 1)
        return pl.pallas_call(
            row_kernel,
            grid=(steps,),
            in_specs=[whole((n_batch, col_bands, LANES)), rows_of(TILE, cols)]
            + [whole((row_bands, LANES)) for _ in extra],
            out_specs=whole((n_proto, height, LANES)),
            out_shape=shape((n_proto, height, LANES)),
            scratch_shapes=[pltpu.VMEM((col_bands, LANES), F32)],
            compiler_params=PARAMS,
        name="row_kernel",
        )(recv, kern, *extra)

    def col_pass(recv):
        return pl.pallas_call(
            col_kernel,
            grid=(steps,),
            in_specs=[whole(recv.shape), rows_of(TILE, cols)],
            out_specs=whole((n_batch, col_bands, LANES)),
            out_shape=shape((n_batch, col_bands, LANES)),
            scratch_shapes=[pltpu.VMEM((col_bands * 8, LANES), F32), pltpu.VMEM((row_bands, LANES), F32)],
            compiler_params=PARAMS,
        name="col_kernel",
        )(recv, kern)

    recv_soft = None
    for step in range(ITERS):
        recv_col = deal(col_msg, "batch")
        recv_row = deal(row_pass(recv_col, () if step else (soft,)), "proto")
        recv_soft = recv_row if recv_soft is None else recv_soft
        if step + 1 < ITERS:
            col_msg = col_pass(recv_row)

    d_unit, *pieces, loss_tile = pl.pallas_call(
        final_kernel,
        grid=(steps // 2,),
        in_specs=[
            pl.BlockSpec(memory_space=pltpu.SMEM),
            whole((rows, width)),
            whole((row_bands, LANES)),
            whole((width, cols)),
            whole((cols, width)),
            whole((width, cols)),
            whole((8, cols)),
            whole(recv_col.shape),
            whole(recv_row.shape),
            whole(recv_soft.shape),
        ],
        out_specs=[rows_of(2 * TILE, width)] + [whole((width // side, cols))] * side + [whole((16, LANES))],
        out_shape=[far_shape((rows, width), BF)]
        + [far_shape((width // side, cols), BF)] * side
        + [far_shape((16, LANES))],
        scratch_shapes=[
            pltpu.VMEM((rows, cols), BF),
            pltpu.VMEM((2 * TILE, rows), BF),
            pltpu.VMEM((16, LANES), F32),
            pltpu.VMEM((col_bands, LANES), F32),
            pltpu.VMEM((row_bands, LANES), F32),
            pltpu.VMEM((row_bands, LANES), F32),
            pltpu.VMEM((width, cols), BF),
            pltpu.VMEM((4 * TILE, width), BF),
        ],
        compiler_params=PARAMS,
        name="final_kernel",
    )(order, block_embed, mate_row, proto_t, proto_bf, raw_t, norm, recv_col, recv_row, recv_soft)


    def shifted(axis, d):
        moves = []
        for b in range(n_batch):
            y, z = divmod(b, side)
            moves.append((b, (y + d) % side * side + z if axis == 0 else y * side + (z + d) % side))
        return moves

    pieces = [pieces[0]] + [lax.ppermute(pieces[d], "batch", shifted(0, d)) for d in range(1, side)]
    d_unit_got = deal(d_unit.reshape(n_proto, own, width), "proto")
    stat_spec = whole((hid_bands, LANES))
    mean_late, inv, _ = lax.optimization_barrier((mean, inv, d_unit))
    normed, slope, hid = pl.pallas_call(
        slab_kernel,
        grid_spec=pltpu.PrefetchScalarGridSpec(
            num_scalar_prefetch=1,
            grid=(1,),
            in_specs=[anywhere] * (5 + len(parts)),
            out_specs=[pl.BlockSpec(memory_space=pltpu.HBM)] * 3,
            scratch_shapes=[pltpu.VMEM((rows, slab), BF)] * 3
            + [pltpu.VMEM((hid_bands, LANES), F32)] * 4
            + [
                pltpu.VMEM((rows, d_in), BF),
                pltpu.VMEM((d_in, slab), BF),
                pltpu.SemaphoreType.DMA((len(parts) + 5 + 3 * (rows // TILE),)),
            ],
        ),
        out_shape=[shape((rows, slab), BF)] * 3,
        name="slab_kernel",
    )(order, mean_late, inv, gain, bias, w_slab, *parts)
    d_unit, normed, slope, hid = lax.optimization_barrier((d_unit_got, normed, slope, hid))
    d_embed = pl.pallas_call(
        d_embed_kernel,
        in_specs=[anywhere] * 2,
        out_shape=far_shape((n_proto, own, width), BF),
        scratch_shapes=[
            pltpu.VMEM((n_proto, own, width), BF),
            pltpu.VMEM((own, width + LANES), F32),
            pltpu.SemaphoreType.DMA((2,)),
        ],
        name="d_embed_kernel",
    )(far(d_unit), far(unit_embed))
    pieces[0], _ = lax.optimization_barrier((pieces[0], d_embed))
    pieces = pl.pallas_call(
        stage_kernel,
        in_specs=[pl.BlockSpec(memory_space=pltpu.SMEM)] + [pl.BlockSpec((width // side, cols), lambda: (0, 0))] * side,
        out_shape=[shape((width // n_batch, cols), BF)] * side,
        scratch_shapes=[pltpu.VMEM((width // side, cols), BF)],
        name="stage_kernel",
    )(order, *pieces)
    pieces = [pieces[0]] + [lax.ppermute(pieces[d], "batch", shifted(1, d)) for d in range(1, side)]
    d_embed = deal(d_embed, "proto")

    shift, msg = pl.pallas_call(
        shift_kernel,
        grid_spec=pltpu.PrefetchScalarGridSpec(
            num_scalar_prefetch=1,
            grid=(1,),
            in_specs=[
                anywhere,
                anywhere,
                anywhere,
                anywhere,
                anywhere,
                anywhere,
            ],
            out_specs=[whole((rows, slab)), whole((n_batch, 2 * slab // n_batch, width))],
            scratch_shapes=[pltpu.VMEM((8, slab), F32), pltpu.VMEM((16, LANES), F32)]
            + [pltpu.VMEM((rows, slab), BF)] * 3
            + [pltpu.VMEM((n_proto, own, width), BF), pltpu.VMEM((slab, width), BF), pltpu.SemaphoreType.DMA((6,))],
        ),
        out_shape=[shape((rows, slab)), shape((n_batch, 2 * slab // n_batch, width), BF)],
        compiler_params=PARAMS,
        name="shift_kernel",
    )(order, far(d_embed), far(w_second), far(normed), far(slope), far(hid), far(loss_tile))
    recv = deal(msg, "batch")

    share = d_in // (n_batch * n_proto)
    lines = slab // LANES * share + 8
    first, second = pl.pallas_call(
        lambda *refs: first_kernel(total_rows, *refs),
        grid_spec=pltpu.PrefetchScalarGridSpec(
            num_scalar_prefetch=1,
            grid=(1,),
            in_specs=[whole(recv.shape), whole((rows, slab)), whole((rows, slab)), stat_spec, stat_spec]
            + [whole(piece.shape) for piece in parts],
            out_specs=[pl.BlockSpec(memory_space=pltpu.HBM), whole((slab // n_batch, width))],
            scratch_shapes=[
                pltpu.VMEM((rows, slab), BF),
                pltpu.VMEM((n_batch * n_proto, lines, LANES), BF),
                pltpu.SemaphoreType.DMA((d_in // TILE,)),
            ],
        ),
        out_shape=[far_shape((n_batch * n_proto, lines, LANES), BF), shape((slab // n_batch, width))],
        compiler_params=PARAMS,
        name="first_kernel",
    )(order, recv, shift, normed, inv, gain, *parts)

    first, *pieces = lax.optimization_barrier((first, *pieces))
    grad_proto = sum(piece.astype(F32) for piece in pieces).T
    first = deal(first, ("batch", "proto")).reshape(n_batch, n_proto, lines, LANES)
    grad_first, grad_gain, grad_bias, loss = pl.pallas_call(
        lambda *refs: tail_kernel(total_rows, *refs),
        out_shape=[shape((share, d_hid)), shape((hid_bands, LANES)), shape((hid_bands, LANES)), shape((1, LANES))],
        compiler_params=PARAMS,
        name="tail_kernel",
    )(first)
    grad_second = lax.ppermute(
        second,
        ("batch", "proto"),
        [(b * n_proto + p, p * n_batch + b) for b in range(n_batch) for p in range(n_proto)],
    )
    grad_gain = grad_gain.reshape(-1)
    grad_bias = grad_bias.reshape(-1)
    loss = loss[0, 0]
    return (grad_first, grad_second, grad_gain, grad_bias, grad_proto, loss)


def solution(mesh):
    return jax.shard_map(
        step_of_device,
        mesh=mesh,
        in_specs=(P(("batch", "proto"), None), P(), P(), P(), P(), P("proto", None), P("batch")),
        out_specs=(
            P(("batch", "proto"), None),
            P(("batch", "proto"), None),
            P(),
            P(),
            P("proto", "batch"),
            P(),
        ),
        check_vma=False,
    )
```

```python
import jax
import jax.numpy as jnp
from jax import lax
from jax.experimental import pallas as pl
from jax.experimental.pallas import tpu as pltpu
from jax.sharding import PartitionSpec as P


ITERS = 3
BF = jnp.bfloat16
F32 = jnp.float32
LANES = 128
TILE = 256
LOG2_E = 1.4426950408889634
PARAMS = pltpu.CompilerParams(vmem_limit_bytes=24 * 1024 * 1024)


def deal(x, axis):
    return lax.all_to_all(x, axis, 0, 0, tiled=True)


def tdot(a, b, a_dim, b_dim):
    return lax.dot_general(a, b, (((a_dim,), (b_dim,)), ((), ())), preferred_element_type=F32)


def fold_rows(v):
    return jnp.sum(v.reshape(v.shape[0] // 8, 8, LANES), axis=0)


def as_column(row):
    return jnp.broadcast_to(row, (LANES, LANES)).T


def lane(j):
    return slice(j * LANES, (j + 1) * LANES)


def whole(shape):
    return pl.BlockSpec(shape, lambda i, *_: (0,) * len(shape))


def rows_of(rows, width):
    return pl.BlockSpec((rows, width), lambda i, *_: (i, 0))


def pre_kernel(features_ref, w_hbm, pre_ref, msg_ref, stat_ref, w_buf, sems):
    pieces, depth, width = w_buf.shape
    copies = [
        pltpu.make_async_copy(w_hbm.at[k * depth : (k + 1) * depth], w_buf.at[k], sems.at[k]) for k in range(pieces)
    ]
    for copy in copies:
        copy.start()
    half = stat_ref.shape[0] // 2
    for k in range(pieces):
        copies[k].wait()
        for j in range(width // TILE):
            span = slice(j * TILE, (j + 1) * TILE)
            part = jnp.dot(features_ref[:, k * depth : (k + 1) * depth], w_buf[k, :, span], preferred_element_type=F32)
            pre = part if k == 0 else pre_ref[:, span] + part
            pre_ref[:, span] = pre
            if k == pieces - 1:
                for h in range(TILE // LANES):
                    at = j * (TILE // LANES) + h
                    piece = pre[:, lane(h)]
                    stat_ref[at : at + 1, :] = jnp.sum(piece, axis=0, keepdims=True)
                    stat_ref[half + at : half + at + 1, :] = jnp.sum(piece * piece, axis=0, keepdims=True)
    msg_ref[...] = jnp.broadcast_to(stat_ref[...][None], msg_ref.shape)


def relay_kernel(recv_ref, msg_ref):
    msg_ref[...] = jnp.broadcast_to(jnp.sum(recv_ref[...], axis=0, keepdims=True), msg_ref.shape)


def embed_kernel(
    total_rows, pre_ref, recv_ref, gain_ref, bias_ref, w2_ref, unit_hbm, mean_hbm, inv_hbm, msg_hbm,
    hid_ref, unit_ref, mean_ref, inv_ref, bf_ref, sems,
):
    stats = jnp.sum(recv_ref[...], axis=0)
    half = stats.shape[0] // 2
    mean = stats[:half] / total_rows
    inv = lax.rsqrt(stats[half:] / total_rows - mean * mean + 1e-05)
    mean_ref[...] = mean
    inv_ref[...] = inv
    for j in range(half):
        normed = (pre_ref[:, lane(j)] - mean[j : j + 1]) * inv[j : j + 1]
        hid_ref[:, lane(j)] = jax.nn.gelu(normed * gain_ref[j : j + 1, :] + bias_ref[j : j + 1, :]).astype(BF)
    embed = jnp.dot(hid_ref[...], w2_ref[...], preferred_element_type=F32)
    scale = lax.rsqrt(jnp.sum(embed * embed, axis=1, keepdims=True) + 1e-06)
    unit = embed * scale
    bf_ref[...] = unit.astype(BF)
    width = unit.shape[1]
    unit_ref[:, :width] = unit
    unit_ref[:, width:] = jnp.broadcast_to(scale, (unit.shape[0], LANES))
    moves = [(bf_ref, msg_hbm.at[k]) for k in range(msg_hbm.shape[0])]
    moves += [(unit_ref, unit_hbm), (mean_ref, mean_hbm), (inv_ref, inv_hbm)]
    copies = [pltpu.make_async_copy(src, dst, sems.at[k]) for k, (src, dst) in enumerate(moves)]
    for copy in copies:
        copy.start()
    for copy in copies:
        copy.wait()


def proto_kernel(order_ref, raw_ref, w_hbm, proto_ref, proto_t_ref, raw_t_ref, norm_ref, slab_hbm, slab_ref, sem):
    slab = slab_ref.shape[1]
    at = pl.ds(pl.multiple_of(order_ref[0] * slab, slab), slab)
    fetch = pltpu.make_async_copy(w_hbm.at[:, at], slab_ref, sem)
    store = pltpu.make_async_copy(slab_ref, slab_hbm, sem)
    fetch.start()
    for k in range(raw_ref.shape[0] // TILE):
        span = slice(k * TILE, (k + 1) * TILE)
        raw_t = raw_ref[span, :].T
        raw_t_ref[:, span] = raw_t
        wide = raw_t.astype(F32)
        scale = lax.rsqrt(jnp.sum(wide * wide, axis=0, keepdims=True) + 1e-06)
        norm_ref[:, span] = jnp.broadcast_to(scale, (8, TILE))
        unit = (wide * scale).astype(BF)
        proto_t_ref[:, span] = unit
        proto_ref[span, :] = unit.T
        if k == 3:
            fetch.wait()
            store.start()
    store.wait()


def score_kernel(embed_ref, proto_t_hbm, kern_ref, msg_ref, soft_ref, acc_ref, proto_t_ref, sems):
    step = pl.program_id(0)
    rows = embed_ref.shape[0]
    cols = proto_t_ref.shape[1]

    def copy(j):
        span = slice(j * TILE, (j + 1) * TILE)
        return pltpu.make_async_copy(proto_t_hbm.at[:, span], proto_t_ref.at[:, span], sems.at[j])

    @pl.when(step == 0)
    def _():
        for j in range(cols // TILE):
            copy(j).start()
        acc_ref[...] = jnp.zeros_like(acc_ref)
        for j in range(cols // TILE):
            copy(j).wait()

    soft = [None] * (rows // LANES)
    for j in range(cols // TILE):
        span = slice(j * TILE, (j + 1) * TILE)
        scores = jnp.dot(embed_ref[...], proto_t_ref[:, span], preferred_element_type=F32)
        tempered = jnp.exp2(scores * (10.0 * LOG2_E))
        kern = tempered * tempered
        kern_ref[:, span] = kern.astype(BF)
        for h in range(TILE // LANES):
            at = (j * (TILE // LANES) + h) * 8
            acc_ref[at : at + 8, :] += fold_rows(kern[:, lane(h)])
        for b in range(rows // LANES):
            part = tempered[b * LANES : (b + 1) * LANES]
            part = part[:, :LANES] + part[:, LANES:]
            soft[b] = part if soft[b] is None else soft[b] + part
    for b in range(rows // LANES):
        soft_ref[pl.ds(step * (rows // LANES) + b, 1), :] = jnp.sum(soft[b].T, axis=0, keepdims=True)

    @pl.when(step == pl.num_programs(0) - 1)
    def _():
        total = jnp.sum(acc_ref[...].reshape(cols // LANES, 8, LANES), axis=1)
        msg_ref[...] = jnp.broadcast_to(total[None], msg_ref.shape)


def row_kernel(recv_ref, kern_ref, *rest):
    soft_ref = rest[0] if len(rest) == 3 else None
    msg_ref, scale_ref = rest[-2:]
    step = pl.program_id(0)
    rows = kern_ref.shape[0]
    copies = msg_ref.shape[0]

    @pl.when(step == 0)
    def _():
        scale_ref[...] = 1.0 / jnp.sum(recv_ref[...], axis=0)
        if soft_ref is not None:
            half = soft_ref.shape[0]
            msg_ref[:, half:, :] = jnp.broadcast_to(soft_ref[...][None], (copies, half, LANES))

    for b in range(rows // LANES):
        acc = None
        for j in range(scale_ref.shape[0]):
            part = kern_ref[b * LANES : (b + 1) * LANES, lane(j)].astype(F32) * scale_ref[j : j + 1, :]
            acc = part if acc is None else acc + part
        row = jnp.sum(acc.T, axis=0, keepdims=True)
        msg_ref[:, pl.ds(step * (rows // LANES) + b, 1), :] = jnp.broadcast_to(row[None], (copies, 1, LANES))


def col_kernel(recv_ref, kern_ref, msg_ref, acc_ref, scale_ref):
    step = pl.program_id(0)
    rows, cols = kern_ref.shape

    @pl.when(step == 0)
    def _():
        acc_ref[...] = jnp.zeros_like(acc_ref)
        scale_ref[...] = 1.0 / jnp.sum(recv_ref[:, : scale_ref.shape[0], :], axis=0)

    for b in range(rows // LANES):
        scale = as_column(scale_ref[pl.ds(step * (rows // LANES) + b, 1), :])
        for j in range(cols // LANES):
            part = kern_ref[b * LANES : (b + 1) * LANES, lane(j)].astype(F32) * scale
            acc_ref[j * 8 : (j + 1) * 8, :] += fold_rows(part)

    @pl.when(step == pl.num_programs(0) - 1)
    def _():
        total = jnp.sum(acc_ref[...].reshape(cols // LANES, 8, LANES), axis=1)
        msg_ref[...] = jnp.broadcast_to(total[None], msg_ref.shape)


def final_kernel(
    order_ref, embed_ref, pair_ref, proto_t_ref, proto_ref, raw_t_ref, norm_ref, recv_col_ref, recv_row_ref, recv_soft_ref,
    d_unit_ref, piece0_ref, piece1_ref, piece2_ref, piece3_ref, loss_ref,
    grad_ref, mate_ref, loss_acc_ref, col_ref, row_ref, soft_ref, term_ref, both_ref,
):
    step = pl.program_id(0)
    rows = d_unit_ref.shape[0]
    cols = proto_t_ref.shape[1]
    bands = row_ref.shape[0]
    chunks = TILE // LANES

    @pl.when(step == 0)
    def _():
        loss_acc_ref[...] = jnp.zeros_like(loss_acc_ref)
        col_ref[...] = 10.0 / jnp.sum(recv_col_ref[...], axis=0)
        row_ref[...] = 1.0 / jnp.sum(recv_row_ref[:, :bands, :], axis=0)
        soft_ref[...] = jnp.sum(recv_soft_ref[:, bands:, :], axis=0)
        loss_acc_ref[8:16, :] = jnp.log(soft_ref[...])

    base = step * (rows // LANES)
    here = pl.ds(pl.multiple_of(step * rows, rows), rows)
    spot = lax.broadcasted_iota(jnp.int32, (LANES, LANES), 1)
    scales = []
    for b in range(rows // LANES):
        pair = as_column(pair_ref[pl.ds(base + b, 1), :]).astype(jnp.int32)
        found = jnp.zeros((LANES, LANES), F32)
        for q in range(bands):
            hot = spot + q * LANES == pair
            found += jnp.where(hot, row_ref[q : q + 1, :], 0.0)
            mate_ref[b * LANES : (b + 1) * LANES, lane(q)] = jnp.where(hot, 1.0, 0.0).astype(BF)
        scales.append(jnp.broadcast_to(jnp.sum(found, axis=1, keepdims=True), (LANES, LANES)))
    mate_scale = jnp.concatenate(scales, axis=0)
    both_ref[0:rows, :] = embed_ref[here, :]
    both_ref[rows:, :] = jnp.dot(mate_ref[...], embed_ref[...], preferred_element_type=F32).astype(BF)
    soft = jnp.concatenate([as_column(soft_ref[pl.ds(base + b, 1), :]) for b in range(rows // LANES)], axis=0)
    inv_soft = 10.0 / soft
    loss_acc = jnp.zeros((8, LANES), F32)
    for j in range(cols // TILE):
        span = slice(j * TILE, (j + 1) * TILE)
        both = jnp.dot(both_ref[...], proto_t_ref[:, span], preferred_element_type=F32)
        scores, mates = both[:rows], both[rows:]
        for h in range(chunks):
            at = j * chunks + h
            target = jnp.exp2(mates[:, lane(h)] * (20.0 * LOG2_E)) * mate_scale * col_ref[at : at + 1, :]
            score = scores[:, lane(h)]
            loss_acc += fold_rows(target * score)
            grad_ref[here, lane(at)] = (jnp.exp2(score * (10.0 * LOG2_E)) * inv_soft - target).astype(BF)
    d_unit_ref[...] = jnp.dot(grad_ref[here, :], proto_ref[...], preferred_element_type=F32).astype(BF)
    loss_acc_ref[0:8, :] += loss_acc

    @pl.when(step == pl.num_programs(0) - 1)
    def _():
        embed_t = embed_ref[...].T
        for j in range(cols // TILE):
            span = slice(j * TILE, (j + 1) * TILE)
            raw = raw_t_ref[:, span].astype(F32)
            scale = norm_ref[0:1, span]
            acc = jnp.dot(embed_t, grad_ref[:, span], preferred_element_type=F32)
            along = scale * scale * jnp.sum(raw * acc, axis=0, keepdims=True)
            term_ref[:, span] = ((acc - raw * along) * scale).astype(BF)
        pieces = (piece0_ref, piece1_ref, piece2_ref, piece3_ref)
        for d, piece in enumerate(pieces):
            height = piece.shape[0]
            at = pl.multiple_of(lax.rem(order_ref[9] + d, len(pieces)) * height, height)
            piece[...] = term_ref[pl.ds(at, height), :]
        loss_ref[...] = loss_acc_ref[...]


def d_embed_kernel(recv_hbm, unit_hbm, msg_ref, recv_ref, unit_ref, sems):
    copies = [pltpu.make_async_copy(recv_hbm, recv_ref, sems.at[0]), pltpu.make_async_copy(unit_hbm, unit_ref, sems.at[1])]
    for copy in copies:
        copy.start()
    for copy in copies:
        copy.wait()
    d_unit = jnp.sum(recv_ref[...].astype(F32), axis=0)
    width = d_unit.shape[1]
    unit = unit_ref[:, :width]
    d_embed = (d_unit - unit * jnp.sum(unit * d_unit, axis=1, keepdims=True)) * unit_ref[:, width : width + 1]
    msg_ref[...] = jnp.broadcast_to(d_embed.astype(BF)[None], msg_ref.shape)


def start_parts(parts, buf_ref, sems):
    copies = []
    at = 0
    for k, part in enumerate(parts):
        height = part.shape[0]
        copies.append(pltpu.make_async_copy(part, buf_ref.at[at : at + height], sems.at[k]))
        at += height
    for copy in copies:
        copy.start()
    return copies


def slab_kernel(order_ref, mean_hbm, inv_hbm, gain_hbm, bias_hbm, w_hbm, *rest):
    parts = rest[:-13]
    outs, bufs = rest[-13:-10], rest[-10:-7]
    mean_ref, inv_ref, gain_ref, bias_ref, buf_ref, w_ref, sems = rest[-7:]
    normed_ref, slope_ref, hid_ref = bufs
    rows, slab = normed_ref.shape
    w_copy = pltpu.make_async_copy(w_hbm, w_ref, sems.at[len(parts)])
    w_copy.start()
    copies = start_parts(parts, buf_ref, sems)
    stops = [sum(part.shape[0] for part in parts[: k + 1]) for k in range(len(parts))]
    moves = ((mean_hbm, mean_ref), (inv_hbm, inv_ref), (gain_hbm, gain_ref), (bias_hbm, bias_ref))
    base = sems.shape[0] - len(moves)
    stats = [pltpu.make_async_copy(src, dst, sems.at[base + k]) for k, (src, dst) in enumerate(moves)]
    for copy in stats:
        copy.start()
    w_copy.wait()
    for copy in stats:
        copy.wait()
    chunks = slab // LANES
    ones = jnp.ones((LANES, LANES), F32)
    done = 0
    sends = []
    for g in range(rows // TILE):
        start = g * TILE
        while done < len(parts) and (stops[done - 1] if done else 0) < start + TILE:
            copies[done].wait()
            done += 1
        pre = jnp.dot(buf_ref[start : start + TILE, :], w_ref[...], preferred_element_type=F32)
        for h in range(chunks):
            at = pl.ds(order_ref[0] * chunks + h, 1)
            mean, inv, gain, bias = mean_ref[at, :], inv_ref[at, :], gain_ref[at, :], bias_ref[at, :]
            for b in range(TILE // LANES):
                band = slice(start + b * LANES, start + (b + 1) * LANES)
                normed = (pre[b * LANES : (b + 1) * LANES, lane(h)] - mean) * inv
                hidden, back = jax.vjp(jax.nn.gelu, normed * gain + bias)
                normed_ref[band, lane(h)] = normed.astype(BF)
                slope_ref[band, lane(h)] = back(ones)[0].astype(BF)
                hid_ref[band, lane(h)] = hidden.astype(BF)
        span = slice(start, start + TILE)
        for k, (buf, out) in enumerate(zip(bufs, outs)):
            sends.append(
                pltpu.make_async_copy(buf.at[span], out.at[span], sems.at[len(parts) + 1 + g * len(outs) + k])
            )
            sends[-1].start()
    for send in sends:
        send.wait()


def shift_kernel(
    order_ref, d_embed_hbm, w2_hbm, normed_hbm, slope_hbm, hid_hbm, loss_hbm, shift_ref, msg_ref, sum_ref, loss_ref,
    normed_ref, slope_ref, hid_ref, d_embed_ref, w2_ref, sems,
):
    slab = w2_ref.shape[0]
    at = pl.ds(pl.multiple_of(order_ref[0] * slab, slab), slab)
    moves = ((d_embed_hbm, d_embed_ref), (w2_hbm.at[at], w2_ref))
    moves += ((slope_hbm, slope_ref), (normed_hbm, normed_ref), (hid_hbm, hid_ref), (loss_hbm, loss_ref))
    copies = [pltpu.make_async_copy(src, dst, sems.at[k]) for k, (src, dst) in enumerate(moves)]
    for copy in copies:
        copy.start()
    n_blocks, own, _ = d_embed_ref.shape
    sum_ref[...] = jnp.zeros_like(sum_ref)
    gains = biases = second = None
    for copy in copies:
        copy.wait()
    for k in range(0, n_blocks, 2):
        d_embed = jnp.concatenate([d_embed_ref[order_ref[k + 1]], d_embed_ref[order_ref[k + 2]]], axis=0)
        band = slice(k * own, (k + 2) * own)
        d_shift = tdot(d_embed, w2_ref[...], 1, 1) * slope_ref[band, :].astype(F32)
        shift_ref[band, :] = d_shift
        gain = jnp.sum(d_shift * normed_ref[band, :].astype(F32), axis=0, keepdims=True)
        bias = jnp.sum(d_shift, axis=0, keepdims=True)
        part = tdot(hid_ref[band, :], d_embed, 0, 0)
        gains = gain if gains is None else gains + gain
        biases = bias if biases is None else biases + bias
        second = part if second is None else second + part
    hits = jnp.sum(loss_ref[0:8, :], axis=0, keepdims=True)
    logs = jnp.sum(loss_ref[8:16, :], axis=0, keepdims=True)
    sum_ref[0:1, :] = gains
    sum_ref[1:2, :] = biases
    sum_ref[2:3, :] = jnp.concatenate([hits, logs], axis=1)
    n, _, slab = msg_ref.shape
    share = slab // n
    sums = sum_ref[...]
    high = sums.astype(BF)
    rest = sums - high.astype(F32)
    mid = rest.astype(BF)
    low = (rest - mid.astype(F32)).astype(BF)
    row = lax.broadcasted_iota(jnp.int32, sums.shape, 0)
    lower = jnp.where(row < 4, mid.astype(F32), pltpu.roll(low.astype(F32), 4, 0))
    packed = jnp.concatenate([high.astype(F32), lower], axis=0).astype(BF)
    msg_ref[:, :share, :] = jnp.broadcast_to(packed[None], (n, share, slab))
    msg_ref[:, share:, :] = second.astype(BF).reshape(n, share, slab)


def halves(v):
    high = v.astype(BF)
    return high, (v - high.astype(F32)).astype(BF)


def first_kernel(total_rows, order_ref, recv_ref, shift_ref, normed_ref, inv_ref, gain_ref, *rest):
    parts = rest[:-5]
    out_hbm, second_ref, d_pre_ref, out_ref, sems = rest[-5:]
    n, _, _ = out_ref.shape
    slab = d_pre_ref.shape[1]
    share = second_ref.shape[0]
    second_ref[...] = jnp.sum(recv_ref[:, share:, :].astype(F32), axis=0)
    got = jnp.sum(recv_ref[:, :share, :].astype(F32), axis=0)
    got = got[0:8] + (got[8:16] + pltpu.roll(got[8:16], 4, 0))
    chunks = slab // LANES
    for h in range(chunks):
        at = pl.ds(order_ref[0] * chunks + h, 1)
        factor = gain_ref[at, :] * inv_ref[at, :]
        gain_mean = got[0:1, lane(h)] / total_rows
        bias_mean = got[1:2, lane(h)] / total_rows
        for b in range(d_pre_ref.shape[0] // LANES):
            band = slice(b * LANES, (b + 1) * LANES)
            d_pre = factor * (shift_ref[band, lane(h)] - bias_mean - normed_ref[band, lane(h)].astype(F32) * gain_mean)
            d_pre_ref[band, lane(h)] = d_pre.astype(BF)
    high, low = halves(got[0:2])
    sums = [piece[k : k + 1, lane(h)] for k in range(2) for piece in (high, low) for h in range(chunks)]
    high, rest_of = got[2:3].astype(BF), got[2:3] - got[2:3].astype(BF).astype(F32)
    losses = [piece[:, lane(h)] for piece in (high,) + halves(rest_of) for h in range(chunks)]
    losses += [jnp.zeros((1, LANES), BF)] * (8 - len(losses))
    odd = lax.rem(order_ref[10], 2) == 1
    extra = jnp.where(
        odd,
        jnp.concatenate([v.astype(F32) for v in losses], axis=0),
        jnp.concatenate([v.astype(F32) for v in sums], axis=0),
    ).astype(BF)
    out_ref[:, chunks * share :, :] = jnp.broadcast_to(extra[None], (n, 8, LANES))
    group = TILE // share
    copies = []
    for j in range(n // group):
        tile = jnp.concatenate([part[:, j * TILE : (j + 1) * TILE] for part in parts], axis=0)
        grad = tdot(tile, d_pre_ref[...], 0, 0).astype(BF)
        span = slice(j * group, (j + 1) * group)
        for h in range(chunks):
            out_ref[span, h * share : (h + 1) * share, :] = grad[:, lane(h)].reshape(group, share, LANES)
        copies.append(pltpu.make_async_copy(out_ref.at[span], out_hbm.at[span], sems.at[j]))
        copies[-1].start()
    for copy in copies:
        copy.wait()


def tail_kernel(total_rows, recv_ref, second_ref, out_ref, gain_ref, bias_ref, loss_ref, second_out_ref):
    second_out_ref[...] = second_ref[...]
    n_batch, n_proto, height, _ = recv_ref.shape
    share = out_ref.shape[0]
    chunks = height // share
    lines = jnp.zeros((8, LANES), F32)
    for p in range(n_proto):
        acc = recv_ref[0, p].astype(F32)
        for b in range(1, n_batch):
            acc += recv_ref[b, p].astype(F32)
        for h in range(chunks):
            at = (p * chunks + h) * LANES
            out_ref[:, at : at + LANES] = acc[h * share : (h + 1) * share, :]
        sums = recv_ref[0, p, chunks * share :, :].astype(F32)
        for h in range(chunks):
            at = p * chunks + h
            gain_ref[at : at + 1, :] = sums[h : h + 1] + sums[chunks + h : chunks + h + 1]
            bias_ref[at : at + 1, :] = sums[2 * chunks + h : 2 * chunks + h + 1] + sums[3 * chunks + h : 3 * chunks + h + 1]
        lines += recv_ref[1, p, chunks * share :, :].astype(F32)
    hits = lines[0:1] + (lines[2:3] + lines[4:5])
    logs = (lines[1:2] + (lines[3:4] + lines[5:6])) / n_proto
    loss = jnp.sum(logs - hits, axis=1, keepdims=True) / total_rows
    loss_ref[...] = jnp.broadcast_to(loss, loss_ref.shape)


def stage_kernel(order_ref, in0_ref, in1_ref, in2_ref, in3_ref, out0_ref, out1_ref, out2_ref, out3_ref, sum_ref):
    near = in0_ref[...].astype(F32) + in1_ref[...].astype(F32)
    sum_ref[...] = (near + (in2_ref[...].astype(F32) + in3_ref[...].astype(F32))).astype(BF)
    outs = (out0_ref, out1_ref, out2_ref, out3_ref)
    for d, out in enumerate(outs):
        height = out.shape[0]
        at = pl.multiple_of(lax.rem(order_ref[10] + d, len(outs)) * height, height)
        out[...] = sum_ref[pl.ds(at, height), :]


def shape(dims, kind=F32):
    return jax.ShapeDtypeStruct(dims, kind)


def far_shape(dims, kind=F32):
    return pltpu.HBM(dims, kind)


def far(x):
    return pltpu.with_memory_space_constraint(x, pltpu.HBM)


def step_of_device(features, w_first, bn_gain, bn_bias, w_second, prototypes, pair):
    n_batch = lax.axis_size("batch")
    n_proto = lax.axis_size("proto")
    own, d_in = features.shape
    d_hid, width = w_second.shape
    cols = prototypes.shape[0]
    total_rows = own * n_batch * n_proto
    rows = own * n_proto
    part = lax.axis_index("proto")
    slab = d_hid // n_proto
    col_bands = cols // LANES
    row_bands = rows // LANES
    hid_bands = d_hid // LANES
    steps = rows // TILE
    gain = bn_gain.reshape(hid_bands, LANES)
    bias = bn_bias.reshape(hid_bands, LANES)

    def hop(x, moves):
        return lax.ppermute(x, "proto", moves)

    ring = n_proto // 2
    right = [(i * 2 + c, (i + 1) % ring * 2 + c) for i in range(ring) for c in range(2)]
    left = [(t, s) for s, t in right]
    swap = [(i, i ^ 1) for i in range(n_proto)]
    from_left = hop(features, right)
    from_right = hop(features, left)
    across = lax.shift_right_logical(part, 1)
    place = lax.axis_index("batch")
    side = 4
    order = jnp.stack(
        [part]
        + [
            (lax.bitwise_and(across + d, ring - 1) * 2 + lax.bitwise_and(part, 1)) ^ o
            for o in range(2)
            for d in (0, 1, 3, 2)
        ]
        + [lax.shift_right_logical(place, 2), lax.bitwise_and(place, side - 1)]
    ).astype(jnp.int32)
    mate_row = (pair - place * rows).astype(F32).reshape(row_bands, LANES)

    anywhere = pl.BlockSpec(memory_space=pl.ANY)
    pre, msg = pl.pallas_call(
        pre_kernel,
        in_specs=[pl.BlockSpec(features.shape, lambda: (0, 0)), anywhere],
        out_shape=[shape((own, d_hid)), shape((n_batch, 2 * hid_bands, LANES))],
        scratch_shapes=[
            pltpu.VMEM((2 * hid_bands, LANES), F32),
            pltpu.VMEM((4, d_in // 4, d_hid), BF),
            pltpu.SemaphoreType.DMA((4,)),
        ],
        name="pre_kernel",
    )(features, w_first)
    near_left, near_right, _ = lax.optimization_barrier((from_left, from_right, pre))
    far_top = hop(near_left[: own // 2], right)
    far_low = hop(near_right[own // 2 :], left)
    got = deal(msg, "batch")
    got, mate_row, order = lax.optimization_barrier((got, mate_row, order))
    msg = pl.pallas_call(
        relay_kernel, out_shape=shape((n_proto, 2 * hid_bands, LANES)), compiler_params=PARAMS, name="relay_kernel"
    )(got)
    got = deal(msg, "proto")
    unit_embed, mean, inv, msg = pl.pallas_call(
        lambda *refs: embed_kernel(total_rows, *refs),
        out_specs=[pl.BlockSpec(memory_space=pltpu.HBM)] * 4,
        out_shape=[
            far_shape((own, width + LANES)),
            far_shape((hid_bands, LANES)),
            far_shape((hid_bands, LANES)),
            far_shape((n_proto, own, width), BF),
        ],
        scratch_shapes=[
            pltpu.VMEM((own, d_hid), BF),
            pltpu.VMEM((own, width + LANES), F32),
            pltpu.VMEM((hid_bands, LANES), F32),
            pltpu.VMEM((hid_bands, LANES), F32),
            pltpu.VMEM((own, width), BF),
            pltpu.SemaphoreType.DMA((n_proto + 3,)),
        ],
        compiler_params=PARAMS,
        name="embed_kernel",
    )(pre, got, gain, bias, w_second)
    raw, *mine, _ = lax.optimization_barrier((prototypes, features, from_right, from_left, far_top, far_low, msg))
    parts = mine + [hop(piece, swap) for piece in mine]
    proto_bf, proto_t, raw_t, norm, w_slab = pl.pallas_call(
        proto_kernel,
        in_specs=[pl.BlockSpec(memory_space=pltpu.SMEM), pl.BlockSpec((cols, width), lambda: (0, 0)), anywhere],
        out_specs=[
            pl.BlockSpec((cols, width), lambda: (0, 0)),
            pl.BlockSpec((width, cols), lambda: (0, 0)),
            pl.BlockSpec((width, cols), lambda: (0, 0)),
            pl.BlockSpec((8, cols), lambda: (0, 0)),
            anywhere,
        ],
        out_shape=[
            shape((cols, width), BF),
            shape((width, cols), BF),
            shape((width, cols), BF),
            shape((8, cols)),
            far_shape((d_in, slab), BF),
        ],
        scratch_shapes=[pltpu.VMEM((d_in, slab), BF), pltpu.SemaphoreType.DMA],
        name="proto_kernel",
    )(order, raw, w_first)
    block_embed, proto_bf, proto_t, raw_t, norm, w_slab, *parts = lax.optimization_barrier(
        (deal(msg, "proto"), proto_bf, proto_t, raw_t, norm, w_slab, *parts)
    )
    block_embed = block_embed.reshape(rows, width)

    kern, col_msg, soft = pl.pallas_call(
        score_kernel,
        grid=(steps,),
        in_specs=[rows_of(TILE, width), anywhere],
        out_specs=[rows_of(TILE, cols), whole((n_batch, col_bands, LANES)), whole((row_bands, LANES))],
        out_shape=[shape((rows, cols), BF), shape((n_batch, col_bands, LANES)), shape((row_bands, LANES))],
        scratch_shapes=[
            pltpu.VMEM((col_bands * 8, LANES), F32),
            pltpu.VMEM((width, cols), BF),
            pltpu.SemaphoreType.DMA((cols // TILE,)),
        ],
        compiler_params=PARAMS,
        name="score_kernel",
    )(block_embed, far(proto_t))

    def row_pass(recv, extra):
        height = row_bands * (2 if extra else 1)
        return pl.pallas_call(
            row_kernel,
            grid=(steps,),
            in_specs=[whole((n_batch, col_bands, LANES)), rows_of(TILE, cols)]
            + [whole((row_bands, LANES)) for _ in extra],
            out_specs=whole((n_proto, height, LANES)),
            out_shape=shape((n_proto, height, LANES)),
            scratch_shapes=[pltpu.VMEM((col_bands, LANES), F32)],
            compiler_params=PARAMS,
        name="row_kernel",
        )(recv, kern, *extra)

    def col_pass(recv):
        return pl.pallas_call(
            col_kernel,
            grid=(steps,),
            in_specs=[whole(recv.shape), rows_of(TILE, cols)],
            out_specs=whole((n_batch, col_bands, LANES)),
            out_shape=shape((n_batch, col_bands, LANES)),
            scratch_shapes=[pltpu.VMEM((col_bands * 8, LANES), F32), pltpu.VMEM((row_bands, LANES), F32)],
            compiler_params=PARAMS,
        name="col_kernel",
        )(recv, kern)

    recv_soft = None
    for step in range(ITERS):
        recv_col = deal(col_msg, "batch")
        recv_row = deal(row_pass(recv_col, () if step else (soft,)), "proto")
        recv_soft = recv_row if recv_soft is None else recv_soft
        if step + 1 < ITERS:
            col_msg = col_pass(recv_row)

    d_unit, *pieces, loss_tile = pl.pallas_call(
        final_kernel,
        grid=(steps // 2,),
        in_specs=[
            pl.BlockSpec(memory_space=pltpu.SMEM),
            whole((rows, width)),
            whole((row_bands, LANES)),
            whole((width, cols)),
            whole((cols, width)),
            whole((width, cols)),
            whole((8, cols)),
            whole(recv_col.shape),
            whole(recv_row.shape),
            whole(recv_soft.shape),
        ],
        out_specs=[rows_of(2 * TILE, width)] + [whole((width // side, cols))] * side + [whole((16, LANES))],
        out_shape=[far_shape((rows, width), BF)]
        + [far_shape((width // side, cols), BF)] * side
        + [far_shape((16, LANES))],
        scratch_shapes=[
            pltpu.VMEM((rows, cols), BF),
            pltpu.VMEM((2 * TILE, rows), BF),
            pltpu.VMEM((16, LANES), F32),
            pltpu.VMEM((col_bands, LANES), F32),
            pltpu.VMEM((row_bands, LANES), F32),
            pltpu.VMEM((row_bands, LANES), F32),
            pltpu.VMEM((width, cols), BF),
            pltpu.VMEM((4 * TILE, width), BF),
        ],
        compiler_params=PARAMS,
        name="final_kernel",
    )(order, block_embed, mate_row, proto_t, proto_bf, raw_t, norm, recv_col, recv_row, recv_soft)


    def shifted(axis, d):
        moves = []
        for b in range(n_batch):
            y, z = divmod(b, side)
            moves.append((b, (y + d) % side * side + z if axis == 0 else y * side + (z + d) % side))
        return moves

    pieces = [pieces[0]] + [lax.ppermute(pieces[d], "batch", shifted(0, d)) for d in range(1, side)]
    d_unit_got = deal(d_unit.reshape(n_proto, own, width), "proto")
    stat_spec = whole((hid_bands, LANES))
    mean_late, inv, _ = lax.optimization_barrier((mean, inv, d_unit))
    normed, slope, hid = pl.pallas_call(
        slab_kernel,
        grid_spec=pltpu.PrefetchScalarGridSpec(
            num_scalar_prefetch=1,
            grid=(1,),
            in_specs=[anywhere] * (5 + len(parts)),
            out_specs=[pl.BlockSpec(memory_space=pltpu.HBM)] * 3,
            scratch_shapes=[pltpu.VMEM((rows, slab), BF)] * 3
            + [pltpu.VMEM((hid_bands, LANES), F32)] * 4
            + [
                pltpu.VMEM((rows, d_in), BF),
                pltpu.VMEM((d_in, slab), BF),
                pltpu.SemaphoreType.DMA((len(parts) + 5 + 3 * (rows // TILE),)),
            ],
        ),
        out_shape=[shape((rows, slab), BF)] * 3,
        name="slab_kernel",
    )(order, mean_late, inv, gain, bias, w_slab, *parts)
    d_unit, normed, slope, hid = lax.optimization_barrier((d_unit_got, normed, slope, hid))
    d_embed = pl.pallas_call(
        d_embed_kernel,
        in_specs=[anywhere] * 2,
        out_shape=far_shape((n_proto, own, width), BF),
        scratch_shapes=[
            pltpu.VMEM((n_proto, own, width), BF),
            pltpu.VMEM((own, width + LANES), F32),
            pltpu.SemaphoreType.DMA((2,)),
        ],
        name="d_embed_kernel",
    )(far(d_unit), far(unit_embed))
    pieces[0], _ = lax.optimization_barrier((pieces[0], d_embed))
    pieces = pl.pallas_call(
        stage_kernel,
        in_specs=[pl.BlockSpec(memory_space=pltpu.SMEM)] + [pl.BlockSpec((width // side, cols), lambda: (0, 0))] * side,
        out_shape=[shape((width // n_batch, cols), BF)] * side,
        scratch_shapes=[pltpu.VMEM((width // side, cols), BF)],
        name="stage_kernel",
    )(order, *pieces)
    pieces = [pieces[0]] + [lax.ppermute(pieces[d], "batch", shifted(1, d)) for d in range(1, side)]
    d_embed = deal(d_embed, "proto")

    shift, msg = pl.pallas_call(
        shift_kernel,
        grid_spec=pltpu.PrefetchScalarGridSpec(
            num_scalar_prefetch=1,
            grid=(1,),
            in_specs=[
                anywhere,
                anywhere,
                anywhere,
                anywhere,
                anywhere,
                anywhere,
            ],
            out_specs=[whole((rows, slab)), whole((n_batch, 2 * slab // n_batch, width))],
            scratch_shapes=[pltpu.VMEM((8, slab), F32), pltpu.VMEM((16, LANES), F32)]
            + [pltpu.VMEM((rows, slab), BF)] * 3
            + [pltpu.VMEM((n_proto, own, width), BF), pltpu.VMEM((slab, width), BF), pltpu.SemaphoreType.DMA((6,))],
        ),
        out_shape=[shape((rows, slab)), shape((n_batch, 2 * slab // n_batch, width), BF)],
        compiler_params=PARAMS,
        name="shift_kernel",
    )(order, far(d_embed), far(w_second), far(normed), far(slope), far(hid), far(loss_tile))
    recv = deal(msg, "batch")

    share = d_in // (n_batch * n_proto)
    lines = slab // LANES * share + 8
    first, second = pl.pallas_call(
        lambda *refs: first_kernel(total_rows, *refs),
        grid_spec=pltpu.PrefetchScalarGridSpec(
            num_scalar_prefetch=1,
            grid=(1,),
            in_specs=[whole(recv.shape), whole((rows, slab)), whole((rows, slab)), stat_spec, stat_spec]
            + [whole(piece.shape) for piece in parts],
            out_specs=[pl.BlockSpec(memory_space=pltpu.HBM), whole((slab // n_batch, width))],
            scratch_shapes=[
                pltpu.VMEM((rows, slab), BF),
                pltpu.VMEM((n_batch * n_proto, lines, LANES), BF),
                pltpu.SemaphoreType.DMA((d_in // TILE,)),
            ],
        ),
        out_shape=[far_shape((n_batch * n_proto, lines, LANES), BF), shape((slab // n_batch, width))],
        compiler_params=PARAMS,
        name="first_kernel",
    )(order, recv, shift, normed, inv, gain, *parts)

    first, *pieces = lax.optimization_barrier((first, *pieces))
    grad_proto = sum(piece.astype(F32) for piece in pieces).T
    first = deal(first, ("batch", "proto")).reshape(n_batch, n_proto, lines, LANES)
    second = lax.ppermute(
        second,
        ("batch", "proto"),
        [(b * n_proto + p, p * n_batch + b) for b in range(n_batch) for p in range(n_proto)],
    )
    grad_first, grad_gain, grad_bias, loss, grad_second = pl.pallas_call(
        lambda *refs: tail_kernel(total_rows, *refs),
        out_shape=[shape((share, d_hid)), shape((hid_bands, LANES)), shape((hid_bands, LANES)), shape((1, LANES)), shape(second.shape)],
        compiler_params=PARAMS,
        name="tail_kernel",
    )(first, second)
    grad_gain = grad_gain.reshape(-1)
    grad_bias = grad_bias.reshape(-1)
    loss = loss[0, 0]
    return (grad_first, grad_second, grad_gain, grad_bias, grad_proto, loss)


def solution(mesh):
    return jax.shard_map(
        step_of_device,
        mesh=mesh,
        in_specs=(P(("batch", "proto"), None), P(), P(), P(), P(), P("proto", None), P("batch")),
        out_specs=(
            P(("batch", "proto"), None),
            P(("batch", "proto"), None),
            P(),
            P(),
            P("proto", "batch"),
            P(),
        ),
        check_vma=False,
    )
```

```python
import jax
import jax.numpy as jnp
from jax import lax
from jax.experimental import pallas as pl
from jax.experimental.pallas import tpu as pltpu
from jax.sharding import PartitionSpec as P


ITERS = 3
BF = jnp.bfloat16
F32 = jnp.float32
LANES = 128
TILE = 256
LOG2_E = 1.4426950408889634
PARAMS = pltpu.CompilerParams(vmem_limit_bytes=24 * 1024 * 1024)


def deal(x, axis):
    return lax.all_to_all(x, axis, 0, 0, tiled=True)


def tdot(a, b, a_dim, b_dim):
    return lax.dot_general(a, b, (((a_dim,), (b_dim,)), ((), ())), preferred_element_type=F32)


def fold_rows(v):
    return jnp.sum(v.reshape(v.shape[0] // 8, 8, LANES), axis=0)


def as_column(row):
    return jnp.broadcast_to(row, (LANES, LANES)).T


def lane(j):
    return slice(j * LANES, (j + 1) * LANES)


def whole(shape):
    return pl.BlockSpec(shape, lambda i, *_: (0,) * len(shape))


def rows_of(rows, width):
    return pl.BlockSpec((rows, width), lambda i, *_: (i, 0))


def pre_kernel(features_ref, w_hbm, pre_ref, msg_ref, stat_ref, w_buf, sems):
    pieces, depth, width = w_buf.shape
    copies = [
        pltpu.make_async_copy(w_hbm.at[k * depth : (k + 1) * depth], w_buf.at[k], sems.at[k]) for k in range(pieces)
    ]
    for copy in copies:
        copy.start()
    half = stat_ref.shape[0] // 2
    for k in range(pieces):
        copies[k].wait()
        for j in range(width // TILE):
            span = slice(j * TILE, (j + 1) * TILE)
            part = jnp.dot(features_ref[:, k * depth : (k + 1) * depth], w_buf[k, :, span], preferred_element_type=F32)
            pre = part if k == 0 else pre_ref[:, span] + part
            pre_ref[:, span] = pre
            if k == pieces - 1:
                for h in range(TILE // LANES):
                    at = j * (TILE // LANES) + h
                    piece = pre[:, lane(h)]
                    stat_ref[at : at + 1, :] = jnp.sum(piece, axis=0, keepdims=True)
                    stat_ref[half + at : half + at + 1, :] = jnp.sum(piece * piece, axis=0, keepdims=True)
    msg_ref[...] = jnp.broadcast_to(stat_ref[...][None], msg_ref.shape)


def relay_kernel(recv_ref, msg_ref):
    msg_ref[...] = jnp.broadcast_to(jnp.sum(recv_ref[...], axis=0, keepdims=True), msg_ref.shape)


def embed_kernel(
    total_rows, pre_hbm, recv_ref, gain_ref, bias_ref, w2_ref, unit_hbm, mean_hbm, inv_hbm, msg_hbm,
    hid_ref, unit_ref, mean_ref, inv_ref, bf_ref, pre_ref, sems, pre_sems,
):
    stretch = 4
    span = pre_ref.shape[1] // stretch
    fetches = [
        pltpu.make_async_copy(
            pre_hbm.at[:, k * span : (k + 1) * span], pre_ref.at[:, k * span : (k + 1) * span], pre_sems.at[k]
        )
        for k in range(stretch)
    ]
    for fetch in fetches:
        fetch.start()
    stats = jnp.sum(recv_ref[...], axis=0)
    half = stats.shape[0] // 2
    mean = stats[:half] / total_rows
    inv = lax.rsqrt(stats[half:] / total_rows - mean * mean + 1e-05)
    mean_ref[...] = mean
    inv_ref[...] = inv
    for j in range(half):
        if j * LANES % span == 0:
            fetches[j * LANES // span].wait()
        normed = (pre_ref[:, lane(j)] - mean[j : j + 1]) * inv[j : j + 1]
        hid_ref[:, lane(j)] = jax.nn.gelu(normed * gain_ref[j : j + 1, :] + bias_ref[j : j + 1, :]).astype(BF)
    embed = jnp.dot(hid_ref[...], w2_ref[...], preferred_element_type=F32)
    scale = lax.rsqrt(jnp.sum(embed * embed, axis=1, keepdims=True) + 1e-06)
    unit = embed * scale
    bf_ref[...] = unit.astype(BF)
    width = unit.shape[1]
    unit_ref[:, :width] = unit
    unit_ref[:, width:] = jnp.broadcast_to(scale, (unit.shape[0], LANES))
    moves = [(bf_ref, msg_hbm.at[k]) for k in range(msg_hbm.shape[0])]
    moves += [(unit_ref, unit_hbm), (mean_ref, mean_hbm), (inv_ref, inv_hbm)]
    copies = [pltpu.make_async_copy(src, dst, sems.at[k]) for k, (src, dst) in enumerate(moves)]
    for copy in copies:
        copy.start()
    for copy in copies:
        copy.wait()


def proto_kernel(order_ref, raw_ref, w_hbm, proto_ref, proto_t_ref, raw_t_ref, norm_ref, slab_hbm, slab_ref, sem):
    slab = slab_ref.shape[1]
    at = pl.ds(pl.multiple_of(order_ref[0] * slab, slab), slab)
    fetch = pltpu.make_async_copy(w_hbm.at[:, at], slab_ref, sem)
    store = pltpu.make_async_copy(slab_ref, slab_hbm, sem)
    fetch.start()
    for k in range(raw_ref.shape[0] // TILE):
        span = slice(k * TILE, (k + 1) * TILE)
        raw_t = raw_ref[span, :].T
        raw_t_ref[:, span] = raw_t
        wide = raw_t.astype(F32)
        scale = lax.rsqrt(jnp.sum(wide * wide, axis=0, keepdims=True) + 1e-06)
        norm_ref[:, span] = jnp.broadcast_to(scale, (8, TILE))
        unit = (wide * scale).astype(BF)
        proto_t_ref[:, span] = unit
        proto_ref[span, :] = unit.T
        if k == 3:
            fetch.wait()
            store.start()
    store.wait()


def score_kernel(embed_ref, proto_t_hbm, kern_ref, msg_ref, soft_ref, acc_ref, proto_t_ref, sems):
    step = pl.program_id(0)
    rows = embed_ref.shape[0]
    cols = proto_t_ref.shape[1]

    def copy(j):
        span = slice(j * TILE, (j + 1) * TILE)
        return pltpu.make_async_copy(proto_t_hbm.at[:, span], proto_t_ref.at[:, span], sems.at[j])

    @pl.when(step == 0)
    def _():
        for j in range(cols // TILE):
            copy(j).start()
        acc_ref[...] = jnp.zeros_like(acc_ref)
        for j in range(cols // TILE):
            copy(j).wait()

    soft = [None] * (rows // LANES)
    for j in range(cols // TILE):
        span = slice(j * TILE, (j + 1) * TILE)
        scores = jnp.dot(embed_ref[...], proto_t_ref[:, span], preferred_element_type=F32)
        tempered = jnp.exp2(scores * (10.0 * LOG2_E))
        kern = tempered * tempered
        kern_ref[:, span] = kern.astype(BF)
        for h in range(TILE // LANES):
            at = (j * (TILE // LANES) + h) * 8
            acc_ref[at : at + 8, :] += fold_rows(kern[:, lane(h)])
        for b in range(rows // LANES):
            part = tempered[b * LANES : (b + 1) * LANES]
            part = part[:, :LANES] + part[:, LANES:]
            soft[b] = part if soft[b] is None else soft[b] + part
    for b in range(rows // LANES):
        soft_ref[pl.ds(step * (rows // LANES) + b, 1), :] = jnp.sum(soft[b].T, axis=0, keepdims=True)

    @pl.when(step == pl.num_programs(0) - 1)
    def _():
        total = jnp.sum(acc_ref[...].reshape(cols // LANES, 8, LANES), axis=1)
        msg_ref[...] = jnp.broadcast_to(total[None], msg_ref.shape)


def row_kernel(recv_ref, kern_ref, *rest):
    soft_ref = rest[0] if len(rest) == 3 else None
    msg_ref, scale_ref = rest[-2:]
    step = pl.program_id(0)
    rows = kern_ref.shape[0]
    copies = msg_ref.shape[0]

    @pl.when(step == 0)
    def _():
        scale_ref[...] = 1.0 / jnp.sum(recv_ref[...], axis=0)
        if soft_ref is not None:
            half = soft_ref.shape[0]
            msg_ref[:, half:, :] = jnp.broadcast_to(soft_ref[...][None], (copies, half, LANES))

    for b in range(rows // LANES):
        acc = None
        for j in range(scale_ref.shape[0]):
            part = kern_ref[b * LANES : (b + 1) * LANES, lane(j)].astype(F32) * scale_ref[j : j + 1, :]
            acc = part if acc is None else acc + part
        row = jnp.sum(acc.T, axis=0, keepdims=True)
        msg_ref[:, pl.ds(step * (rows // LANES) + b, 1), :] = jnp.broadcast_to(row[None], (copies, 1, LANES))


def col_kernel(recv_ref, kern_ref, msg_ref, acc_ref, scale_ref):
    step = pl.program_id(0)
    rows, cols = kern_ref.shape

    @pl.when(step == 0)
    def _():
        acc_ref[...] = jnp.zeros_like(acc_ref)
        scale_ref[...] = 1.0 / jnp.sum(recv_ref[:, : scale_ref.shape[0], :], axis=0)

    for b in range(rows // LANES):
        scale = as_column(scale_ref[pl.ds(step * (rows // LANES) + b, 1), :])
        for j in range(cols // LANES):
            part = kern_ref[b * LANES : (b + 1) * LANES, lane(j)].astype(F32) * scale
            acc_ref[j * 8 : (j + 1) * 8, :] += fold_rows(part)

    @pl.when(step == pl.num_programs(0) - 1)
    def _():
        total = jnp.sum(acc_ref[...].reshape(cols // LANES, 8, LANES), axis=1)
        msg_ref[...] = jnp.broadcast_to(total[None], msg_ref.shape)


def final_kernel(
    order_ref, embed_ref, pair_ref, proto_t_ref, proto_ref, raw_t_ref, norm_ref, recv_col_ref, recv_row_ref, recv_soft_ref,
    d_unit_ref, piece0_ref, piece1_ref, piece2_ref, piece3_ref, loss_ref,
    grad_ref, mate_ref, loss_acc_ref, col_ref, row_ref, soft_ref, term_ref, both_ref,
):
    step = pl.program_id(0)
    rows = d_unit_ref.shape[0]
    cols = proto_t_ref.shape[1]
    bands = row_ref.shape[0]
    chunks = TILE // LANES

    @pl.when(step == 0)
    def _():
        loss_acc_ref[...] = jnp.zeros_like(loss_acc_ref)
        col_ref[...] = 10.0 / jnp.sum(recv_col_ref[...], axis=0)
        row_ref[...] = 1.0 / jnp.sum(recv_row_ref[:, :bands, :], axis=0)
        soft_ref[...] = jnp.sum(recv_soft_ref[:, bands:, :], axis=0)
        loss_acc_ref[8:16, :] = jnp.log(soft_ref[...])

    base = step * (rows // LANES)
    here = pl.ds(pl.multiple_of(step * rows, rows), rows)
    spot = lax.broadcasted_iota(jnp.int32, (LANES, LANES), 1)
    scales = []
    for b in range(rows // LANES):
        pair = as_column(pair_ref[pl.ds(base + b, 1), :]).astype(jnp.int32)
        found = jnp.zeros((LANES, LANES), F32)
        for q in range(bands):
            hot = spot + q * LANES == pair
            found += jnp.where(hot, row_ref[q : q + 1, :], 0.0)
            mate_ref[b * LANES : (b + 1) * LANES, lane(q)] = jnp.where(hot, 1.0, 0.0).astype(BF)
        scales.append(jnp.broadcast_to(jnp.sum(found, axis=1, keepdims=True), (LANES, LANES)))
    mate_scale = jnp.concatenate(scales, axis=0)
    both_ref[0:rows, :] = embed_ref[here, :]
    both_ref[rows:, :] = jnp.dot(mate_ref[...], embed_ref[...], preferred_element_type=F32).astype(BF)
    soft = jnp.concatenate([as_column(soft_ref[pl.ds(base + b, 1), :]) for b in range(rows // LANES)], axis=0)
    inv_soft = 10.0 / soft
    loss_acc = jnp.zeros((8, LANES), F32)
    for j in range(cols // TILE):
        span = slice(j * TILE, (j + 1) * TILE)
        both = jnp.dot(both_ref[...], proto_t_ref[:, span], preferred_element_type=F32)
        scores, mates = both[:rows], both[rows:]
        for h in range(chunks):
            at = j * chunks + h
            target = jnp.exp2(mates[:, lane(h)] * (20.0 * LOG2_E)) * mate_scale * col_ref[at : at + 1, :]
            score = scores[:, lane(h)]
            loss_acc += fold_rows(target * score)
            grad_ref[here, lane(at)] = (jnp.exp2(score * (10.0 * LOG2_E)) * inv_soft - target).astype(BF)
    d_unit_ref[...] = jnp.dot(grad_ref[here, :], proto_ref[...], preferred_element_type=F32).astype(BF)
    loss_acc_ref[0:8, :] += loss_acc

    @pl.when(step == pl.num_programs(0) - 1)
    def _():
        embed_t = embed_ref[...].T
        for j in range(cols // TILE):
            span = slice(j * TILE, (j + 1) * TILE)
            raw = raw_t_ref[:, span].astype(F32)
            scale = norm_ref[0:1, span]
            acc = jnp.dot(embed_t, grad_ref[:, span], preferred_element_type=F32)
            along = scale * scale * jnp.sum(raw * acc, axis=0, keepdims=True)
            term_ref[:, span] = ((acc - raw * along) * scale).astype(BF)
        pieces = (piece0_ref, piece1_ref, piece2_ref, piece3_ref)
        for d, piece in enumerate(pieces):
            height = piece.shape[0]
            at = pl.multiple_of(lax.rem(order_ref[9] + d, len(pieces)) * height, height)
            piece[...] = term_ref[pl.ds(at, height), :]
        loss_ref[...] = loss_acc_ref[...]


def d_embed_kernel(recv_hbm, unit_hbm, msg_ref, recv_ref, unit_ref, sems):
    copies = [pltpu.make_async_copy(recv_hbm, recv_ref, sems.at[0]), pltpu.make_async_copy(unit_hbm, unit_ref, sems.at[1])]
    for copy in copies:
        copy.start()
    for copy in copies:
        copy.wait()
    d_unit = jnp.sum(recv_ref[...].astype(F32), axis=0)
    width = d_unit.shape[1]
    unit = unit_ref[:, :width]
    d_embed = (d_unit - unit * jnp.sum(unit * d_unit, axis=1, keepdims=True)) * unit_ref[:, width : width + 1]
    msg_ref[...] = jnp.broadcast_to(d_embed.astype(BF)[None], msg_ref.shape)


def start_parts(parts, buf_ref, sems):
    copies = []
    at = 0
    for k, part in enumerate(parts):
        height = part.shape[0]
        copies.append(pltpu.make_async_copy(part, buf_ref.at[at : at + height], sems.at[k]))
        at += height
    for copy in copies:
        copy.start()
    return copies


def slab_kernel(order_ref, mean_hbm, inv_hbm, gain_hbm, bias_hbm, w_hbm, *rest):
    parts = rest[:-13]
    outs, bufs = rest[-13:-10], rest[-10:-7]
    mean_ref, inv_ref, gain_ref, bias_ref, buf_ref, w_ref, sems = rest[-7:]
    normed_ref, slope_ref, hid_ref = bufs
    rows, slab = normed_ref.shape
    w_copy = pltpu.make_async_copy(w_hbm, w_ref, sems.at[len(parts)])
    w_copy.start()
    copies = start_parts(parts, buf_ref, sems)
    stops = [sum(part.shape[0] for part in parts[: k + 1]) for k in range(len(parts))]
    moves = ((mean_hbm, mean_ref), (inv_hbm, inv_ref), (gain_hbm, gain_ref), (bias_hbm, bias_ref))
    base = sems.shape[0] - len(moves)
    stats = [pltpu.make_async_copy(src, dst, sems.at[base + k]) for k, (src, dst) in enumerate(moves)]
    for copy in stats:
        copy.start()
    w_copy.wait()
    for copy in stats:
        copy.wait()
    chunks = slab // LANES
    ones = jnp.ones((LANES, LANES), F32)
    done = 0
    sends = []
    for g in range(rows // TILE):
        start = g * TILE
        while done < len(parts) and (stops[done - 1] if done else 0) < start + TILE:
            copies[done].wait()
            done += 1
        pre = jnp.dot(buf_ref[start : start + TILE, :], w_ref[...], preferred_element_type=F32)
        for h in range(chunks):
            at = pl.ds(order_ref[0] * chunks + h, 1)
            mean, inv, gain, bias = mean_ref[at, :], inv_ref[at, :], gain_ref[at, :], bias_ref[at, :]
            for b in range(TILE // LANES):
                band = slice(start + b * LANES, start + (b + 1) * LANES)
                normed = (pre[b * LANES : (b + 1) * LANES, lane(h)] - mean) * inv
                hidden, back = jax.vjp(jax.nn.gelu, normed * gain + bias)
                normed_ref[band, lane(h)] = normed.astype(BF)
                slope_ref[band, lane(h)] = back(ones)[0].astype(BF)
                hid_ref[band, lane(h)] = hidden.astype(BF)
        span = slice(start, start + TILE)
        for k, (buf, out) in enumerate(zip(bufs, outs)):
            sends.append(
                pltpu.make_async_copy(buf.at[span], out.at[span], sems.at[len(parts) + 1 + g * len(outs) + k])
            )
            sends[-1].start()
    for send in sends:
        send.wait()


def shift_kernel(
    order_ref, d_embed_hbm, w2_hbm, normed_hbm, slope_hbm, hid_hbm, loss_hbm, shift_ref, msg_ref, sum_ref, loss_ref,
    normed_ref, slope_ref, hid_ref, d_embed_ref, w2_ref, sems,
):
    slab = w2_ref.shape[0]
    at = pl.ds(pl.multiple_of(order_ref[0] * slab, slab), slab)
    moves = ((d_embed_hbm, d_embed_ref), (w2_hbm.at[at], w2_ref))
    moves += ((slope_hbm, slope_ref), (normed_hbm, normed_ref), (hid_hbm, hid_ref), (loss_hbm, loss_ref))
    copies = [pltpu.make_async_copy(src, dst, sems.at[k]) for k, (src, dst) in enumerate(moves)]
    for copy in copies:
        copy.start()
    n_blocks, own, _ = d_embed_ref.shape
    sum_ref[...] = jnp.zeros_like(sum_ref)
    gains = biases = second = None
    for copy in copies:
        copy.wait()
    for k in range(0, n_blocks, 2):
        d_embed = jnp.concatenate([d_embed_ref[order_ref[k + 1]], d_embed_ref[order_ref[k + 2]]], axis=0)
        band = slice(k * own, (k + 2) * own)
        d_shift = tdot(d_embed, w2_ref[...], 1, 1) * slope_ref[band, :].astype(F32)
        shift_ref[band, :] = d_shift
        gain = jnp.sum(d_shift * normed_ref[band, :].astype(F32), axis=0, keepdims=True)
        bias = jnp.sum(d_shift, axis=0, keepdims=True)
        part = tdot(hid_ref[band, :], d_embed, 0, 0)
        gains = gain if gains is None else gains + gain
        biases = bias if biases is None else biases + bias
        second = part if second is None else second + part
    hits = jnp.sum(loss_ref[0:8, :], axis=0, keepdims=True)
    logs = jnp.sum(loss_ref[8:16, :], axis=0, keepdims=True)
    sum_ref[0:1, :] = gains
    sum_ref[1:2, :] = biases
    sum_ref[2:3, :] = jnp.concatenate([hits, logs], axis=1)
    n, _, slab = msg_ref.shape
    share = slab // n
    sums = sum_ref[...]
    high = sums.astype(BF)
    rest = sums - high.astype(F32)
    mid = rest.astype(BF)
    low = (rest - mid.astype(F32)).astype(BF)
    row = lax.broadcasted_iota(jnp.int32, sums.shape, 0)
    lower = jnp.where(row < 4, mid.astype(F32), pltpu.roll(low.astype(F32), 4, 0))
    packed = jnp.concatenate([high.astype(F32), lower], axis=0).astype(BF)
    msg_ref[:, :share, :] = jnp.broadcast_to(packed[None], (n, share, slab))
    msg_ref[:, share:, :] = second.astype(BF).reshape(n, share, slab)


def halves(v):
    high = v.astype(BF)
    return high, (v - high.astype(F32)).astype(BF)


def first_kernel(total_rows, order_ref, recv_ref, shift_ref, normed_ref, inv_ref, gain_ref, *rest):
    parts = rest[:-5]
    out_hbm, second_ref, d_pre_ref, out_ref, sems = rest[-5:]
    n, _, _ = out_ref.shape
    slab = d_pre_ref.shape[1]
    share = second_ref.shape[0]
    second_ref[...] = jnp.sum(recv_ref[:, share:, :].astype(F32), axis=0)
    got = jnp.sum(recv_ref[:, :share, :].astype(F32), axis=0)
    got = got[0:8] + (got[8:16] + pltpu.roll(got[8:16], 4, 0))
    chunks = slab // LANES
    for h in range(chunks):
        at = pl.ds(order_ref[0] * chunks + h, 1)
        factor = gain_ref[at, :] * inv_ref[at, :]
        gain_mean = got[0:1, lane(h)] / total_rows
        bias_mean = got[1:2, lane(h)] / total_rows
        for b in range(d_pre_ref.shape[0] // LANES):
            band = slice(b * LANES, (b + 1) * LANES)
            d_pre = factor * (shift_ref[band, lane(h)] - bias_mean - normed_ref[band, lane(h)].astype(F32) * gain_mean)
            d_pre_ref[band, lane(h)] = d_pre.astype(BF)
    high, low = halves(got[0:2])
    sums = [piece[k : k + 1, lane(h)] for k in range(2) for piece in (high, low) for h in range(chunks)]
    high, rest_of = got[2:3].astype(BF), got[2:3] - got[2:3].astype(BF).astype(F32)
    losses = [piece[:, lane(h)] for piece in (high,) + halves(rest_of) for h in range(chunks)]
    losses += [jnp.zeros((1, LANES), BF)] * (8 - len(losses))
    odd = lax.rem(order_ref[10], 2) == 1
    extra = jnp.where(
        odd,
        jnp.concatenate([v.astype(F32) for v in losses], axis=0),
        jnp.concatenate([v.astype(F32) for v in sums], axis=0),
    ).astype(BF)
    out_ref[:, chunks * share :, :] = jnp.broadcast_to(extra[None], (n, 8, LANES))
    group = TILE // share
    copies = []
    for j in range(n // group):
        tile = jnp.concatenate([part[:, j * TILE : (j + 1) * TILE] for part in parts], axis=0)
        grad = tdot(tile, d_pre_ref[...], 0, 0).astype(BF)
        span = slice(j * group, (j + 1) * group)
        for h in range(chunks):
            out_ref[span, h * share : (h + 1) * share, :] = grad[:, lane(h)].reshape(group, share, LANES)
        copies.append(pltpu.make_async_copy(out_ref.at[span], out_hbm.at[span], sems.at[j]))
        copies[-1].start()
    for copy in copies:
        copy.wait()


def tail_kernel(total_rows, recv_ref, second_ref, out_ref, gain_ref, bias_ref, loss_ref, second_out_ref):
    second_out_ref[...] = second_ref[...]
    n_batch, n_proto, height, _ = recv_ref.shape
    share = out_ref.shape[0]
    chunks = height // share
    lines = jnp.zeros((8, LANES), F32)
    for p in range(n_proto):
        acc = recv_ref[0, p].astype(F32)
        for b in range(1, n_batch):
            acc += recv_ref[b, p].astype(F32)
        for h in range(chunks):
            at = (p * chunks + h) * LANES
            out_ref[:, at : at + LANES] = acc[h * share : (h + 1) * share, :]
        sums = recv_ref[0, p, chunks * share :, :].astype(F32)
        for h in range(chunks):
            at = p * chunks + h
            gain_ref[at : at + 1, :] = sums[h : h + 1] + sums[chunks + h : chunks + h + 1]
            bias_ref[at : at + 1, :] = sums[2 * chunks + h : 2 * chunks + h + 1] + sums[3 * chunks + h : 3 * chunks + h + 1]
        lines += recv_ref[1, p, chunks * share :, :].astype(F32)
    hits = lines[0:1] + (lines[2:3] + lines[4:5])
    logs = (lines[1:2] + (lines[3:4] + lines[5:6])) / n_proto
    loss = jnp.sum(logs - hits, axis=1, keepdims=True) / total_rows
    loss_ref[...] = jnp.broadcast_to(loss, loss_ref.shape)


def stage_kernel(order_ref, in0_ref, in1_ref, in2_ref, in3_ref, out0_ref, out1_ref, out2_ref, out3_ref, sum_ref):
    near = in0_ref[...].astype(F32) + in1_ref[...].astype(F32)
    sum_ref[...] = (near + (in2_ref[...].astype(F32) + in3_ref[...].astype(F32))).astype(BF)
    outs = (out0_ref, out1_ref, out2_ref, out3_ref)
    for d, out in enumerate(outs):
        height = out.shape[0]
        at = pl.multiple_of(lax.rem(order_ref[10] + d, len(outs)) * height, height)
        out[...] = sum_ref[pl.ds(at, height), :]


def shape(dims, kind=F32):
    return jax.ShapeDtypeStruct(dims, kind)


def far_shape(dims, kind=F32):
    return pltpu.HBM(dims, kind)


def far(x):
    return pltpu.with_memory_space_constraint(x, pltpu.HBM)


def step_of_device(features, w_first, bn_gain, bn_bias, w_second, prototypes, pair):
    n_batch = lax.axis_size("batch")
    n_proto = lax.axis_size("proto")
    own, d_in = features.shape
    d_hid, width = w_second.shape
    cols = prototypes.shape[0]
    total_rows = own * n_batch * n_proto
    rows = own * n_proto
    part = lax.axis_index("proto")
    slab = d_hid // n_proto
    col_bands = cols // LANES
    row_bands = rows // LANES
    hid_bands = d_hid // LANES
    steps = rows // TILE
    gain = bn_gain.reshape(hid_bands, LANES)
    bias = bn_bias.reshape(hid_bands, LANES)

    def hop(x, moves):
        return lax.ppermute(x, "proto", moves)

    ring = n_proto // 2
    right = [(i * 2 + c, (i + 1) % ring * 2 + c) for i in range(ring) for c in range(2)]
    left = [(t, s) for s, t in right]
    swap = [(i, i ^ 1) for i in range(n_proto)]
    from_left = hop(features, right)
    from_right = hop(features, left)
    across = lax.shift_right_logical(part, 1)
    place = lax.axis_index("batch")
    side = 4
    order = jnp.stack(
        [part]
        + [
            (lax.bitwise_and(across + d, ring - 1) * 2 + lax.bitwise_and(part, 1)) ^ o
            for o in range(2)
            for d in (0, 1, 3, 2)
        ]
        + [lax.shift_right_logical(place, 2), lax.bitwise_and(place, side - 1)]
    ).astype(jnp.int32)
    mate_row = (pair - place * rows).astype(F32).reshape(row_bands, LANES)

    anywhere = pl.BlockSpec(memory_space=pl.ANY)
    pre, msg = pl.pallas_call(
        pre_kernel,
        in_specs=[pl.BlockSpec(features.shape, lambda: (0, 0)), anywhere],
        out_shape=[shape((own, d_hid)), shape((n_batch, 2 * hid_bands, LANES))],
        scratch_shapes=[
            pltpu.VMEM((2 * hid_bands, LANES), F32),
            pltpu.VMEM((4, d_in // 4, d_hid), BF),
            pltpu.SemaphoreType.DMA((4,)),
        ],
        name="pre_kernel",
    )(features, w_first)
    near_left, near_right, _ = lax.optimization_barrier((from_left, from_right, pre))
    far_top = hop(near_left[: own // 2], right)
    far_low = hop(near_right[own // 2 :], left)
    got = deal(msg, "batch")
    got, mate_row, order = lax.optimization_barrier((got, mate_row, order))
    msg = pl.pallas_call(
        relay_kernel, out_shape=shape((n_proto, 2 * hid_bands, LANES)), compiler_params=PARAMS, name="relay_kernel"
    )(got)
    got = deal(msg, "proto")
    unit_embed, mean, inv, msg = pl.pallas_call(
        lambda *refs: embed_kernel(total_rows, *refs),
        in_specs=[
            anywhere,
            pl.BlockSpec((n_proto, 2 * hid_bands, LANES), lambda: (0, 0, 0)),
            pl.BlockSpec((hid_bands, LANES), lambda: (0, 0)),
            pl.BlockSpec((hid_bands, LANES), lambda: (0, 0)),
            pl.BlockSpec((d_hid, width), lambda: (0, 0)),
        ],
        out_specs=[pl.BlockSpec(memory_space=pltpu.HBM)] * 4,
        out_shape=[
            far_shape((own, width + LANES)),
            far_shape((hid_bands, LANES)),
            far_shape((hid_bands, LANES)),
            far_shape((n_proto, own, width), BF),
        ],
        scratch_shapes=[
            pltpu.VMEM((own, d_hid), BF),
            pltpu.VMEM((own, width + LANES), F32),
            pltpu.VMEM((hid_bands, LANES), F32),
            pltpu.VMEM((hid_bands, LANES), F32),
            pltpu.VMEM((own, width), BF),
            pltpu.VMEM((own, d_hid), F32),
            pltpu.SemaphoreType.DMA((n_proto + 3,)),
            pltpu.SemaphoreType.DMA((4,)),
        ],
        compiler_params=PARAMS,
        name="embed_kernel",
    )(far(pre), got, gain, bias, w_second)
    raw, *mine, _ = lax.optimization_barrier((prototypes, features, from_right, from_left, far_top, far_low, msg))
    parts = mine + [hop(piece, swap) for piece in mine]
    proto_bf, proto_t, raw_t, norm, w_slab = pl.pallas_call(
        proto_kernel,
        in_specs=[pl.BlockSpec(memory_space=pltpu.SMEM), pl.BlockSpec((cols, width), lambda: (0, 0)), anywhere],
        out_specs=[
            pl.BlockSpec((cols, width), lambda: (0, 0)),
            pl.BlockSpec((width, cols), lambda: (0, 0)),
            pl.BlockSpec((width, cols), lambda: (0, 0)),
            pl.BlockSpec((8, cols), lambda: (0, 0)),
            anywhere,
        ],
        out_shape=[
            shape((cols, width), BF),
            shape((width, cols), BF),
            shape((width, cols), BF),
            shape((8, cols)),
            far_shape((d_in, slab), BF),
        ],
        scratch_shapes=[pltpu.VMEM((d_in, slab), BF), pltpu.SemaphoreType.DMA],
        name="proto_kernel",
    )(order, raw, w_first)
    block_embed, proto_bf, proto_t, raw_t, norm, w_slab, *parts = lax.optimization_barrier(
        (deal(msg, "proto"), proto_bf, proto_t, raw_t, norm, w_slab, *parts)
    )
    block_embed = block_embed.reshape(rows, width)

    kern, col_msg, soft = pl.pallas_call(
        score_kernel,
        grid=(steps,),
        in_specs=[rows_of(TILE, width), anywhere],
        out_specs=[rows_of(TILE, cols), whole((n_batch, col_bands, LANES)), whole((row_bands, LANES))],
        out_shape=[shape((rows, cols), BF), shape((n_batch, col_bands, LANES)), shape((row_bands, LANES))],
        scratch_shapes=[
            pltpu.VMEM((col_bands * 8, LANES), F32),
            pltpu.VMEM((width, cols), BF),
            pltpu.SemaphoreType.DMA((cols // TILE,)),
        ],
        compiler_params=PARAMS,
        name="score_kernel",
    )(block_embed, far(proto_t))

    def row_pass(recv, extra):
        height = row_bands * (2 if extra else 1)
        return pl.pallas_call(
            row_kernel,
            grid=(steps,),
            in_specs=[whole((n_batch, col_bands, LANES)), rows_of(TILE, cols)]
            + [whole((row_bands, LANES)) for _ in extra],
            out_specs=whole((n_proto, height, LANES)),
            out_shape=shape((n_proto, height, LANES)),
            scratch_shapes=[pltpu.VMEM((col_bands, LANES), F32)],
            compiler_params=PARAMS,
        name="row_kernel",
        )(recv, kern, *extra)

    def col_pass(recv):
        return pl.pallas_call(
            col_kernel,
            grid=(steps,),
            in_specs=[whole(recv.shape), rows_of(TILE, cols)],
            out_specs=whole((n_batch, col_bands, LANES)),
            out_shape=shape((n_batch, col_bands, LANES)),
            scratch_shapes=[pltpu.VMEM((col_bands * 8, LANES), F32), pltpu.VMEM((row_bands, LANES), F32)],
            compiler_params=PARAMS,
        name="col_kernel",
        )(recv, kern)

    recv_soft = None
    for step in range(ITERS):
        recv_col = deal(col_msg, "batch")
        recv_row = deal(row_pass(recv_col, () if step else (soft,)), "proto")
        recv_soft = recv_row if recv_soft is None else recv_soft
        if step + 1 < ITERS:
            col_msg = col_pass(recv_row)

    d_unit, *pieces, loss_tile = pl.pallas_call(
        final_kernel,
        grid=(steps // 2,),
        in_specs=[
            pl.BlockSpec(memory_space=pltpu.SMEM),
            whole((rows, width)),
            whole((row_bands, LANES)),
            whole((width, cols)),
            whole((cols, width)),
            whole((width, cols)),
            whole((8, cols)),
            whole(recv_col.shape),
            whole(recv_row.shape),
            whole(recv_soft.shape),
        ],
        out_specs=[rows_of(2 * TILE, width)] + [whole((width // side, cols))] * side + [whole((16, LANES))],
        out_shape=[far_shape((rows, width), BF)]
        + [far_shape((width // side, cols), BF)] * side
        + [far_shape((16, LANES))],
        scratch_shapes=[
            pltpu.VMEM((rows, cols), BF),
            pltpu.VMEM((2 * TILE, rows), BF),
            pltpu.VMEM((16, LANES), F32),
            pltpu.VMEM((col_bands, LANES), F32),
            pltpu.VMEM((row_bands, LANES), F32),
            pltpu.VMEM((row_bands, LANES), F32),
            pltpu.VMEM((width, cols), BF),
            pltpu.VMEM((4 * TILE, width), BF),
        ],
        compiler_params=PARAMS,
        name="final_kernel",
    )(order, block_embed, mate_row, proto_t, proto_bf, raw_t, norm, recv_col, recv_row, recv_soft)


    def shifted(axis, d):
        moves = []
        for b in range(n_batch):
            y, z = divmod(b, side)
            moves.append((b, (y + d) % side * side + z if axis == 0 else y * side + (z + d) % side))
        return moves

    pieces = [pieces[0]] + [lax.ppermute(pieces[d], "batch", shifted(0, d)) for d in range(1, side)]
    d_unit_got = deal(d_unit.reshape(n_proto, own, width), "proto")
    stat_spec = whole((hid_bands, LANES))
    mean_late, inv, _ = lax.optimization_barrier((mean, inv, d_unit))
    normed, slope, hid = pl.pallas_call(
        slab_kernel,
        grid_spec=pltpu.PrefetchScalarGridSpec(
            num_scalar_prefetch=1,
            grid=(1,),
            in_specs=[anywhere] * (5 + len(parts)),
            out_specs=[pl.BlockSpec(memory_space=pltpu.HBM)] * 3,
            scratch_shapes=[pltpu.VMEM((rows, slab), BF)] * 3
            + [pltpu.VMEM((hid_bands, LANES), F32)] * 4
            + [
                pltpu.VMEM((rows, d_in), BF),
                pltpu.VMEM((d_in, slab), BF),
                pltpu.SemaphoreType.DMA((len(parts) + 5 + 3 * (rows // TILE),)),
            ],
        ),
        out_shape=[shape((rows, slab), BF)] * 3,
        name="slab_kernel",
    )(order, mean_late, inv, gain, bias, w_slab, *parts)
    d_unit, normed, slope, hid = lax.optimization_barrier((d_unit_got, normed, slope, hid))
    d_embed = pl.pallas_call(
        d_embed_kernel,
        in_specs=[anywhere] * 2,
        out_shape=far_shape((n_proto, own, width), BF),
        scratch_shapes=[
            pltpu.VMEM((n_proto, own, width), BF),
            pltpu.VMEM((own, width + LANES), F32),
            pltpu.SemaphoreType.DMA((2,)),
        ],
        name="d_embed_kernel",
    )(far(d_unit), far(unit_embed))
    pieces[0], _ = lax.optimization_barrier((pieces[0], d_embed))
    pieces = pl.pallas_call(
        stage_kernel,
        in_specs=[pl.BlockSpec(memory_space=pltpu.SMEM)] + [pl.BlockSpec((width // side, cols), lambda: (0, 0))] * side,
        out_shape=[shape((width // n_batch, cols), BF)] * side,
        scratch_shapes=[pltpu.VMEM((width // side, cols), BF)],
        name="stage_kernel",
    )(order, *pieces)
    pieces = [pieces[0]] + [lax.ppermute(pieces[d], "batch", shifted(1, d)) for d in range(1, side)]
    d_embed = deal(d_embed, "proto")

    shift, msg = pl.pallas_call(
        shift_kernel,
        grid_spec=pltpu.PrefetchScalarGridSpec(
            num_scalar_prefetch=1,
            grid=(1,),
            in_specs=[
                anywhere,
                anywhere,
                anywhere,
                anywhere,
                anywhere,
                anywhere,
            ],
            out_specs=[whole((rows, slab)), whole((n_batch, 2 * slab // n_batch, width))],
            scratch_shapes=[pltpu.VMEM((8, slab), F32), pltpu.VMEM((16, LANES), F32)]
            + [pltpu.VMEM((rows, slab), BF)] * 3
            + [pltpu.VMEM((n_proto, own, width), BF), pltpu.VMEM((slab, width), BF), pltpu.SemaphoreType.DMA((6,))],
        ),
        out_shape=[shape((rows, slab)), shape((n_batch, 2 * slab // n_batch, width), BF)],
        compiler_params=PARAMS,
        name="shift_kernel",
    )(order, far(d_embed), far(w_second), far(normed), far(slope), far(hid), far(loss_tile))
    recv = deal(msg, "batch")

    share = d_in // (n_batch * n_proto)
    lines = slab // LANES * share + 8
    first, second = pl.pallas_call(
        lambda *refs: first_kernel(total_rows, *refs),
        grid_spec=pltpu.PrefetchScalarGridSpec(
            num_scalar_prefetch=1,
            grid=(1,),
            in_specs=[whole(recv.shape), whole((rows, slab)), whole((rows, slab)), stat_spec, stat_spec]
            + [whole(piece.shape) for piece in parts],
            out_specs=[pl.BlockSpec(memory_space=pltpu.HBM), whole((slab // n_batch, width))],
            scratch_shapes=[
                pltpu.VMEM((rows, slab), BF),
                pltpu.VMEM((n_batch * n_proto, lines, LANES), BF),
                pltpu.SemaphoreType.DMA((d_in // TILE,)),
            ],
        ),
        out_shape=[far_shape((n_batch * n_proto, lines, LANES), BF), shape((slab // n_batch, width))],
        compiler_params=PARAMS,
        name="first_kernel",
    )(order, recv, shift, normed, inv, gain, *parts)

    first, *pieces = lax.optimization_barrier((first, *pieces))
    grad_proto = sum(piece.astype(F32) for piece in pieces).T
    first = deal(first, ("batch", "proto")).reshape(n_batch, n_proto, lines, LANES)
    second = lax.ppermute(
        second,
        ("batch", "proto"),
        [(b * n_proto + p, p * n_batch + b) for b in range(n_batch) for p in range(n_proto)],
    )
    grad_first, grad_gain, grad_bias, loss, grad_second = pl.pallas_call(
        lambda *refs: tail_kernel(total_rows, *refs),
        out_shape=[shape((share, d_hid)), shape((hid_bands, LANES)), shape((hid_bands, LANES)), shape((1, LANES)), shape(second.shape)],
        compiler_params=PARAMS,
        name="tail_kernel",
    )(first, second)
    grad_gain = grad_gain.reshape(-1)
    grad_bias = grad_bias.reshape(-1)
    loss = loss[0, 0]
    return (grad_first, grad_second, grad_gain, grad_bias, grad_proto, loss)


def solution(mesh):
    return jax.shard_map(
        step_of_device,
        mesh=mesh,
        in_specs=(P(("batch", "proto"), None), P(), P(), P(), P(), P("proto", None), P("batch")),
        out_specs=(
            P(("batch", "proto"), None),
            P(("batch", "proto"), None),
            P(),
            P(),
            P("proto", "batch"),
            P(),
        ),
        check_vma=False,
    )
```
